32 devices in a mesh: ctx: 4 (over z), exp: 8 (over y, x, core).
Axes of the slice: x: 2, y: 2, z: 4, core: 2. Of those that a mesh axis runs over, the one named last changes fastest.
Arguments:
- resid_input: bfloat16 [512, 4096], P(('ctx', 'exp')), may hold values from -80 to 80
- norm_gain: float32 [4096], replicated, may hold values from 0.1 to 1.9
- expert_ids: int32 [512, 2], P(('ctx', 'exp')), may hold values from 0 to 3, all different within a row
- route_probs: bfloat16 [512, 2], P(('ctx', 'exp')), may hold values from 0.19921875 to 0.796875
- gate_weight: bfloat16 [8, 6144, 4096], P('exp', 'ctx'), may hold values from -0.09375 to 0.09375
- up_weight: bfloat16 [8, 6144, 4096], P('exp', 'ctx'), may hold values from -0.09375 to 0.09375
- down_weight: bfloat16 [8, 6144, 4096], P('exp', 'ctx'), may hold values from -0.09375 to 0.09375
- grad_output: bfloat16 [512, 4096], P('ctx', 'exp'), may hold values from -6 to 6
- mixer_input: bfloat16 [512, 4096], P('ctx', 'exp'), may hold values from -0.29882812 to 0.29882812
- state_input: bfloat16 [512, 2048], P('ctx', 'exp'), may hold values from -0.5 to 0.5
- state_output: bfloat16 [512, 2048], P('ctx', 'exp'), may hold values from -0.119628906 to 0.119628906
- step_size: float32 [512, 64], P('ctx', 'exp'), may hold values from 0.3 to 1.5
- log_retention: float32 [512, 64], P('ctx', 'exp'), may hold values from -1.5 to 0, as said below
- skip_gain: float32 [64], P('exp'), may hold values from 0.5 to 1.5
Outputs:
- resid_grad: bfloat16 [512, 4096], P('ctx', 'exp')
- mixer_grad: bfloat16 [512, 4096], P('ctx', 'exp')
- state_input_grad: float32 [512, 2048], P('ctx', 'exp')
The draws below stay inside these ranges and needn't reach their ends.
Inputs may be any that keep to these rules, and one draw needn't show every extreme that they name: `expert_ids`: each token names 2 different experts. `log_retention`: strictly negative.
All inputs are finite; a program needn't handle non-finite values.
Results may differ from the reference program's by a relative error of at most 0.009.
Values may be sent and summed in bfloat16 or wider, within the bound.
No kernel may reach another device: no remote copies, remote signals or barrier semaphores. Data moves between devices by JAX's collectives and lax.ppermute only.
A program may use at most 128 MiB of HBM per device.

```python
import math
import jax
import jax.numpy as jnp
from jax import lax

BLENDER_COUNT = 64
P_SIZE = 64
N = 128
G = 16
FFW = 12288
TOK_CTX = 128
D = 4096
EXPERTS = 4
FF_DEV = 1536
CAP = 64
SPAN_ITEMS = 512
N_CTX = 4


def draw_resid_input(key, part):
    key_base, key_rows, key_cols = jax.random.split(key, 3)
    base = jax.random.truncated_normal(key_base, -5.0, 5.0, (SPAN_ITEMS, D), jnp.float32)
    row_scale = jnp.exp(jax.random.uniform(key_rows, (SPAN_ITEMS, 1), jnp.float32, jnp.log(0.5), jnp.log(5.0)))
    col_scale = jnp.exp(jax.random.uniform(key_cols, (1, D), jnp.float32, jnp.log(0.3), jnp.log(3.0)))
    values = row_scale * col_scale * base
    return values.astype(jnp.bfloat16)


def draw_log_retention(key, part):
    sampler_seeds = jax.random.split(key, 7)
    fast_limit = 5
    fast_pick = jax.random.randint(sampler_seeds[0], (1, BLENDER_COUNT), 0, 10) < fast_limit
    fast_rate = jnp.exp(jax.random.uniform(sampler_seeds[1], (1, BLENDER_COUNT), jnp.float32, jnp.log(1.0 / 50.0), jnp.log(1.0 / 30.0)))
    slow_rate = jnp.exp(jax.random.uniform(sampler_seeds[2], (1, BLENDER_COUNT), jnp.float32, jnp.log(0.05), jnp.log(0.4))) / SPAN_ITEMS
    rate_head = jnp.where(fast_pick, fast_rate, slow_rate)
    block_total = SPAN_ITEMS // TOK_CTX
    block_factor = jnp.exp(jax.random.uniform(sampler_seeds[3], (block_total, 1, BLENDER_COUNT), jnp.float32, jnp.log(0.6), jnp.log(1.5)))
    roughness = jax.random.uniform(sampler_seeds[4], (block_total, TOK_CTX, BLENDER_COUNT), jnp.float32, 0.5, 1.5)
    constant_amplitude = -(rate_head[None] * block_factor * roughness).reshape(SPAN_ITEMS, BLENDER_COUNT)
    segment_begin = jax.random.randint(sampler_seeds[5], (2, BLENDER_COUNT), 0, SPAN_ITEMS)
    segment_extent = jnp.log(jax.random.uniform(sampler_seeds[6], (2, BLENDER_COUNT), jnp.float32, 0.5, 0.8))
    sequence_indices = jnp.arange(SPAN_ITEMS)[:, None, None]
    segment_array = jnp.sum(jnp.where(sequence_indices == segment_begin[None], segment_extent[None], 0.0), axis=1)
    return (constant_amplitude + segment_array).astype(jnp.float32)


def level_of(rng, extent, cuts, low, top_value):
    def one(dim, shards_of):
        steps = jax.random.uniform(jax.random.fold_in(jax.random.fold_in(rng, 6), dim), (shards_of,), jnp.float32, low / len(cuts), top_value / len(cuts))
        return jnp.repeat(jnp.exp(steps), extent[dim] // shards_of).reshape((-1,) + (1,) * (len(extent) - dim - 1))

    gain = one(*cuts[0])
    for cut in cuts[1:]:
        gain = gain * one(*cut)
    return gain


def different_ones(rng, rows, amount, top, lift):
    order = jax.random.permutation(jax.random.fold_in(rng, 1), amount)
    favour = order
    for power in range(3):
        favour = favour * favour // amount
    favour = favour * lift // amount
    lots = jax.random.randint(jax.random.fold_in(rng, 2), (rows, amount), 0, 4096) + favour
    holders = jax.random.permutation(jax.random.fold_in(rng, 3), rows)[jnp.arange(amount) % rows]
    lots = jnp.where(jnp.arange(rows)[:, None] == holders[None, :], 1 << 14, lots)
    priority = lots * amount + jnp.arange(amount)
    return lax.top_k(priority.astype(jnp.int32), top)[1].astype(jnp.int32)


def normal_values(rng, shape, scale, bound, cuts=(), kind=jnp.bfloat16):
    gain = level_of(rng, shape, cuts, -0.22, 0.18) if cuts else 1.0
    entries = jax.random.normal(rng, shape, jnp.float32) * scale * gain
    return jnp.minimum(jnp.maximum(entries, -bound), bound).astype(kind)


def setup_inputs(seed: int = 0) -> dict:
    key_of = jax.random.split(jax.random.key(seed), 15)
    resid_input = draw_resid_input(jax.random.fold_in(key_of[14], 71), 0)
    norm_gain = jnp.clip(1.0 + 0.18 * jax.random.normal(key_of[1], (D,), jnp.float32), 0.1, 1.9)
    expert_ids = different_ones(key_of[2], SPAN_ITEMS, EXPERTS, 2, 8192)
    route_probs = jnp.clip(0.19921875 + 0.59765625 * jax.random.uniform(key_of[3], (SPAN_ITEMS, 2), jnp.float32) ** level_of(key_of[3], (SPAN_ITEMS, 2), ((0, 32),), -0.2, 0.2), 0.19921875, 0.796875).astype(jnp.bfloat16)
    gate_weight = normal_values(key_of[4], (2 * EXPERTS, FFW // 2, D), D ** -0.5, 0.09375, ((0, 8), (1, 4)))
    up_weight = normal_values(key_of[5], (2 * EXPERTS, FFW // 2, D), D ** -0.5, 0.09375, ((0, 8), (1, 4)))
    down_weight = normal_values(key_of[6], (2 * EXPERTS, FFW // 2, D), D ** -0.5, 0.09375, ((0, 8), (1, 4)))
    grad_output = normal_values(key_of[7], (SPAN_ITEMS, D), 1.0, 6.0, ((0, 4), (1, 8)))
    mixer_input = normal_values(key_of[8], (SPAN_ITEMS, D), 0.05, 0.29882812, ((0, 4), (1, 8)))
    state_input = normal_values(key_of[9], (SPAN_ITEMS, G * N), N ** -0.5, 0.5, ((0, 4), (1, 8)))
    state_output = normal_values(key_of[10], (SPAN_ITEMS, G * N), 0.02, 0.119628906, ((0, 4), (1, 8)))
    step_size = jnp.clip(jnp.exp(math.log(1.5) - 1.60943787 * jax.random.uniform(key_of[11], (SPAN_ITEMS, BLENDER_COUNT), jnp.float32) ** level_of(key_of[11], (SPAN_ITEMS, BLENDER_COUNT), ((0, 4), (1, 8)), -0.2, 0.2)), 0.3, 1.5)
    log_retention = draw_log_retention(jax.random.fold_in(key_of[14], 71), 0)
    skip_gain = jnp.clip(0.5 + 1.0 * jax.random.uniform(key_of[13], (BLENDER_COUNT,), jnp.float32) ** level_of(key_of[13], (BLENDER_COUNT,), ((0, 8),), -0.2, 0.2), 0.5, 1.5)
    return {"resid_input": resid_input, "norm_gain": norm_gain, "expert_ids": expert_ids, "route_probs": route_probs, "gate_weight": gate_weight, "up_weight": up_weight, "down_weight": down_weight, "grad_output": grad_output, "mixer_input": mixer_input, "state_input": state_input, "state_output": state_output, "step_size": step_size, "log_retention": log_retention, "skip_gain": skip_gain}


highest = lax.Precision.HIGHEST
norm_epsilon = 1e-05
block_length = 64

def expert_grads(normed_slots, grad_slots, prob_slots, gate_rows, up_rows, down_rows):
    row_count = normed_slots.shape[0]
    gate_pre = jnp.dot(normed_slots, gate_rows.T, preferred_element_type=jnp.float32)
    up_pre = jnp.dot(normed_slots, up_rows.T, preferred_element_type=jnp.float32)
    hidden_grad = jnp.dot(grad_slots, down_rows.T, preferred_element_type=jnp.float32) * prob_slots[:, None]
    sigmoid_gate = jax.nn.sigmoid(gate_pre)
    gate_grad = (hidden_grad * up_pre * sigmoid_gate * (1.0 + gate_pre * (1.0 - sigmoid_gate))).astype(jnp.bfloat16)
    up_grad = (hidden_grad * gate_pre * sigmoid_gate).astype(jnp.bfloat16)
    block_total = 2 * N_CTX
    gate_blocks = gate_grad.reshape(row_count, block_total, FF_DEV).transpose(1, 0, 2)
    up_blocks = up_grad.reshape(row_count, block_total, FF_DEV).transpose(1, 0, 2)
    gate_weights = gate_rows.reshape(block_total, FF_DEV, D)
    up_weights = up_rows.reshape(block_total, FF_DEV, D)

    def add_block(total, pieces):
        gate_piece, up_piece, gate_w, up_w = pieces
        term = jnp.dot(gate_piece, gate_w, preferred_element_type=jnp.float32) + jnp.dot(up_piece, up_w, preferred_element_type=jnp.float32)
        rounded = lax.optimization_barrier(term.astype(jnp.bfloat16))
        return (total + rounded.astype(jnp.float32), None)
    total, ignored = lax.scan(add_block, jnp.zeros((row_count, D), jnp.float32), (gate_blocks, up_blocks, gate_weights, up_weights))
    return total

def mixer_block(incoming, pieces):
    upstream, mixer_input, state_input, state_output, step_size, log_retention = pieces
    token_count = log_retention.shape[0]
    head_groups = BLENDER_COUNT // G
    inputs_float = mixer_input.astype(jnp.float32)
    input_states = state_input.astype(jnp.float32)
    output_states = state_output.astype(jnp.float32)
    cumulative = jnp.cumsum(log_retention, axis=0)
    later_mask = jnp.arange(token_count)[None, :] >= jnp.arange(token_count)[:, None]
    difference = cumulative.T[:, None, :] - cumulative.T[:, :, None]
    decay_matrix = jnp.where(later_mask[None], jnp.exp(jnp.where(later_mask[None], difference, 0.0)), 0.0)
    intersection = jnp.einsum('tgn,sgn->gts', input_states, output_states, precision=highest)
    grouped_up = upstream.reshape(token_count, G, head_groups, P_SIZE)
    mixed_weights = decay_matrix.reshape(G, head_groups, token_count, token_count) * intersection[:, None]
    intra_x = jnp.einsum('gjts,sgjp->tgjp', mixed_weights, grouped_up, precision=highest).reshape(token_count, BLENDER_COUNT, P_SIZE)
    tail_decay = jnp.exp(cumulative[-1][None, :] - cumulative)
    grouped_far = incoming.reshape(G, head_groups, N, P_SIZE)
    far_x = jnp.einsum('tgn,gjnp->tgjp', input_states, grouped_far, precision=highest).reshape(token_count, BLENDER_COUNT, P_SIZE)
    far_x = far_x * tail_decay[:, :, None]
    x_part = step_size[:, :, None] * (intra_x + far_x)
    inner_product = jnp.einsum('thp,shp->hts', inputs_float, upstream, precision=highest)
    weighted = decay_matrix * inner_product * step_size.T[:, :, None]
    grouped = weighted.reshape(G, head_groups, token_count, token_count).sum(axis=1)
    intra_b = jnp.einsum('gts,sgn->tgn', grouped, output_states, precision=highest)
    far_weight = (inputs_float * (step_size * tail_decay)[:, :, None]).reshape(token_count, G, head_groups, P_SIZE)
    far_b = jnp.einsum('gjnp,tgjp->tgn', grouped_far, far_weight, precision=highest)
    head_decay = jnp.exp(cumulative).reshape(token_count, G, head_groups)
    local_state = jnp.einsum('sgj,sgn,sgjp->gjnp', head_decay, output_states, grouped_up, precision=highest)
    outgoing = local_state.reshape(BLENDER_COUNT, N, P_SIZE) + jnp.exp(cumulative[-1])[:, None, None] * incoming
    return (outgoing, (x_part, intra_b + far_b))

def reference(resid_input, norm_gain, expert_ids, route_probs, gate_weight, up_weight, down_weight, grad_output, mixer_input, state_input, state_output, step_size, log_retention, skip_gain):
    input_float = resid_input.astype(jnp.float32)
    inverse_rms = lax.rsqrt(lax.optimization_barrier(jnp.mean(input_float * input_float, axis=1, keepdims=True)) + norm_epsilon)
    scaled_input = input_float * inverse_rms
    normed_rows = (scaled_input * norm_gain[None, :]).astype(jnp.bfloat16)
    block_count = N_CTX
    route_ids = expert_ids.reshape(block_count, 2 * TOK_CTX)
    onehot = (route_ids[:, :, None] == jnp.arange(EXPERTS, dtype=jnp.int32)[None, None, :]).astype(jnp.int32)
    position = lax.optimization_barrier(jnp.sum((jnp.cumsum(onehot, axis=1) - onehot) * onehot, axis=2))
    slot_index = jnp.where(position < CAP, route_ids * CAP + position, -1).astype(jnp.int32)
    match_table = (jnp.arange(EXPERTS * CAP, dtype=jnp.int32)[None, :, None] == slot_index[:, None, :]).astype(jnp.int32)
    route_token = jnp.arange(block_count, dtype=jnp.int32)[:, None] * TOK_CTX + jnp.arange(2 * TOK_CTX, dtype=jnp.int32)[None, :] // 2
    slot_token = lax.optimization_barrier(jnp.sum(match_table * route_token[:, None, :], axis=2)).astype(jnp.int32)
    slot_valid = lax.optimization_barrier(jnp.sum(match_table, axis=2)).astype(jnp.float32)
    flat_probs = route_probs.reshape(block_count, 2 * TOK_CTX).astype(jnp.float32)
    slot_prob = lax.optimization_barrier(jnp.sum(match_table.astype(jnp.float32) * flat_probs[:, None, :], axis=2))
    slot_token = slot_token.reshape(block_count, EXPERTS, CAP).transpose(1, 0, 2).reshape(EXPERTS, block_count * CAP)
    slot_valid = slot_valid.reshape(block_count, EXPERTS, CAP).transpose(1, 0, 2).reshape(EXPERTS, block_count * CAP)
    slot_prob = slot_prob.reshape(block_count, EXPERTS, CAP).transpose(1, 0, 2).reshape(EXPERTS, block_count * CAP)
    gate_all = gate_weight.reshape(EXPERTS, FFW, D)
    up_all = up_weight.reshape(EXPERTS, FFW, D)
    down_all = down_weight.reshape(EXPERTS, FFW, D)

    def one_expert(total, pieces):
        gate_rows, up_rows, down_rows, token_index, valid_rows, prob_rows = pieces
        routed = expert_grads(normed_rows[token_index], grad_output[token_index], prob_rows, gate_rows, up_rows, down_rows)
        return (total.at[token_index].add(routed * valid_rows[:, None]), None)
    route_sum, ignored = lax.scan(one_expert, jnp.zeros((SPAN_ITEMS, D), jnp.float32), (gate_all, up_all, down_all, slot_token, slot_valid, slot_prob))
    scaled_grad = route_sum * norm_gain[None, :]
    projection = lax.optimization_barrier(jnp.mean(scaled_grad * scaled_input, axis=1, keepdims=True))
    moe_grad = (inverse_rms * (scaled_grad - scaled_input * projection)).astype(jnp.bfloat16)
    upstream = grad_output.astype(jnp.float32) + moe_grad.astype(jnp.float32)
    resid_grad = upstream.astype(jnp.bfloat16)
    block_total = SPAN_ITEMS // block_length
    pieces = (upstream.reshape(block_total, block_length, BLENDER_COUNT, P_SIZE), mixer_input.reshape(block_total, block_length, BLENDER_COUNT, P_SIZE), state_input.reshape(block_total, block_length, G, N), state_output.reshape(block_total, block_length, G, N), step_size.reshape(block_total, block_length, BLENDER_COUNT), log_retention.reshape(block_total, block_length, BLENDER_COUNT))
    final_state, outputs = lax.scan(mixer_block, jnp.zeros((BLENDER_COUNT, N, P_SIZE), jnp.float32), pieces, reverse=True)
    x_part, b_part = outputs
    mixer_grad = x_part.reshape(SPAN_ITEMS, BLENDER_COUNT, P_SIZE) + skip_gain[None, :, None] * upstream.reshape(SPAN_ITEMS, BLENDER_COUNT, P_SIZE)
    mixer_grad = mixer_grad.astype(jnp.bfloat16).reshape(SPAN_ITEMS, D)
    state_input_grad = b_part.reshape(SPAN_ITEMS, G * N)
    return (resid_grad, mixer_grad, state_input_grad)
```

```python
from functools import partial

import jax
import jax.numpy as jnp
from jax import lax
from jax.experimental import pallas as pl
from jax.experimental.pallas import tpu as pltpu
from jax.sharding import PartitionSpec as P

N = 128
LANES = 128
norm_epsilon = 1e-05
f32 = jnp.float32
bf16 = jnp.bfloat16
highest = lax.Precision.HIGHEST
vmem_bytes = 56 * 1024 * 1024


def params(steps=0):
    return pltpu.CompilerParams(
        dimension_semantics=("arbitrary",) * steps, vmem_limit_bytes=vmem_bytes
    )


def whole(shape):
    return pl.BlockSpec(shape, lambda *_: (0,) * len(shape))


def iota(shape, dim):
    return lax.broadcasted_iota(jnp.int32, shape, dim)


def dot(a, b, ca, cb, precision=None):
    return lax.dot_general(
        a, b, (((ca,), (cb,)), ((), ())), precision=precision, preferred_element_type=f32
    )


def dispatch_kernel(packed, grad, table, probs, rows_x, rows_g, *, experts, capacity):
    tokens, width = grad.shape
    meta = packed[:, width:].astype(f32)
    lane = iota((tokens, LANES), 1).astype(f32)
    first = meta[:, 0:1] == lane
    second = meta[:, 1:2] == lane
    member = jnp.where(first | second, 1.0, 0.0).astype(bf16)
    weight = (jnp.where(first, meta[:, 2:3], 0.0) + jnp.where(second, meta[:, 3:4], 0.0)).astype(bf16)
    row = iota((tokens, tokens), 0)
    col = iota((tokens, tokens), 1)
    before = jnp.where(row < col, 1.0, 0.0).astype(bf16)
    same = jnp.where(row == col, 1.0, 0.0).astype(bf16)
    position = dot(member, before, 0, 0)
    member_t = dot(member, same, 0, 0)
    weight_t = dot(weight, same, 0, 0)
    slot = iota((capacity, tokens), 0).astype(f32)
    for e in range(experts):
        hit = (slot == position[e : e + 1, :]) & (member_t[e : e + 1, :] > 0.5)
        entry = jnp.where(hit, 1.0, 0.0)
        table[e * capacity : (e + 1) * capacity, :] = entry.astype(bf16)
        share = jnp.sum(entry * weight_t[e : e + 1, :], axis=1, keepdims=True)
        probs[e * capacity : (e + 1) * capacity, :] = jnp.broadcast_to(share, (capacity, LANES))
    sel = table[...]
    out_x = dot(sel, packed[:, :width], 1, 0).astype(bf16)
    out_g = dot(sel, grad[...], 1, 0).astype(bf16)
    for c in range(rows_x.shape[0]):
        rows_x[c] = out_x
        rows_g[c] = out_g


def gate_up_kernel(own, other, gain, gate_w, up_w, coef_gate, coef_up, normed):
    ctx, peers, slots, width = own.shape
    half = ctx * slots
    model = peers * width

    @pl.when(pl.program_id(0) == 0)
    def _():
        for side, ref in enumerate((own, other)):
            total = jnp.zeros((half, 1), f32)
            for j in range(peers):
                x = ref[:, j].reshape(half, width).astype(f32)
                total = total + jnp.sum(x * x, axis=1, keepdims=True)
            inverse = lax.rsqrt(total * (1.0 / model) + norm_epsilon)
            for j in range(peers):
                x = ref[:, j].reshape(half, width).astype(f32)
                cols = slice(j * width, (j + 1) * width)
                normed[side * half : (side + 1) * half, cols] = (x * inverse * gain[:, cols]).astype(bf16)

    rows = normed[...]
    gate = dot(rows, gate_w[0], 1, 1)
    up = dot(rows, up_w[0], 1, 1)
    sig = jax.nn.sigmoid(gate)
    coef_gate[...] = up * sig * (1.0 + gate * (1.0 - sig))
    coef_up[...] = gate * sig


def hidden_kernel(own, other, coef_gate, coef_up, down_w, gate_grad, up_grad, grads):
    ctx, peers, slots, width = own.shape
    half = ctx * slots

    @pl.when(pl.program_id(0) == 0)
    def _():
        for side, ref in enumerate((own, other)):
            for j in range(peers):
                cols = slice(j * width, (j + 1) * width)
                grads[side * half : (side + 1) * half, cols] = ref[:, j].reshape(half, width)

    hidden = dot(grads[...], down_w[0], 1, 1)
    gate_grad[...] = (hidden * coef_gate[...]).astype(bf16)
    up_grad[...] = (hidden * coef_up[...]).astype(bf16)


def output_kernel(gate_grad, up_grad, gate_w, up_w, out):
    out[...] = (
        dot(gate_grad[...], gate_w[0], 1, 0) + dot(up_grad[...], up_w[0], 1, 0)
    ).astype(bf16)


def slot_kernel(place, parts, probs, gain, x_rows, out):
    ctx, slots, model = parts.shape
    peers, width = x_rows.shape[1], x_rows.shape[3]
    prob = probs[:, 0:1]
    squares = jnp.zeros((slots, 1), f32)
    product = jnp.zeros((slots, 1), f32)
    for j in range(peers):
        cols = slice(j * width, (j + 1) * width)
        total = parts[0, :, cols].astype(f32)
        for c in range(1, ctx):
            total = total + parts[c, :, cols].astype(f32)
        x = x_rows[0, j].astype(f32)
        squares = squares + jnp.sum(x * x, axis=1, keepdims=True)
        product = product + jnp.sum(total * gain[:, cols] * x, axis=1, keepdims=True)
    inverse = lax.rsqrt(squares * (1.0 / model) + norm_epsilon)
    scale = prob * inverse
    shift = scale * product * inverse * inverse * (1.0 / model)
    for j in range(peers):
        cols = slice(j * width, (j + 1) * width)
        total = parts[0, :, cols].astype(f32)
        for c in range(1, ctx):
            total = total + parts[c, :, cols].astype(f32)
        x = x_rows[0, j].astype(f32)
        out[j] = (total * gain[:, cols] * scale - x * shift).astype(bf16)


def mixer_setup_kernel(
    log_ret, step, state_in, state_out, mix, weigh, step_l, tail_l, head_l, total_l, *, groups
):
    tokens, heads = log_ret.shape
    width = step_l.shape[1]
    size = width // heads
    row = iota((tokens, tokens), 0)
    col = iota((tokens, tokens), 1)
    upto = jnp.where(row <= col, 1.0, 0.0)
    logs = log_ret[...]
    cum_t = dot(logs, upto, 0, 0, highest)
    cum = dot(upto, logs, 0, 0, highest)
    last = cum[tokens - 1 : tokens, :]
    spread = jnp.where(iota((heads, width), 0) == iota((heads, width), 1) // size, 1.0, 0.0)
    steps = step[...]
    step_l[...] = dot(steps, spread, 1, 0, highest)
    tail_l[...] = dot(steps * jnp.exp(last - cum), spread, 1, 0, highest)
    head_l[...] = dot(jnp.exp(cum), spread, 1, 0, highest)
    total_l[...] = dot(jnp.broadcast_to(last, (8, heads)), spread, 1, 0, highest)
    later = col >= row
    for g in range(groups):
        cols = slice(g * N, (g + 1) * N)
        inter = dot(state_in[:, cols], state_out[:, cols], 1, 1)
        for h in range(g * heads // groups, (g + 1) * heads // groups):
            gap = cum_t[h : h + 1, :] - cum[:, h : h + 1]
            decay = jnp.where(later, jnp.exp(jnp.where(later, gap, 0.0)), 0.0)
            mix[h] = decay * inter
            weigh[h] = decay * steps[:, h : h + 1]


def mixer_local_kernel(
    moved, table, grad, mixer, state_out, mix, weigh, step_l, head_l, skip, resid_grad, base, local_b, state
):
    tokens, width = grad.shape
    heads = mix.shape[0]
    size = width // heads
    groups = state_out.shape[1] // N
    moe = dot(table[...], moved[...], 0, 0).astype(bf16)
    upstream = grad[...].astype(f32) + moe.astype(f32)
    resid_grad[...] = upstream.astype(bf16)
    span = width // groups
    for g in range(groups):
        cols = slice(g * N, (g + 1) * N)
        wide = slice(g * span, (g + 1) * span)
        scaled = upstream[:, wide] * head_l[:, wide]
        state[:, wide] = dot(state_out[:, cols].astype(f32), scaled, 0, 0, highest).astype(bf16)
        weighted = jnp.zeros((tokens, tokens), f32)
        for h in range(g * heads // groups, (g + 1) * heads // groups):
            part = slice(h * size, (h + 1) * size)
            up_h = upstream[:, part]
            mixed = dot(mix[h], up_h, 1, 0, highest)
            base[:, part] = step_l[:, part] * mixed + skip[:, part] * up_h
            inner = dot(mixer[:, part].astype(f32), up_h, 1, 1, highest)
            weighted = weighted + weigh[h] * inner
        local_b[:, cols] = dot(weighted, state_out[:, cols].astype(f32), 1, 0, highest)


def mixer_far_kernel(place, states, totals, base, local_b, mixer, state_in, tail_l, mixer_grad, input_grad):
    ctx = states.shape[0]
    groups = state_in.shape[1] // N
    width = base.shape[1]
    span = width // groups
    here = place[0]
    incoming = jnp.zeros(states.shape[1:], f32)
    for c in range(ctx - 1, 0, -1):
        joined = states[c].astype(f32) + jnp.exp(totals[c, 0:1, :]) * incoming
        incoming = jnp.where(here < c, joined, incoming)
    for g in range(groups):
        cols = slice(g * N, (g + 1) * N)
        wide = slice(g * span, (g + 1) * span)
        far = dot(state_in[:, cols].astype(f32), incoming[:, wide], 1, 0, highest)
        mixer_grad[:, wide] = (base[:, wide] + tail_l[:, wide] * far).astype(bf16)
        scaled = mixer[:, wide].astype(f32) * tail_l[:, wide]
        input_grad[:, cols] = local_b[:, cols] + dot(scaled, incoming[:, wide], 1, 1, highest)


def block_of(total, most):
    size = min(total, most)
    while total % size:
        size -= LANES if size > LANES else 1
    return size


def body(
    resid_input,
    norm_gain,
    expert_ids,
    route_probs,
    gate_weight,
    up_weight,
    down_weight,
    grad_output,
    mixer_input,
    state_input,
    state_output,
    step_size,
    log_retention,
    skip_gain,
):
    ctx = lax.axis_size("ctx")
    peers = lax.axis_size("exp")
    place = jnp.stack([lax.axis_index("ctx"), lax.axis_index("exp")]).astype(jnp.int32)
    experts = peers // 2
    token_rows, model = resid_input.shape
    tokens, width = grad_output.shape
    capacity = 2 * tokens // experts
    slots = capacity // 2
    heads = skip_gain.shape[0]
    groups = state_input.shape[1] // N
    hidden = gate_weight.shape[1]
    gain = norm_gain.reshape(1, model)
    skip = jnp.repeat(skip_gain, width // heads).reshape(1, width)
    partner = [(i, i ^ 1) for i in range(peers)]
    shape = jax.ShapeDtypeStruct

    meta = jnp.concatenate(
        [expert_ids.astype(bf16), route_probs, jnp.zeros((token_rows, LANES - 4), bf16)], axis=1
    )
    packed = jnp.concatenate(
        [
            resid_input.reshape(token_rows, peers, width),
            jnp.broadcast_to(meta[:, None, :], (token_rows, peers, LANES)),
        ],
        axis=2,
    ).reshape(token_rows, peers * (width + LANES))
    packed = lax.all_to_all(packed, "exp", split_axis=1, concat_axis=0, tiled=True)

    mix, weigh, step_l, tail_l, head_l, total_l = pl.pallas_call(
        partial(mixer_setup_kernel, groups=groups),
        out_shape=(
            shape((heads, tokens, tokens), f32),
            shape((heads, tokens, tokens), f32),
            shape((tokens, width), f32),
            shape((tokens, width), f32),
            shape((tokens, width), f32),
            shape((8, width), f32),
        ),
        compiler_params=params(),
    )(log_retention, step_size, state_input, state_output)
    totals = lax.all_to_all(
        jnp.broadcast_to(total_l[None], (ctx, 8, width)), "ctx", split_axis=0, concat_axis=0, tiled=True
    )

    table, probs, rows_x, rows_g = pl.pallas_call(
        partial(dispatch_kernel, experts=experts, capacity=capacity),
        out_shape=(
            shape((experts * capacity, tokens), bf16),
            shape((experts * capacity, LANES), f32),
            shape((ctx, experts * capacity, width), bf16),
            shape((ctx, experts * capacity, width), bf16),
        ),
        compiler_params=params(),
    )(packed, grad_output)

    def spread(rows):
        got = lax.all_to_all(
            rows.reshape(ctx * peers, slots, width), ("ctx", "exp"), split_axis=0, concat_axis=0, tiled=True
        ).reshape(ctx, peers, slots, width)
        return got, lax.ppermute(got, "exp", partner)

    own_x, other_x = spread(rows_x)
    own_g, other_g = spread(rows_g)
    rows = 2 * ctx * slots
    slab = (ctx, peers, slots, width)
    block = block_of(hidden, 256)
    steps = hidden // block
    weight_spec = pl.BlockSpec((1, block, model), lambda i: (0, i, 0))
    act_spec = pl.BlockSpec((rows, block), lambda i: (0, i))
    coef_gate, coef_up = pl.pallas_call(
        gate_up_kernel,
        grid=(steps,),
        in_specs=[whole(slab), whole(slab), whole((1, model)), weight_spec, weight_spec],
        out_specs=[act_spec, act_spec],
        out_shape=(shape((rows, hidden), f32), shape((rows, hidden), f32)),
        scratch_shapes=[pltpu.VMEM((rows, model), bf16)],
        compiler_params=params(1),
    )(own_x, other_x, gain, gate_weight, up_weight)
    gate_grad, up_grad = pl.pallas_call(
        hidden_kernel,
        grid=(steps,),
        in_specs=[whole(slab), whole(slab), act_spec, act_spec, weight_spec],
        out_specs=[act_spec, act_spec],
        out_shape=(shape((rows, hidden), bf16), shape((rows, hidden), bf16)),
        scratch_shapes=[pltpu.VMEM((rows, model), bf16)],
        compiler_params=params(1),
    )(own_g, other_g, coef_gate, coef_up, down_weight)
    column = block_of(model, 512)
    col_spec = pl.BlockSpec((1, hidden, column), lambda i: (0, 0, i))
    block_grad = pl.pallas_call(
        output_kernel,
        grid=(model // column,),
        in_specs=[whole((rows, hidden)), whole((rows, hidden)), col_spec, col_spec],
        out_specs=pl.BlockSpec((rows, column), lambda i: (0, i)),
        out_shape=shape((rows, model), bf16),
        compiler_params=params(1),
    )(gate_grad, up_grad, gate_weight, up_weight)

    half = rows // 2
    swapped = lax.ppermute(block_grad[half:], "exp", partner)
    summed = (block_grad[:half].astype(f32) + swapped.astype(f32)).astype(bf16)
    parts = lax.all_to_all(
        summed.reshape(ctx, slots, model), "ctx", split_axis=0, concat_axis=0, tiled=True
    )
    moved = pl.pallas_call(
        slot_kernel,
        grid_spec=pltpu.PrefetchScalarGridSpec(
            num_scalar_prefetch=1,
            grid=(1,),
            in_specs=[
                whole((ctx, slots, model)),
                pl.BlockSpec((slots, LANES), lambda i, at: (at[1], 0)),
                whole((1, model)),
                pl.BlockSpec((1, peers, slots, width), lambda i, at: (at[0], 0, 0, 0)),
            ],
            out_specs=whole((peers, slots, width)),
        ),
        out_shape=shape((peers, slots, width), bf16),
        compiler_params=params(1),
    )(place, parts, probs, gain, own_x)
    moved = lax.all_to_all(moved, "exp", split_axis=0, concat_axis=0, tiled=True).reshape(
        experts * capacity, width
    )

    resid_grad, base, local_b, state = pl.pallas_call(
        mixer_local_kernel,
        out_shape=(
            shape((tokens, width), bf16),
            shape((tokens, width), f32),
            shape((tokens, groups * N), f32),
            shape((N, width), bf16),
        ),
        compiler_params=params(),
    )(moved, table, grad_output, mixer_input, state_output, mix, weigh, step_l, head_l, skip)
    states = lax.all_to_all(
        jnp.broadcast_to(state[None], (ctx, N, width)), "ctx", split_axis=0, concat_axis=0, tiled=True
    )
    mixer_grad, state_input_grad = pl.pallas_call(
        mixer_far_kernel,
        grid_spec=pltpu.PrefetchScalarGridSpec(
            num_scalar_prefetch=1,
            grid=(1,),
            in_specs=[
                whole((ctx, N, width)),
                whole((ctx, 8, width)),
                whole((tokens, width)),
                whole((tokens, groups * N)),
                whole((tokens, width)),
                whole((tokens, groups * N)),
                whole((tokens, width)),
            ],
            out_specs=[whole((tokens, width)), whole((tokens, groups * N))],
        ),
        out_shape=(shape((tokens, width), bf16), shape((tokens, groups * N), f32)),
        compiler_params=params(1),
    )(place, states, totals, base, local_b, mixer_input, state_input, tail_l)
    return (resid_grad, mixer_grad, state_input_grad)


def solution(mesh):
    in_specs = (
        P(("ctx", "exp"), None),
        P(),
        P(("ctx", "exp"), None),
        P(("ctx", "exp"), None),
        P("exp", "ctx", None),
        P("exp", "ctx", None),
        P("exp", "ctx", None),
        P("ctx", "exp"),
        P("ctx", "exp"),
        P("ctx", "exp"),
        P("ctx", "exp"),
        P("ctx", "exp"),
        P("ctx", "exp"),
        P("exp"),
    )
    out_specs = (P("ctx", "exp"), P("ctx", "exp"), P("ctx", "exp"))
    return jax.shard_map(body, mesh=mesh, in_specs=in_specs, out_specs=out_specs, check_vma=False)
```

```python
from functools import partial

import jax
import jax.numpy as jnp
from jax import lax
from jax.experimental import pallas as pl
from jax.experimental.pallas import tpu as pltpu
from jax.sharding import PartitionSpec as P


N = 128
LANES = 128
norm_epsilon = 1e-05
f32 = jnp.float32
bf16 = jnp.bfloat16
highest = lax.Precision.HIGHEST
vmem_bytes = 56 * 1024 * 1024


def params(steps=0):
    return pltpu.CompilerParams(
        dimension_semantics=("arbitrary",) * steps, vmem_limit_bytes=vmem_bytes
    )


def whole(shape):
    return pl.BlockSpec(shape, lambda *_: (0,) * len(shape))


def iota(shape, dim):
    return lax.broadcasted_iota(jnp.int32, shape, dim)


def dot(a, b, ca, cb, precision=None):
    return lax.dot_general(
        a, b, (((ca,), (cb,)), ((), ())), precision=precision, preferred_element_type=f32
    )


def pack_kernel(resid, ids_t, probs_t, out):
    peers, rows = out.shape[0], out.shape[1]
    width = out.shape[2] - LANES
    eye = jnp.where(iota((rows, rows), 0) == iota((rows, rows), 1), 1.0, 0.0).astype(bf16)
    ids = dot(eye, ids_t[...].astype(f32).astype(bf16), 1, 1)
    probs = dot(eye, probs_t[...], 1, 1)
    lane = iota((rows, LANES), 1)
    meta = jnp.where(lane == 0, ids[:, 0:1], 0.0) + jnp.where(lane == 1, ids[:, 1:2], 0.0)
    meta = meta + jnp.where(lane == 2, probs[:, 0:1], 0.0) + jnp.where(lane == 3, probs[:, 1:2], 0.0)
    meta = meta.astype(bf16)
    for j in range(peers):
        out[j, :, :width] = resid[:, j * width : (j + 1) * width]
        out[j, :, width:] = meta


def dispatch_kernel(packed, table, probs, rows_x, *, experts, capacity):
    tokens = packed.shape[0]
    width = packed.shape[1] - LANES
    meta = packed[:, width:].astype(f32)
    lane = iota((tokens, LANES), 1).astype(f32)
    first = meta[:, 0:1] == lane
    second = meta[:, 1:2] == lane
    member = jnp.where(first | second, 1.0, 0.0).astype(bf16)
    weight = (jnp.where(first, meta[:, 2:3], 0.0) + jnp.where(second, meta[:, 3:4], 0.0)).astype(bf16)
    row = iota((tokens, tokens), 0)
    col = iota((tokens, tokens), 1)
    before = jnp.where(row < col, 1.0, 0.0).astype(bf16)
    same = jnp.where(row == col, 1.0, 0.0).astype(bf16)
    position = dot(member, before, 0, 0)
    member_t = dot(member, same, 0, 0)
    weight_t = dot(weight, same, 0, 0)
    slot = iota((capacity, tokens), 0).astype(f32)
    for e in range(experts):
        hit = (slot == position[e : e + 1, :]) & (member_t[e : e + 1, :] > 0.5)
        entry = jnp.where(hit, 1.0, 0.0)
        table[e * capacity : (e + 1) * capacity, :] = entry.astype(bf16)
        share = jnp.sum(entry * weight_t[e : e + 1, :], axis=1, keepdims=True)
        probs[e * capacity : (e + 1) * capacity, :] = jnp.broadcast_to(share, (capacity, LANES))
    out_x = dot(table[...], packed[:, :width], 1, 0).astype(bf16)
    for c in range(rows_x.shape[0]):
        rows_x[c] = out_x


def select_kernel(table, grad, rows_g):
    out_g = dot(table[...], grad[...], 1, 0).astype(bf16)
    for c in range(rows_g.shape[0]):
        rows_g[c] = out_g


def gate_up_kernel(own, other, gain, gate_w, up_w, coef_gate, coef_up, normed):
    ctx, peers, slots, width = own.shape
    half = ctx * slots
    model = peers * width

    @pl.when(pl.program_id(0) == 0)
    def _():
        for side, ref in enumerate((own, other)):
            total = jnp.zeros((half, 1), f32)
            for j in range(peers):
                x = ref[:, j].reshape(half, width).astype(f32)
                total = total + jnp.sum(x * x, axis=1, keepdims=True)
            inverse = lax.rsqrt(total * (1.0 / model) + norm_epsilon)
            for j in range(peers):
                x = ref[:, j].reshape(half, width).astype(f32)
                cols = slice(j * width, (j + 1) * width)
                normed[side * half : (side + 1) * half, cols] = (x * inverse * gain[:, cols]).astype(bf16)

    rows = normed[...]
    gate = dot(rows, gate_w[0], 1, 1)
    up = dot(rows, up_w[0], 1, 1)
    sig = jax.nn.sigmoid(gate)
    coef_gate[...] = up * sig * (1.0 + gate * (1.0 - sig))
    coef_up[...] = gate * sig


def back_kernel(
    own, other, coef_gate, coef_up, gate_hbm, up_hbm, down_hbm, out_own, out_other,
    grads, gate_grad, up_grad, down_w, gate_w, up_w, staged, in_sems, out_sems,
):
    ctx, peers, slots, width = own.shape
    half = ctx * slots
    blocks, block, _ = down_w.shape
    columns, _, column = gate_w.shape

    def down_copy(i):
        return pltpu.make_async_copy(
            down_hbm.at[0, i * block : (i + 1) * block, :], down_w.at[i], in_sems.at[i]
        )

    def pair_copies(i):
        cols = slice(i * column, (i + 1) * column)
        at = blocks + 2 * i
        return (
            pltpu.make_async_copy(gate_hbm.at[0, :, cols], gate_w.at[i], in_sems.at[at]),
            pltpu.make_async_copy(up_hbm.at[0, :, cols], up_w.at[i], in_sems.at[at + 1]),
        )

    def out_copies(i):
        cols = slice(i * column, (i + 1) * column)
        return (
            pltpu.make_async_copy(staged.at[i, 0:half], out_own.at[:, cols], out_sems.at[2 * i]),
            pltpu.make_async_copy(staged.at[i, half : 2 * half], out_other.at[:, cols], out_sems.at[2 * i + 1]),
        )

    for i in range(blocks):
        down_copy(i).start()
    for i in range(columns):
        for copy in pair_copies(i):
            copy.start()
    for side, ref in enumerate((own, other)):
        for j in range(peers):
            cols = slice(j * width, (j + 1) * width)
            grads[side * half : (side + 1) * half, cols] = ref[:, j].reshape(half, width)
    rows = grads[...]
    for i in range(blocks):
        down_copy(i).wait()
        part = slice(i * block, (i + 1) * block)
        grad = dot(rows, down_w[i], 1, 1)
        gate_grad[:, part] = (grad * coef_gate[:, part]).astype(bf16)
        up_grad[:, part] = (grad * coef_up[:, part]).astype(bf16)
    for i in range(columns):
        for copy in pair_copies(i):
            copy.wait()
        staged[i] = (dot(gate_grad[...], gate_w[i], 1, 0) + dot(up_grad[...], up_w[i], 1, 0)).astype(bf16)
        for copy in out_copies(i):
            copy.start()
    for i in range(columns):
        for copy in out_copies(i):
            copy.wait()


def slot_kernel(place, parts, probs, gain, x_rows, out, sums):
    ctx, slots, model = parts.shape
    peers, width = x_rows.shape[1], x_rows.shape[3]
    prob = probs[:, 0:1]
    squares = jnp.zeros((slots, 1), f32)
    product = jnp.zeros((slots, 1), f32)
    for j in range(peers):
        cols = slice(j * width, (j + 1) * width)
        total = parts[0, :, cols].astype(f32)
        for c in range(1, ctx):
            total = total + parts[c, :, cols].astype(f32)
        total = total * gain[:, cols]
        sums[:, cols] = total
        x = x_rows[0, j].astype(f32)
        squares = squares + jnp.sum(x * x, axis=1, keepdims=True)
        product = product + jnp.sum(total * x, axis=1, keepdims=True)
    inverse = lax.rsqrt(squares * (1.0 / model) + norm_epsilon)
    scale = prob * inverse
    shift = scale * product * inverse * inverse * (1.0 / model)
    for j in range(peers):
        cols = slice(j * width, (j + 1) * width)
        out[j] = (sums[:, cols] * scale - x_rows[0, j].astype(f32) * shift).astype(bf16)


def mixer_setup_kernel(
    log_t, step_t, skip, state_in, state_out, mix, weigh, step_l, tail_l, head_l, skip_l, total_l, *, groups
):
    heads, tokens = log_t.shape
    width = step_l.shape[1]
    size = width // heads
    row = iota((tokens, tokens), 0)
    col = iota((tokens, tokens), 1)
    upto = jnp.where(row <= col, 1.0, 0.0)
    eye = jnp.where(row == col, 1.0, 0.0)
    cum_t = dot(log_t[...], upto, 1, 0, highest)
    cum = dot(upto, log_t[...], 0, 1, highest)
    steps = dot(eye, step_t[...], 1, 1, highest)
    last = cum[tokens - 1 : tokens, :]
    spread = jnp.where(iota((heads, width), 0) == iota((heads, width), 1) // size, 1.0, 0.0)
    step_l[...] = dot(steps, spread, 1, 0, highest)
    tail_l[...] = dot(steps * jnp.exp(last - cum), spread, 1, 0, highest)
    head_l[...] = dot(jnp.exp(cum), spread, 1, 0, highest)
    skip_l[...] = dot(jnp.broadcast_to(skip[...], (8, heads)), spread, 1, 0, highest)
    total_l[...] = dot(jnp.broadcast_to(jnp.exp(last), (8, heads)), spread, 1, 0, highest)
    later = col >= row
    for g in range(groups):
        cols = slice(g * N, (g + 1) * N)
        inter = dot(state_in[:, cols], state_out[:, cols], 1, 1)
        for h in range(g * heads // groups, (g + 1) * heads // groups):
            gap = cum_t[h : h + 1, :] - cum[:, h : h + 1]
            decay = jnp.where(later, jnp.exp(jnp.where(later, gap, 0.0)), 0.0)
            mix[h] = (decay * inter).astype(bf16)
            weigh[h] = decay * steps[:, h : h + 1]


def upstream_kernel(moved, table, grad, state_out, head_l, total_l, upstream, resid_grad, state):
    width = grad.shape[1]
    groups = state_out.shape[1] // N
    span = width // groups
    moe = dot(table[...], moved[...], 0, 0).astype(bf16)
    up = grad[...].astype(f32) + moe.astype(f32)
    upstream[...] = up
    resid_grad[...] = up.astype(bf16)
    for g in range(groups):
        cols = slice(g * N, (g + 1) * N)
        wide = slice(g * span, (g + 1) * span)
        scaled = (up[:, wide] * head_l[:, wide]).astype(bf16)
        state[0:N, wide] = dot(state_out[:, cols], scaled, 0, 0).astype(bf16)
    total = total_l[...]
    high = total.astype(bf16)
    low = (total - high.astype(f32)).astype(bf16)
    state[N : N + 8, :] = high
    state[N + 8 : N + 16, :] = low


def mixer_local_kernel(upstream, resid_grad, mixer, state_out, mix, weigh, step_l, skip_l, base, local_b):
    tokens, width = upstream.shape
    heads = mix.shape[0]
    size = width // heads
    groups = state_out.shape[1] // N
    for g in range(groups):
        cols = slice(g * N, (g + 1) * N)
        weighted = jnp.zeros((tokens, tokens), f32)
        for h in range(g * heads // groups, (g + 1) * heads // groups):
            part = slice(h * size, (h + 1) * size)
            up_h = resid_grad[:, part]
            mixed = dot(mix[h], up_h, 1, 0)
            base[:, part] = step_l[:, part] * mixed + skip_l[0:1, part] * upstream[:, part]
            weighted = weighted + weigh[h] * dot(mixer[:, part], up_h, 1, 1)
        local_b[:, cols] = dot(weighted.astype(bf16), state_out[:, cols], 1, 0)


def mixer_far_kernel(*refs):
    base, local_b, mixer, state_in, tail_l, mixer_grad, input_grad = refs[-7:]
    states = refs[:-7]
    groups = state_in.shape[1] // N
    width = base.shape[1]
    span = width // groups
    incoming = states[-1][0:N, :].astype(f32)
    for ref in states[-2::-1]:
        decay = ref[N : N + 1, :].astype(f32) + ref[N + 8 : N + 9, :].astype(f32)
        incoming = ref[0:N, :].astype(f32) + decay * incoming
    incoming = incoming.astype(bf16)
    for g in range(groups):
        cols = slice(g * N, (g + 1) * N)
        wide = slice(g * span, (g + 1) * span)
        far = dot(state_in[:, cols], incoming[:, wide], 1, 0)
        mixer_grad[:, wide] = (base[:, wide] + tail_l[:, wide] * far).astype(bf16)
        scaled = (mixer[:, wide].astype(f32) * tail_l[:, wide]).astype(bf16)
        input_grad[:, cols] = local_b[:, cols] + dot(scaled, incoming[:, wide], 1, 1)


def block_of(total, most):
    size = min(total, most)
    while total % size:
        size -= LANES if size > LANES else 1
    return size


def cost(flops, moved):
    return pl.CostEstimate(flops=flops, transcendentals=0, bytes_accessed=moved)


def body(
    resid_input,
    norm_gain,
    expert_ids,
    route_probs,
    gate_weight,
    up_weight,
    down_weight,
    grad_output,
    mixer_input,
    state_input,
    state_output,
    step_size,
    log_retention,
    skip_gain,
):
    ctx = lax.axis_size("ctx")
    peers = lax.axis_size("exp")
    place = jnp.stack([lax.axis_index("ctx"), lax.axis_index("exp")]).astype(jnp.int32)
    experts = peers // 2
    token_rows, model = resid_input.shape
    tokens, width = grad_output.shape
    capacity = 2 * tokens // experts
    slots = capacity // 2
    heads = skip_gain.shape[0]
    groups = state_input.shape[1] // N
    hidden = gate_weight.shape[1]
    gain = norm_gain.reshape(1, model)
    partner = [(i, i ^ 1) for i in range(peers)]
    shape = jax.ShapeDtypeStruct

    packed = pl.pallas_call(
        pack_kernel,
        out_shape=shape((peers, token_rows, width + LANES), bf16),
        compiler_params=params(),
        name="pack",
    )(resid_input, expert_ids.T, route_probs.T)
    packed = lax.all_to_all(packed, "exp", split_axis=0, concat_axis=0, tiled=True)

    mix, weigh, step_l, tail_l, head_l, skip_l, total_l = pl.pallas_call(
        partial(mixer_setup_kernel, groups=groups),
        out_shape=(
            shape((heads, tokens, tokens), bf16),
            shape((heads, tokens, tokens), f32),
            shape((tokens, width), f32),
            shape((tokens, width), f32),
            shape((tokens, width), f32),
            shape((8, width), f32),
            shape((8, width), f32),
        ),
        compiler_params=params(),
        cost_estimate=cost(2 * 10**9, 2 * 10**6),
        name="mixer_setup",
    )(log_retention.T, step_size.T, skip_gain.reshape(1, heads), state_input, state_output)

    table, probs, rows_x = pl.pallas_call(
        partial(dispatch_kernel, experts=experts, capacity=capacity),
        out_shape=(
            shape((experts * capacity, tokens), bf16),
            shape((experts * capacity, LANES), f32),
            shape((ctx, experts * capacity, width), bf16),
        ),
        compiler_params=params(),
        name="dispatch",
    )(packed.reshape(tokens, width + LANES))
    rows_g = pl.pallas_call(
        select_kernel,
        out_shape=shape((ctx, experts * capacity, width), bf16),
        compiler_params=params(),
        cost_estimate=cost(10**9, 2 * 10**6),
        name="select",
    )(table, grad_output)

    def spread(rows):
        got = lax.all_to_all(
            rows.reshape(ctx * peers, slots, width), ("ctx", "exp"), split_axis=0, concat_axis=0, tiled=True
        ).reshape(ctx, peers, slots, width)
        return got, lax.ppermute(got, "exp", partner)

    own_x, other_x = spread(rows_x)
    own_g, other_g = spread(rows_g)
    rows = 2 * ctx * slots
    half = rows // 2
    slab = (ctx, peers, slots, width)
    block = block_of(hidden, 256)
    blocks = hidden // block
    weight_spec = pl.BlockSpec((1, block, model), lambda i: (0, i, 0))
    act_spec = pl.BlockSpec((rows, block), lambda i: (0, i))
    product = 2 * rows * model * hidden
    coef_gate, coef_up = pl.pallas_call(
        gate_up_kernel,
        grid=(blocks,),
        in_specs=[whole(slab), whole(slab), whole((1, model)), weight_spec, weight_spec],
        out_specs=[act_spec, act_spec],
        out_shape=(shape((rows, hidden), f32), shape((rows, hidden), f32)),
        scratch_shapes=[pltpu.VMEM((rows, model), bf16)],
        compiler_params=params(1),
        cost_estimate=cost(2 * product, 4 * model * hidden),
        name="gate_up",
    )(own_x, other_x, gain, gate_weight, up_weight)
    column = block_of(model, 512)
    columns = model // column
    in_hbm = pl.BlockSpec(memory_space=pl.ANY)
    in_vmem = pl.BlockSpec(memory_space=pltpu.VMEM)
    out_own, out_other = pl.pallas_call(
        back_kernel,
        in_specs=[in_vmem, in_vmem, in_vmem, in_vmem, in_hbm, in_hbm, in_hbm],
        out_specs=[in_hbm, in_hbm],
        out_shape=(shape((half, model), bf16), shape((half, model), bf16)),
        scratch_shapes=[
            pltpu.VMEM((rows, model), bf16),
            pltpu.VMEM((rows, hidden), bf16),
            pltpu.VMEM((rows, hidden), bf16),
            pltpu.VMEM((blocks, block, model), bf16),
            pltpu.VMEM((columns, hidden, column), bf16),
            pltpu.VMEM((columns, hidden, column), bf16),
            pltpu.VMEM((columns, rows, column), bf16),
            pltpu.SemaphoreType.DMA((blocks + 2 * columns,)),
            pltpu.SemaphoreType.DMA((2 * columns,)),
        ],
        compiler_params=params(),
        cost_estimate=cost(3 * product, 6 * model * hidden),
        name="back",
    )(own_g, other_g, coef_gate, coef_up, gate_weight, up_weight, down_weight)

    swapped = lax.ppermute(out_other, "exp", partner)
    summed = (out_own.astype(f32) + swapped.astype(f32)).astype(bf16)
    parts = lax.all_to_all(
        summed.reshape(ctx, slots, model), "ctx", split_axis=0, concat_axis=0, tiled=True
    )
    moved = pl.pallas_call(
        slot_kernel,
        grid_spec=pltpu.PrefetchScalarGridSpec(
            num_scalar_prefetch=1,
            grid=(1,),
            in_specs=[
                whole((ctx, slots, model)),
                pl.BlockSpec((slots, LANES), lambda i, at: (at[1], 0)),
                whole((1, model)),
                pl.BlockSpec((1, peers, slots, width), lambda i, at: (at[0], 0, 0, 0)),
            ],
            out_specs=whole((peers, slots, width)),
            scratch_shapes=[pltpu.VMEM((slots, model), f32)],
        ),
        out_shape=shape((peers, slots, width), bf16),
        compiler_params=params(1),
        name="slot",
    )(place, parts, probs, gain, own_x)
    moved = lax.all_to_all(moved, "exp", split_axis=0, concat_axis=0, tiled=True).reshape(
        experts * capacity, width
    )

    upstream, resid_grad, state = pl.pallas_call(
        upstream_kernel,
        out_shape=(
            shape((tokens, width), f32),
            shape((tokens, width), bf16),
            shape((N + 16, width), bf16),
        ),
        compiler_params=params(),
        name="upstream",
    )(moved, table, grad_output, state_output, head_l, total_l)
    states = [
        lax.ppermute(state, "ctx", [(i, i - k) for i in range(k, ctx)]) for k in range(1, ctx)
    ]
    base, local_b = pl.pallas_call(
        mixer_local_kernel,
        out_shape=(shape((tokens, width), f32), shape((tokens, groups * N), f32)),
        compiler_params=params(),
        cost_estimate=cost(3 * 10**9, 2 * 10**6),
        name="mixer_local",
    )(upstream, resid_grad, mixer_input, state_output, mix, weigh, step_l, skip_l)
    mixer_grad, state_input_grad = pl.pallas_call(
        mixer_far_kernel,
        out_shape=(shape((tokens, width), bf16), shape((tokens, groups * N), f32)),
        compiler_params=params(),
        name="mixer_far",
    )(*states, base, local_b, mixer_input, state_input, tail_l)
    return (resid_grad, mixer_grad, state_input_grad)


def solution(mesh):
    in_specs = (
        P(("ctx", "exp"), None),
        P(),
        P(("ctx", "exp"), None),
        P(("ctx", "exp"), None),
        P("exp", "ctx", None),
        P("exp", "ctx", None),
        P("exp", "ctx", None),
        P("ctx", "exp"),
        P("ctx", "exp"),
        P("ctx", "exp"),
        P("ctx", "exp"),
        P("ctx", "exp"),
        P("ctx", "exp"),
        P("exp"),
    )
    out_specs = (P("ctx", "exp"), P("ctx", "exp"), P("ctx", "exp"))
    return jax.shard_map(body, mesh=mesh, in_specs=in_specs, out_specs=out_specs, check_vma=False)
```

```python
import math
from functools import partial

import jax
import jax.numpy as jnp
from jax import lax
from jax.experimental import pallas as pl
from jax.experimental.pallas import tpu as pltpu
from jax.sharding import PartitionSpec as P


N = 128
LANES = 128
norm_epsilon = 1e-05
f32 = jnp.float32
bf16 = jnp.bfloat16
highest = lax.Precision.HIGHEST
vmem_bytes = 56 * 1024 * 1024
resident_bytes = 1024 * 1024


def params(steps=0):
    return pltpu.CompilerParams(
        dimension_semantics=("arbitrary",) * steps, vmem_limit_bytes=vmem_bytes
    )


def whole(shape):
    return pl.BlockSpec(shape, lambda *_: (0,) * len(shape))


def iota(shape, dim):
    return lax.broadcasted_iota(jnp.int32, shape, dim)


def dot(a, b, ca, cb, precision=None):
    return lax.dot_general(
        a, b, (((ca,), (cb,)), ((), ())), precision=precision, preferred_element_type=f32
    )


def pack_kernel(resid, ids_t, probs_t, out):
    peers, rows = out.shape[0], out.shape[1]
    width = out.shape[2] - LANES
    eye = jnp.where(iota((rows, rows), 0) == iota((rows, rows), 1), 1.0, 0.0).astype(bf16)
    ids = dot(eye, ids_t[...].astype(f32).astype(bf16), 1, 1)
    probs = dot(eye, probs_t[...], 1, 1)
    lane = iota((rows, LANES), 1)
    meta = jnp.where(lane == 0, ids[:, 0:1], 0.0) + jnp.where(lane == 1, ids[:, 1:2], 0.0)
    meta = meta + jnp.where(lane == 2, probs[:, 0:1], 0.0) + jnp.where(lane == 3, probs[:, 1:2], 0.0)
    meta = meta.astype(bf16)
    for j in range(peers):
        out[j, :, :width] = resid[:, j * width : (j + 1) * width]
        out[j, :, width:] = meta


def dispatch_kernel(packed, table, shares, rows_x, *, experts, capacity):
    tokens = packed.shape[0]
    width = packed.shape[1] - LANES
    meta = packed[:, width:].astype(f32)
    lane = iota((tokens, LANES), 1).astype(f32)
    first = meta[:, 0:1] == lane
    second = meta[:, 1:2] == lane
    member = jnp.where(first | second, 1.0, 0.0).astype(bf16)
    weight = (jnp.where(first, meta[:, 2:3], 0.0) + jnp.where(second, meta[:, 3:4], 0.0)).astype(bf16)
    row = iota((tokens, tokens), 0)
    col = iota((tokens, tokens), 1)
    before = jnp.where(row < col, 1.0, 0.0).astype(bf16)
    same = jnp.where(row == col, 1.0, 0.0).astype(bf16)
    position = dot(member, before, 0, 0)
    member_t = dot(member, same, 0, 0)
    weight_t = dot(weight, same, 0, 0)
    slot = iota((capacity, tokens), 0).astype(f32)
    for e in range(experts):
        hit = (slot == position[e : e + 1, :]) & (member_t[e : e + 1, :] > 0.5)
        entry = jnp.where(hit, 1.0, 0.0)
        table[e * capacity : (e + 1) * capacity, :] = entry.astype(bf16)
        shares[e * capacity : (e + 1) * capacity, :] = (entry * weight_t[e : e + 1, :]).astype(bf16)
    out_x = dot(table[...], packed[:, :width], 1, 0).astype(bf16)
    for c in range(rows_x.shape[0]):
        rows_x[c] = out_x


def select_kernel(table, grad, rows_g):
    out_g = dot(table[...], grad[...], 1, 0).astype(bf16)
    for c in range(rows_g.shape[0]):
        rows_g[c] = out_g


def gate_up_kernel(own, other, gain, gate_w, up_w, coef_gate, coef_up, inverses, normed):
    ctx, peers, slots, width = own.shape
    half = ctx * slots
    model = peers * width

    @pl.when(pl.program_id(0) == 0)
    def _():
        for side, ref in enumerate((own, other)):
            total = jnp.zeros((half, 1), f32)
            for j in range(peers):
                x = ref[:, j].reshape(half, width).astype(f32)
                total = total + jnp.sum(x * x, axis=1, keepdims=True)
            inverse = lax.rsqrt(total * (1.0 / model) + norm_epsilon)
            if side == 0:
                inverses[...] = jnp.broadcast_to(inverse, (half, LANES))
            for j in range(peers):
                x = ref[:, j].reshape(half, width).astype(f32)
                cols = slice(j * width, (j + 1) * width)
                normed[side * half : (side + 1) * half, cols] = (x * inverse * gain[:, cols]).astype(bf16)

    rows = normed[...]
    gate = dot(rows, gate_w[0], 1, 1)
    up = dot(rows, up_w[0], 1, 1)
    sig = jax.nn.sigmoid(gate)
    coef_gate[...] = up * sig * (1.0 + gate * (1.0 - sig))
    coef_up[...] = gate * sig


def back_kernel(
    own, other, coef_gate_hbm, coef_up_hbm, gate_hbm, up_hbm, down_hbm, out_own, out_other,
    grads, coef_gate, coef_up, gate_grad, up_grad, down_w, gate_w, up_w, sems,
):
    ctx, peers, slots, width = own.shape
    half = ctx * slots
    blocks, block, _ = down_w.shape
    columns, _, column = gate_w.shape

    def down_copy(i):
        return pltpu.make_async_copy(down_hbm.at[0, i * block : (i + 1) * block, :], down_w.at[i], sems.at[i])

    def pair_copies(i):
        cols = slice(i * column, (i + 1) * column)
        at = blocks + 2 * i
        return (
            pltpu.make_async_copy(gate_hbm.at[0, :, cols], gate_w.at[i], sems.at[at]),
            pltpu.make_async_copy(up_hbm.at[0, :, cols], up_w.at[i], sems.at[at + 1]),
        )

    coef_copies = (
        pltpu.make_async_copy(coef_gate_hbm, coef_gate, sems.at[blocks + 2 * columns]),
        pltpu.make_async_copy(coef_up_hbm, coef_up, sems.at[blocks + 2 * columns + 1]),
    )
    down_copy(0).start()
    for copy in coef_copies:
        copy.start()
    for i in range(1, blocks):
        down_copy(i).start()
    for i in range(columns):
        for copy in pair_copies(i):
            copy.start()
    for side, ref in enumerate((own, other)):
        for j in range(peers):
            cols = slice(j * width, (j + 1) * width)
            grads[side * half : (side + 1) * half, cols] = ref[:, j].reshape(half, width)
    rows = grads[...]
    for i in range(blocks):
        down_copy(i).wait()
        part = slice(i * block, (i + 1) * block)
        grad = dot(rows, down_w[i], 1, 1)
        if i == 0:
            for copy in coef_copies:
                copy.wait()
        gate_grad[:, part] = (grad * coef_gate[:, part]).astype(bf16)
        up_grad[:, part] = (grad * coef_up[:, part]).astype(bf16)
    for i in range(columns):
        for copy in pair_copies(i):
            copy.wait()
        cols = slice(i * column, (i + 1) * column)
        out = (dot(gate_grad[...], gate_w[i], 1, 0) + dot(up_grad[...], up_w[i], 1, 0)).astype(bf16)
        out_own[:, cols] = out[:half]
        out_other[:, cols] = out[half:]


def slot_kernel(own, swapped, gain, inverses, x_rows, out, sums):
    ctx, peers, slots, width = x_rows.shape
    half = ctx * slots
    model = peers * width
    product = jnp.zeros((half, 1), f32)
    for j in range(peers):
        cols = slice(j * width, (j + 1) * width)
        total = (own[:, cols].astype(f32) + swapped[:, cols].astype(f32)) * gain[:, cols]
        sums[:, cols] = total
        x = x_rows[:, j].reshape(half, width).astype(f32)
        product = product + jnp.sum(total * x, axis=1, keepdims=True)
    inverse = inverses[:, 0:1]
    shift = inverse * inverse * inverse * product * (1.0 / model)
    for j in range(peers):
        cols = slice(j * width, (j + 1) * width)
        x = x_rows[:, j].reshape(half, width).astype(f32)
        out[:, j] = (sums[:, cols] * inverse - x * shift).astype(bf16).reshape(ctx, slots, width)


def mixer_setup_kernel(
    log_t, step_t, skip, state_in, state_out, mix, weigh, step_l, tail_l, head_l, skip_l, total_l, *, groups
):
    heads, tokens = log_t.shape
    width = step_l.shape[1]
    size = width // heads
    row = iota((tokens, tokens), 0)
    col = iota((tokens, tokens), 1)
    upto = jnp.where(row <= col, 1.0, 0.0)
    eye = jnp.where(row == col, 1.0, 0.0)
    cum_t = dot(log_t[...], upto, 1, 0, highest)
    cum = dot(upto, log_t[...], 0, 1, highest)
    steps = dot(eye, step_t[...], 1, 1, highest)
    last = cum[tokens - 1 : tokens, :]
    spread = jnp.where(iota((heads, width), 0) == iota((heads, width), 1) // size, 1.0, 0.0)
    step_l[...] = dot(steps, spread, 1, 0, highest)
    tail_l[...] = dot(steps * jnp.exp(last - cum), spread, 1, 0, highest)
    head_l[...] = dot(jnp.exp(cum), spread, 1, 0, highest)
    skip_l[...] = dot(jnp.broadcast_to(skip[...], (8, heads)), spread, 1, 0, highest)
    total_l[...] = dot(jnp.broadcast_to(jnp.exp(last), (8, heads)), spread, 1, 0, highest)
    later = col >= row
    for g in range(groups):
        cols = slice(g * N, (g + 1) * N)
        inter = dot(state_in[:, cols], state_out[:, cols], 1, 1)
        for h in range(g * heads // groups, (g + 1) * heads // groups):
            gap = cum_t[h : h + 1, :] - cum[:, h : h + 1]
            decay = jnp.where(later, jnp.exp(jnp.where(later, gap, 0.0)), 0.0)
            mix[h] = (decay * inter).astype(bf16)
            weigh[h] = decay * steps[:, h : h + 1]


def upstream_kernel(moved, shares, grad, state_out, head_l, total_l, upstream, resid_grad, state):
    width = grad.shape[1]
    groups = state_out.shape[1] // N
    span = width // groups
    moe = dot(shares[...], moved[0], 0, 0)
    for c in range(1, moved.shape[0]):
        moe = moe + dot(shares[...], moved[c], 0, 0)
    moe = moe.astype(bf16)
    up = grad[...].astype(f32) + moe.astype(f32)
    upstream[...] = up
    resid_grad[...] = up.astype(bf16)
    for g in range(groups):
        cols = slice(g * N, (g + 1) * N)
        wide = slice(g * span, (g + 1) * span)
        scaled = (up[:, wide] * head_l[:, wide]).astype(bf16)
        state[0:N, wide] = dot(state_out[:, cols], scaled, 0, 0).astype(bf16)
    total = total_l[...]
    high = total.astype(bf16)
    low = (total - high.astype(f32)).astype(bf16)
    state[N : N + 8, :] = high
    state[N + 8 : N + 16, :] = low


def mixer_local_kernel(upstream, resid_grad, mixer, state_out, mix, weigh, step_l, skip_l, base, local_b):
    tokens, width = upstream.shape
    heads = mix.shape[0]
    size = width // heads
    groups = state_out.shape[1] // N
    for g in range(groups):
        cols = slice(g * N, (g + 1) * N)
        weighted = jnp.zeros((tokens, tokens), f32)
        for h in range(g * heads // groups, (g + 1) * heads // groups):
            part = slice(h * size, (h + 1) * size)
            up_h = resid_grad[:, part]
            mixed = dot(mix[h], up_h, 1, 0)
            base[:, part] = step_l[:, part] * mixed + skip_l[0:1, part] * upstream[:, part]
            weighted = weighted + weigh[h] * dot(mixer[:, part], up_h, 1, 1)
        local_b[:, cols] = dot(weighted.astype(bf16), state_out[:, cols], 1, 0)


def mixer_far_kernel(*refs):
    base, local_b, mixer, state_in, tail_l, mixer_grad, input_grad = refs[-7:]
    states = refs[:-7]
    groups = state_in.shape[1] // N
    width = base.shape[1]
    span = width // groups
    incoming = states[-1][0:N, :].astype(f32)
    for ref in states[-2::-1]:
        decay = ref[N : N + 1, :].astype(f32) + ref[N + 8 : N + 9, :].astype(f32)
        incoming = ref[0:N, :].astype(f32) + decay * incoming
    incoming = incoming.astype(bf16)
    for g in range(groups):
        cols = slice(g * N, (g + 1) * N)
        wide = slice(g * span, (g + 1) * span)
        far = dot(state_in[:, cols], incoming[:, wide], 1, 0)
        mixer_grad[:, wide] = (base[:, wide] + tail_l[:, wide] * far).astype(bf16)
        scaled = (mixer[:, wide].astype(f32) * tail_l[:, wide]).astype(bf16)
        input_grad[:, cols] = local_b[:, cols] + dot(scaled, incoming[:, wide], 1, 1)


def block_of(total, most):
    size = min(total, most)
    while total % size:
        size -= LANES if size > LANES else 1
    return size


def small(dims, dtype):
    return math.prod(dims) * jnp.dtype(dtype).itemsize <= resident_bytes


def in_vmem(x):
    return pltpu.with_memory_space_constraint(x, pltpu.VMEM) if small(x.shape, x.dtype) else x


def vmem_out(dims, dtype):
    return pltpu.VMEM(dims, dtype) if small(dims, dtype) else jax.ShapeDtypeStruct(dims, dtype)


def cost(flops, moved):
    return pl.CostEstimate(flops=flops, transcendentals=0, bytes_accessed=moved)


def body(
    resid_input,
    norm_gain,
    expert_ids,
    route_probs,
    gate_weight,
    up_weight,
    down_weight,
    grad_output,
    mixer_input,
    state_input,
    state_output,
    step_size,
    log_retention,
    skip_gain,
):
    ctx = lax.axis_size("ctx")
    peers = lax.axis_size("exp")
    experts = peers // 2
    token_rows, model = resid_input.shape
    tokens, width = grad_output.shape
    capacity = 2 * tokens // experts
    slots = capacity // 2
    heads = skip_gain.shape[0]
    groups = state_input.shape[1] // N
    hidden = gate_weight.shape[1]
    gain = norm_gain.reshape(1, model)
    partner = [(i, i ^ 1) for i in range(peers)]
    shape = jax.ShapeDtypeStruct

    packed = pl.pallas_call(
        pack_kernel,
        out_shape=shape((peers, token_rows, width + LANES), bf16),
        compiler_params=params(),
        name="pack",
    )(resid_input, expert_ids.T, route_probs.T)
    packed = lax.all_to_all(packed, "exp", split_axis=0, concat_axis=0, tiled=True)

    mix, weigh, step_l, tail_l, head_l, skip_l, total_l = pl.pallas_call(
        partial(mixer_setup_kernel, groups=groups),
        out_shape=(
            shape((heads, tokens, tokens), bf16),
            shape((heads, tokens, tokens), f32),
            shape((tokens, width), f32),
            shape((tokens, width), f32),
            shape((tokens, width), f32),
            shape((8, width), f32),
            shape((8, width), f32),
        ),
        compiler_params=params(),
        cost_estimate=cost(2 * 10**9, 2 * 10**6),
        name="mixer_setup",
    )(log_retention.T, step_size.T, skip_gain.reshape(1, heads), state_input, state_output)

    table, shares, rows_x = pl.pallas_call(
        partial(dispatch_kernel, experts=experts, capacity=capacity),
        out_shape=(
            shape((experts * capacity, tokens), bf16),
            shape((experts * capacity, tokens), bf16),
            shape((ctx, experts * capacity, width), bf16),
        ),
        compiler_params=params(),
        name="dispatch",
    )(in_vmem(packed.reshape(tokens, width + LANES)))
    rows_g = pl.pallas_call(
        select_kernel,
        out_shape=shape((ctx, experts * capacity, width), bf16),
        compiler_params=params(),
        cost_estimate=cost(10**9, 2 * 10**6),
        name="select",
    )(table, grad_output)

    def spread(rows):
        got = lax.all_to_all(
            rows.reshape(ctx * peers, slots, width), ("ctx", "exp"), split_axis=0, concat_axis=0, tiled=True
        ).reshape(ctx, peers, slots, width)
        return got, lax.ppermute(got, "exp", partner)

    own_x, other_x = spread(rows_x)
    own_g, other_g = spread(rows_g)
    rows = 2 * ctx * slots
    half = rows // 2
    slab = (ctx, peers, slots, width)
    block = block_of(hidden, 256)
    blocks = hidden // block
    weight_spec = pl.BlockSpec((1, block, model), lambda i: (0, i, 0))
    act_spec = pl.BlockSpec((rows, block), lambda i: (0, i))
    product = 2 * rows * model * hidden
    coef_gate, coef_up, inverses = pl.pallas_call(
        gate_up_kernel,
        grid=(blocks,),
        in_specs=[whole(slab), whole(slab), whole((1, model)), weight_spec, weight_spec],
        out_specs=[act_spec, act_spec, whole((half, LANES))],
        out_shape=(shape((rows, hidden), f32), shape((rows, hidden), f32), shape((half, LANES), f32)),
        scratch_shapes=[pltpu.VMEM((rows, model), bf16)],
        compiler_params=params(1),
        cost_estimate=cost(2 * product, 4 * model * hidden),
        name="gate_up",
    )(in_vmem(own_x), in_vmem(other_x), gain, gate_weight, up_weight)
    column = block_of(model, 512)
    columns = model // column
    any_spec = pl.BlockSpec(memory_space=pl.ANY)
    vmem_spec = pl.BlockSpec(memory_space=pltpu.VMEM)
    out_own, out_other = pl.pallas_call(
        back_kernel,
        in_specs=[vmem_spec, vmem_spec] + [any_spec] * 5,
        out_specs=[vmem_spec, vmem_spec],
        out_shape=(vmem_out((half, model), bf16), vmem_out((half, model), bf16)),
        scratch_shapes=[
            pltpu.VMEM((rows, model), bf16),
            pltpu.VMEM((rows, hidden), f32),
            pltpu.VMEM((rows, hidden), f32),
            pltpu.VMEM((rows, hidden), bf16),
            pltpu.VMEM((rows, hidden), bf16),
            pltpu.VMEM((blocks, block, model), bf16),
            pltpu.VMEM((columns, hidden, column), bf16),
            pltpu.VMEM((columns, hidden, column), bf16),
            pltpu.SemaphoreType.DMA((blocks + 2 * columns + 2,)),
        ],
        compiler_params=params(),
        cost_estimate=cost(3 * product, 6 * model * hidden),
        name="back",
    )(in_vmem(own_g), in_vmem(other_g), coef_gate, coef_up, gate_weight, up_weight, down_weight)

    swapped = lax.ppermute(out_other, "exp", partner)
    moved = pl.pallas_call(
        slot_kernel,
        out_shape=shape((ctx, peers, slots, width), bf16),
        scratch_shapes=[pltpu.VMEM((half, model), f32)],
        compiler_params=params(),
        name="slot",
    )(in_vmem(out_own), in_vmem(swapped), gain, inverses, own_x)
    moved = lax.all_to_all(
        moved.reshape(ctx * peers, slots, width), ("ctx", "exp"), split_axis=0, concat_axis=0, tiled=True
    ).reshape(ctx, experts * capacity, width)

    upstream, resid_grad, state = pl.pallas_call(
        upstream_kernel,
        out_shape=(
            shape((tokens, width), f32),
            shape((tokens, width), bf16),
            shape((N + 16, width), bf16),
        ),
        compiler_params=params(),
        name="upstream",
    )(in_vmem(moved), shares, grad_output, state_output, head_l, total_l)
    states = [
        lax.ppermute(state, "ctx", [(i, i - k) for i in range(k, ctx)]) for k in range(1, ctx)
    ]
    base, local_b = pl.pallas_call(
        mixer_local_kernel,
        out_shape=(shape((tokens, width), f32), shape((tokens, groups * N), f32)),
        compiler_params=params(),
        cost_estimate=cost(3 * 10**9, 2 * 10**6),
        name="mixer_local",
    )(upstream, resid_grad, mixer_input, state_output, mix, weigh, step_l, skip_l)
    mixer_grad, state_input_grad = pl.pallas_call(
        mixer_far_kernel,
        out_shape=(shape((tokens, width), bf16), shape((tokens, groups * N), f32)),
        compiler_params=params(),
        name="mixer_far",
    )(*map(in_vmem, states), base, local_b, mixer_input, state_input, tail_l)
    return (resid_grad, mixer_grad, state_input_grad)


def solution(mesh):
    in_specs = (
        P(("ctx", "exp"), None),
        P(),
        P(("ctx", "exp"), None),
        P(("ctx", "exp"), None),
        P("exp", "ctx", None),
        P("exp", "ctx", None),
        P("exp", "ctx", None),
        P("ctx", "exp"),
        P("ctx", "exp"),
        P("ctx", "exp"),
        P("ctx", "exp"),
        P("ctx", "exp"),
        P("ctx", "exp"),
        P("exp"),
    )
    out_specs = (P("ctx", "exp"), P("ctx", "exp"), P("ctx", "exp"))
    return jax.shard_map(body, mesh=mesh, in_specs=in_specs, out_specs=out_specs, check_vma=False)
```

```python
import math
from functools import partial

import jax
import jax.numpy as jnp
from jax import lax
from jax.experimental import pallas as pl
from jax.experimental.pallas import tpu as pltpu
from jax.sharding import PartitionSpec as P


N = 128
LANES = 128
norm_epsilon = 1e-05
f32 = jnp.float32
bf16 = jnp.bfloat16
highest = lax.Precision.HIGHEST
vmem_bytes = 56 * 1024 * 1024
resident_bytes = 1024 * 1024


def params(steps=0, limit=vmem_bytes):
    return pltpu.CompilerParams(dimension_semantics=("arbitrary",) * steps, vmem_limit_bytes=limit)


def whole(shape):
    return pl.BlockSpec(shape, lambda *_: (0,) * len(shape))


def iota(shape, dim):
    return lax.broadcasted_iota(jnp.int32, shape, dim)


def dot(a, b, ca, cb, precision=None):
    return lax.dot_general(
        a, b, (((ca,), (cb,)), ((), ())), precision=precision, preferred_element_type=f32
    )


def pack_kernel(resid, ids_t, probs_t, out):
    peers, rows = out.shape[0], out.shape[1]
    width = out.shape[2] - LANES
    eye = jnp.where(iota((rows, rows), 0) == iota((rows, rows), 1), 1.0, 0.0).astype(bf16)
    ids = dot(eye, ids_t[...].astype(f32).astype(bf16), 1, 1)
    probs = dot(eye, probs_t[...], 1, 1)
    lane = iota((rows, LANES), 1)
    meta = jnp.where(lane == 0, ids[:, 0:1], 0.0) + jnp.where(lane == 1, ids[:, 1:2], 0.0)
    meta = meta + jnp.where(lane == 2, probs[:, 0:1], 0.0) + jnp.where(lane == 3, probs[:, 1:2], 0.0)
    meta = meta.astype(bf16)
    for j in range(peers):
        out[j, :, :width] = resid[:, j * width : (j + 1) * width]
        out[j, :, width:] = meta


def dispatch_kernel(packed, table, shares, rows_x, *, experts, capacity):
    tokens = packed.shape[0]
    width = packed.shape[1] - LANES
    meta = packed[:, width:].astype(f32)
    lane = iota((tokens, LANES), 1).astype(f32)
    first = meta[:, 0:1] == lane
    second = meta[:, 1:2] == lane
    member = jnp.where(first | second, 1.0, 0.0).astype(bf16)
    weight = (jnp.where(first, meta[:, 2:3], 0.0) + jnp.where(second, meta[:, 3:4], 0.0)).astype(bf16)
    row = iota((tokens, tokens), 0)
    col = iota((tokens, tokens), 1)
    before = jnp.where(row < col, 1.0, 0.0).astype(bf16)
    same = jnp.where(row == col, 1.0, 0.0).astype(bf16)
    position = dot(member, before, 0, 0)
    member_t = dot(member, same, 0, 0)
    weight_t = dot(weight, same, 0, 0)
    slot = iota((capacity, tokens), 0).astype(f32)
    for e in range(experts):
        hit = (slot == position[e : e + 1, :]) & (member_t[e : e + 1, :] > 0.5)
        entry = jnp.where(hit, 1.0, 0.0)
        table[e * capacity : (e + 1) * capacity, :] = entry.astype(bf16)
        shares[e * capacity : (e + 1) * capacity, :] = (entry * weight_t[e : e + 1, :]).astype(bf16)
    out_x = dot(table[...], packed[:, :width], 1, 0).astype(bf16)
    for c in range(rows_x.shape[0]):
        rows_x[c] = out_x


def select_kernel(table, grad, rows_g):
    out_g = dot(table[...], grad[...], 1, 0).astype(bf16)
    for c in range(rows_g.shape[0]):
        rows_g[c] = out_g


def gate_up_kernel(own, other, gain, gate_w, up_w, coef_gate, coef_up, inverses, normed):
    ctx, peers, slots, width = own.shape
    half = ctx * slots
    model = peers * width

    @pl.when(pl.program_id(0) == 0)
    def _():
        for side, ref in enumerate((own, other)):
            total = jnp.zeros((half, 1), f32)
            for j in range(peers):
                x = ref[:, j].reshape(half, width).astype(f32)
                total = total + jnp.sum(x * x, axis=1, keepdims=True)
            inverse = lax.rsqrt(total * (1.0 / model) + norm_epsilon)
            if side == 0:
                inverses[...] = jnp.broadcast_to(inverse, (half, LANES))
            for j in range(peers):
                x = ref[:, j].reshape(half, width).astype(f32)
                cols = slice(j * width, (j + 1) * width)
                normed[side * half : (side + 1) * half, cols] = (x * inverse * gain[:, cols]).astype(bf16)

    rows = normed[...]
    gate = dot(rows, gate_w[0], 1, 1)
    up = dot(rows, up_w[0], 1, 1)
    sig = jax.nn.sigmoid(gate)
    coef_gate[...] = up * sig * (1.0 + gate * (1.0 - sig))
    coef_up[...] = gate * sig


def back_kernel(
    own, other, coef_gate_hbm, coef_up_hbm, gate_hbm, up_hbm, down_hbm, out_own, out_other,
    grads, coef_gate, coef_up, gate_grad, up_grad, down_w, gate_w, up_w, sems,
):
    ctx, peers, slots, width = own.shape
    half = ctx * slots
    blocks, block, _ = down_w.shape
    columns, _, column = gate_w.shape

    def down_copy(i):
        return pltpu.make_async_copy(down_hbm.at[0, i * block : (i + 1) * block, :], down_w.at[i], sems.at[i])

    def pair_copies(i):
        cols = slice(i * column, (i + 1) * column)
        at = blocks + 2 * i
        return (
            pltpu.make_async_copy(gate_hbm.at[0, :, cols], gate_w.at[i], sems.at[at]),
            pltpu.make_async_copy(up_hbm.at[0, :, cols], up_w.at[i], sems.at[at + 1]),
        )

    coef_copies = (
        pltpu.make_async_copy(coef_gate_hbm, coef_gate, sems.at[blocks + 2 * columns]),
        pltpu.make_async_copy(coef_up_hbm, coef_up, sems.at[blocks + 2 * columns + 1]),
    )
    down_copy(0).start()
    for copy in coef_copies:
        copy.start()
    for i in range(1, blocks):
        down_copy(i).start()
    for i in range(columns):
        for copy in pair_copies(i):
            copy.start()
    for side, ref in enumerate((own, other)):
        for j in range(peers):
            cols = slice(j * width, (j + 1) * width)
            grads[side * half : (side + 1) * half, cols] = ref[:, j].reshape(half, width)
    rows = grads[...]
    for i in range(blocks):
        down_copy(i).wait()
        part = slice(i * block, (i + 1) * block)
        grad = dot(rows, down_w[i], 1, 1)
        if i == 0:
            for copy in coef_copies:
                copy.wait()
        gate_grad[:, part] = (grad * coef_gate[:, part]).astype(bf16)
        up_grad[:, part] = (grad * coef_up[:, part]).astype(bf16)
    for i in range(columns):
        for copy in pair_copies(i):
            copy.wait()
        cols = slice(i * column, (i + 1) * column)
        out = (dot(gate_grad[...], gate_w[i], 1, 0) + dot(up_grad[...], up_w[i], 1, 0)).astype(bf16)
        out_own[:, cols] = out[:half]
        out_other[:, cols] = out[half:]


def slot_kernel(own, swapped, gain, inverses, x_rows, out, sums):
    ctx, peers, slots, width = x_rows.shape
    half = ctx * slots
    model = peers * width
    product = jnp.zeros((half, 1), f32)
    for j in range(peers):
        cols = slice(j * width, (j + 1) * width)
        total = (own[:, cols].astype(f32) + swapped[:, cols].astype(f32)) * gain[:, cols]
        sums[:, cols] = total
        x = x_rows[:, j].reshape(half, width).astype(f32)
        product = product + jnp.sum(total * x, axis=1, keepdims=True)
    inverse = inverses[:, 0:1]
    shift = inverse * inverse * inverse * product * (1.0 / model)
    for j in range(peers):
        cols = slice(j * width, (j + 1) * width)
        x = x_rows[:, j].reshape(half, width).astype(f32)
        out[:, j] = (sums[:, cols] * inverse - x * shift).astype(bf16).reshape(ctx, slots, width)


def mixer_setup_kernel(
    log_t, step_t, skip, state_in, state_out, mix, weigh, step_l, tail_l, head_l, skip_l, total_l, *, groups
):
    heads, tokens = log_t.shape
    width = step_l.shape[1]
    size = width // heads
    row = iota((tokens, tokens), 0)
    col = iota((tokens, tokens), 1)
    upto = jnp.where(row <= col, 1.0, 0.0)
    eye = jnp.where(row == col, 1.0, 0.0)
    cum_t = dot(log_t[...], upto, 1, 0, highest)
    cum = dot(upto, log_t[...], 0, 1, highest)
    steps = dot(eye, step_t[...], 1, 1, highest)
    last = cum[tokens - 1 : tokens, :]
    spread = jnp.where(iota((heads, width), 0) == iota((heads, width), 1) // size, 1.0, 0.0)
    step_l[...] = dot(steps, spread, 1, 0, highest)
    tail_l[...] = dot(steps * jnp.exp(last - cum), spread, 1, 0, highest)
    head_l[...] = dot(jnp.exp(cum), spread, 1, 0, highest)
    skip_l[...] = dot(jnp.broadcast_to(skip[...], (8, heads)), spread, 1, 0, highest)
    total_l[...] = dot(jnp.broadcast_to(jnp.exp(last), (8, heads)), spread, 1, 0, highest)
    later = col >= row
    for g in range(groups):
        cols = slice(g * N, (g + 1) * N)
        inter = dot(state_in[:, cols], state_out[:, cols], 1, 1)
        for h in range(g * heads // groups, (g + 1) * heads // groups):
            gap = cum_t[h : h + 1, :] - cum[:, h : h + 1]
            decay = jnp.where(later, jnp.exp(jnp.where(later, gap, 0.0)), 0.0)
            mix[h] = (decay * inter).astype(bf16)
            weigh[h] = decay * steps[:, h : h + 1]


def upstream_kernel(moved, shares, grad, state_out, head_l, total_l, upstream, resid_grad, state):
    width = grad.shape[1]
    groups = state_out.shape[1] // N
    span = width // groups
    moe = dot(shares[...], moved[0], 0, 0)
    for c in range(1, moved.shape[0]):
        moe = moe + dot(shares[...], moved[c], 0, 0)
    moe = moe.astype(bf16)
    up = grad[...].astype(f32) + moe.astype(f32)
    upstream[...] = up
    resid_grad[...] = up.astype(bf16)
    for g in range(groups):
        cols = slice(g * N, (g + 1) * N)
        wide = slice(g * span, (g + 1) * span)
        scaled = (up[:, wide] * head_l[:, wide]).astype(bf16)
        state[0:N, wide] = dot(state_out[:, cols], scaled, 0, 0).astype(bf16)
    total = total_l[...]
    high = total.astype(bf16).astype(f32)
    state[N : N + 8, :] = jnp.where(iota(total.shape, 0) == 0, high, total - high).astype(bf16)


def mixer_local_kernel(upstream, resid_grad, mixer, state_out, mix, weigh, step_l, skip_l, base, local_b):
    tokens, width = upstream.shape
    heads = mix.shape[0]
    size = width // heads
    groups = state_out.shape[1] // N
    for g in range(groups):
        cols = slice(g * N, (g + 1) * N)
        weighted = jnp.zeros((tokens, tokens), f32)
        for h in range(g * heads // groups, (g + 1) * heads // groups):
            part = slice(h * size, (h + 1) * size)
            up_h = resid_grad[:, part]
            mixed = dot(mix[h], up_h, 1, 0)
            base[:, part] = step_l[:, part] * mixed + skip_l[0:1, part] * upstream[:, part]
            weighted = weighted + weigh[h] * dot(mixer[:, part], up_h, 1, 1)
        local_b[:, cols] = dot(weighted.astype(bf16), state_out[:, cols], 1, 0)


def mixer_far_kernel(*refs):
    base, local_b, mixer, state_in, tail_l, mixer_grad, input_grad = refs[-7:]
    states = refs[:-7]
    groups = state_in.shape[1] // N
    width = base.shape[1]
    span = width // groups
    incoming = states[-1][0:N, :].astype(f32)
    for ref in states[-2::-1]:
        decay = ref[N : N + 1, :].astype(f32) + ref[N + 1 : N + 2, :].astype(f32)
        incoming = ref[0:N, :].astype(f32) + decay * incoming
    incoming = incoming.astype(bf16)
    for g in range(groups):
        cols = slice(g * N, (g + 1) * N)
        wide = slice(g * span, (g + 1) * span)
        far = dot(state_in[:, cols], incoming[:, wide], 1, 0)
        mixer_grad[:, wide] = (base[:, wide] + tail_l[:, wide] * far).astype(bf16)
        scaled = (mixer[:, wide].astype(f32) * tail_l[:, wide]).astype(bf16)
        input_grad[:, cols] = local_b[:, cols] + dot(scaled, incoming[:, wide], 1, 1)


def block_of(total, most):
    size = min(total, most)
    while total % size:
        size -= LANES if size > LANES else 1
    return size


def small(dims, dtype):
    return math.prod(dims) * jnp.dtype(dtype).itemsize <= resident_bytes


def in_vmem(x):
    return pltpu.with_memory_space_constraint(x, pltpu.VMEM) if small(x.shape, x.dtype) else x


def vmem_out(dims, dtype):
    return pltpu.VMEM(dims, dtype) if small(dims, dtype) else jax.ShapeDtypeStruct(dims, dtype)


def cost(flops, moved):
    return pl.CostEstimate(flops=flops, transcendentals=0, bytes_accessed=moved)


def body(
    resid_input,
    norm_gain,
    expert_ids,
    route_probs,
    gate_weight,
    up_weight,
    down_weight,
    grad_output,
    mixer_input,
    state_input,
    state_output,
    step_size,
    log_retention,
    skip_gain,
):
    ctx = lax.axis_size("ctx")
    peers = lax.axis_size("exp")
    experts = peers // 2
    token_rows, model = resid_input.shape
    tokens, width = grad_output.shape
    capacity = 2 * tokens // experts
    slots = capacity // 2
    heads = skip_gain.shape[0]
    groups = state_input.shape[1] // N
    hidden = gate_weight.shape[1]
    gain = norm_gain.reshape(1, model)
    partner = [(i, i ^ 1) for i in range(peers)]
    shape = jax.ShapeDtypeStruct

    packed = pl.pallas_call(
        pack_kernel,
        out_shape=vmem_out((peers, token_rows, width + LANES), bf16),
        compiler_params=params(),
        name="pack",
    )(resid_input, expert_ids.T, route_probs.T)
    packed = lax.all_to_all(packed, "exp", split_axis=0, concat_axis=0, tiled=True)

    mix, weigh, step_l, tail_l, head_l, skip_l, total_l = pl.pallas_call(
        partial(mixer_setup_kernel, groups=groups),
        out_shape=(
            shape((heads, tokens, tokens), bf16),
            shape((heads, tokens, tokens), f32),
            shape((tokens, width), f32),
            shape((tokens, width), f32),
            shape((tokens, width), f32),
            shape((8, width), f32),
            shape((8, width), f32),
        ),
        compiler_params=params(),
        cost_estimate=cost(2 * 10**9, 2 * 10**6),
        name="mixer_setup",
    )(log_retention.T, step_size.T, skip_gain.reshape(1, heads), state_input, state_output)

    table, shares, rows_x = pl.pallas_call(
        partial(dispatch_kernel, experts=experts, capacity=capacity),
        out_shape=(
            shape((experts * capacity, tokens), bf16),
            shape((experts * capacity, tokens), bf16),
            vmem_out((ctx, experts * capacity, width), bf16),
        ),
        compiler_params=params(),
        name="dispatch",
    )(in_vmem(packed.reshape(tokens, width + LANES)))
    rows_g = pl.pallas_call(
        select_kernel,
        out_shape=shape((ctx, experts * capacity, width), bf16),
        compiler_params=params(),
        cost_estimate=cost(10**9, 2 * 10**6),
        name="select",
    )(table, grad_output)

    def spread(rows):
        got = lax.all_to_all(
            rows.reshape(ctx * peers, slots, width), ("ctx", "exp"), split_axis=0, concat_axis=0, tiled=True
        ).reshape(ctx, peers, slots, width)
        return got, lax.ppermute(got, "exp", partner)

    own_x, other_x = spread(rows_x)
    own_g, other_g = spread(rows_g)
    rows = 2 * ctx * slots
    half = rows // 2
    slab = (ctx, peers, slots, width)
    block = block_of(hidden, 256)
    blocks = hidden // block
    weight_spec = pl.BlockSpec((1, block, model), lambda i: (0, i, 0))
    act_spec = pl.BlockSpec((rows, block), lambda i: (0, i))
    product = 2 * rows * model * hidden
    coef_gate, coef_up, inverses = pl.pallas_call(
        gate_up_kernel,
        grid=(blocks,),
        in_specs=[whole(slab), whole(slab), whole((1, model)), weight_spec, weight_spec],
        out_specs=[act_spec, act_spec, whole((half, LANES))],
        out_shape=(shape((rows, hidden), f32), shape((rows, hidden), f32), shape((half, LANES), f32)),
        scratch_shapes=[pltpu.VMEM((rows, model), bf16)],
        compiler_params=params(1),
        cost_estimate=cost(2 * product, 4 * model * hidden),
        name="gate_up",
    )(in_vmem(own_x), in_vmem(other_x), gain, gate_weight, up_weight)
    column = block_of(model, 512)
    columns = model // column
    any_spec = pl.BlockSpec(memory_space=pl.ANY)
    vmem_spec = pl.BlockSpec(memory_space=pltpu.VMEM)
    out_own, out_other = pl.pallas_call(
        back_kernel,
        in_specs=[vmem_spec, vmem_spec] + [any_spec] * 5,
        out_specs=[vmem_spec, vmem_spec],
        out_shape=(vmem_out((half, model), bf16), vmem_out((half, model), bf16)),
        scratch_shapes=[
            pltpu.VMEM((rows, model), bf16),
            pltpu.VMEM((rows, hidden), f32),
            pltpu.VMEM((rows, hidden), f32),
            pltpu.VMEM((rows, hidden), bf16),
            pltpu.VMEM((rows, hidden), bf16),
            pltpu.VMEM((blocks, block, model), bf16),
            pltpu.VMEM((columns, hidden, column), bf16),
            pltpu.VMEM((columns, hidden, column), bf16),
            pltpu.SemaphoreType.DMA((blocks + 2 * columns + 2,)),
        ],
        compiler_params=params(),
        cost_estimate=cost(3 * product, 6 * model * hidden),
        name="back",
    )(in_vmem(own_g), in_vmem(other_g), coef_gate, coef_up, gate_weight, up_weight, down_weight)

    swapped = lax.ppermute(out_other, "exp", partner)
    moved = pl.pallas_call(
        slot_kernel,
        out_shape=vmem_out((ctx, peers, slots, width), bf16),
        scratch_shapes=[pltpu.VMEM((half, model), f32)],
        compiler_params=params(),
        name="slot",
    )(in_vmem(out_own), in_vmem(swapped), gain, in_vmem(inverses), in_vmem(own_x))
    moved = lax.all_to_all(
        moved.reshape(ctx * peers, slots, width), ("ctx", "exp"), split_axis=0, concat_axis=0, tiled=True
    ).reshape(ctx, experts * capacity, width)

    upstream, resid_grad, state = pl.pallas_call(
        upstream_kernel,
        out_shape=(
            vmem_out((tokens, width), f32),
            vmem_out((tokens, width), bf16),
            vmem_out((N + 8, width), bf16),
        ),
        compiler_params=params(),
        name="upstream",
    )(*map(in_vmem, (moved, shares, grad_output, state_output, head_l, total_l)))
    states = [
        lax.ppermute(state, "ctx", [(i, i - k) for i in range(k, ctx)]) for k in range(1, ctx)
    ]
    base, local_b = pl.pallas_call(
        mixer_local_kernel,
        out_shape=(vmem_out((tokens, width), f32), vmem_out((tokens, groups * N), f32)),
        compiler_params=params(),
        cost_estimate=cost(3 * 10**9, 2 * 10**6),
        name="mixer_local",
    )(*map(in_vmem, (upstream, resid_grad, mixer_input, state_output, mix, weigh, step_l, skip_l)))
    mixer_grad, state_input_grad = pl.pallas_call(
        mixer_far_kernel,
        out_shape=(shape((tokens, width), bf16), shape((tokens, groups * N), f32)),
        compiler_params=params(),
        name="mixer_far",
    )(*map(in_vmem, (*states, base, local_b, mixer_input, state_input, tail_l)))
    return (resid_grad, mixer_grad, state_input_grad)


def solution(mesh):
    in_specs = (
        P(("ctx", "exp"), None),
        P(),
        P(("ctx", "exp"), None),
        P(("ctx", "exp"), None),
        P("exp", "ctx", None),
        P("exp", "ctx", None),
        P("exp", "ctx", None),
        P("ctx", "exp"),
        P("ctx", "exp"),
        P("ctx", "exp"),
        P("ctx", "exp"),
        P("ctx", "exp"),
        P("ctx", "exp"),
        P("exp"),
    )
    out_specs = (P("ctx", "exp"), P("ctx", "exp"), P("ctx", "exp"))
    return jax.shard_map(body, mesh=mesh, in_specs=in_specs, out_specs=out_specs, check_vma=False)
```

```python
import math
from functools import partial

import jax
import jax.numpy as jnp
from jax import lax
from jax.experimental import pallas as pl
from jax.experimental.pallas import tpu as pltpu
from jax.sharding import PartitionSpec as P


N = 128
LANES = 128
norm_epsilon = 1e-05
f32 = jnp.float32
bf16 = jnp.bfloat16
highest = lax.Precision.HIGHEST
vmem_bytes = 56 * 1024 * 1024
resident_bytes = 2 * 1024 * 1024


def params(steps=0, limit=vmem_bytes):
    return pltpu.CompilerParams(dimension_semantics=("arbitrary",) * steps, vmem_limit_bytes=limit)


def iota(shape, dim):
    return lax.broadcasted_iota(jnp.int32, shape, dim)


def dot(a, b, ca, cb, precision=None):
    return lax.dot_general(
        a, b, (((ca,), (cb,)), ((), ())), precision=precision, preferred_element_type=f32
    )


def pack_kernel(resid, ids_t, probs_t, grad, out, grad_early):
    grad_early[...] = grad[:, : grad_early.shape[1]]
    peers, rows = out.shape[0], out.shape[1]
    width = out.shape[2] - LANES
    eye = jnp.where(iota((rows, rows), 0) == iota((rows, rows), 1), 1.0, 0.0).astype(bf16)
    ids = dot(eye, ids_t[...].astype(f32).astype(bf16), 1, 1)
    probs = dot(eye, probs_t[...], 1, 1)
    lane = iota((rows, LANES), 1)
    meta = jnp.where(lane == 0, ids[:, 0:1], 0.0) + jnp.where(lane == 1, ids[:, 1:2], 0.0)
    meta = meta + jnp.where(lane == 2, probs[:, 0:1], 0.0) + jnp.where(lane == 3, probs[:, 1:2], 0.0)
    meta = meta.astype(bf16)
    for j in range(peers):
        out[j, :, :width] = resid[:, j * width : (j + 1) * width]
        out[j, :, width:] = meta


def dispatch_kernel(packed, grad, table, shares, rows, *, experts, capacity):
    tokens = packed.shape[0]
    width = packed.shape[1] - LANES
    meta = packed[:, width:].astype(f32)
    lane = iota((tokens, LANES), 1).astype(f32)
    first = meta[:, 0:1] == lane
    second = meta[:, 1:2] == lane
    member = jnp.where(first | second, 1.0, 0.0).astype(bf16)
    weight = (jnp.where(first, meta[:, 2:3], 0.0) + jnp.where(second, meta[:, 3:4], 0.0)).astype(bf16)
    row = iota((tokens, tokens), 0)
    col = iota((tokens, tokens), 1)
    before = jnp.where(row < col, 1.0, 0.0).astype(bf16)
    same = jnp.where(row == col, 1.0, 0.0).astype(bf16)
    position = dot(member, before, 0, 0)
    member_t = dot(member, same, 0, 0)
    weight_t = dot(weight, same, 0, 0)
    slot = iota((capacity, tokens), 0).astype(f32)
    for e in range(experts):
        hit = (slot == position[e : e + 1, :]) & (member_t[e : e + 1, :] > 0.5)
        entry = jnp.where(hit, 1.0, 0.0)
        table[e * capacity : (e + 1) * capacity, :] = entry.astype(bf16)
        shares[e * capacity : (e + 1) * capacity, :] = (entry * weight_t[e : e + 1, :]).astype(bf16)
    out_x = dot(table[...], packed[:, :width], 1, 0).astype(bf16)
    out_g = dot(table[...], grad[...], 1, 0).astype(bf16)
    for c in range(rows.shape[0]):
        rows[c, :, :width] = out_x
        rows[c, :, width:] = out_g


def select_kernel(table, grad, rows):
    late = rows.shape[2]
    out_g = dot(table[...], grad[:, grad.shape[1] - late :], 1, 0).astype(bf16)
    for c in range(rows.shape[0]):
        rows[c] = out_g


def gather_rows(own, other, start, stop, out):
    ctx, peers, slots = own.shape[:3]
    half = ctx * slots
    for side, ref in enumerate((own, other)):
        for j in range(peers):
            at = slice(j * (stop - start), (j + 1) * (stop - start))
            out[side * half : (side + 1) * half, at] = ref[:, j, :, start:stop].reshape(half, stop - start)


def packed_copies(hbm, rows, width, start, stop, out, sems, base):
    size = stop - start
    return [
        pltpu.make_async_copy(
            hbm.at[0, rows, j * width + start : j * width + stop],
            out.at[rows, j * size : (j + 1) * size],
            sems.at[base + j],
        )
        for j in range(out.shape[1] // size)
    ]


def launch(copies):
    for copy in copies:
        copy.start()
    return copies


def finish(copies):
    for copy in copies:
        copy.wait()


def gate_up_kernel(
    own, other, gain, gate_hbm, up_hbm, down_hbm, coef_gate_hbm, coef_up_hbm, hidden_hbm, inverses,
    normed, grads, gate_w, up_w, down_w, coef_gate, coef_up, hidden_early, in_sems, out_sems, *, width, block,
):
    ctx, peers, slots, both = own.shape
    half = ctx * slots
    model = peers * width
    blocks = gate_w.shape[0] // block
    parts = [slice(i * block, (i + 1) * block) for i in range(blocks)]
    pairs = [
        launch(
            [
                pltpu.make_async_copy(gate_hbm.at[0, part, :], gate_w.at[part, :], in_sems.at[2 * i]),
                pltpu.make_async_copy(up_hbm.at[0, part, :], up_w.at[part, :], in_sems.at[2 * i + 1]),
            ]
        )
        for i, part in enumerate(parts)
    ]
    downs = launch(
        packed_copies(down_hbm, slice(0, gate_w.shape[0]), width, 0, both - width, down_w, in_sems, 2 * blocks)
    )
    for side, ref in enumerate((own, other)):
        total = jnp.zeros((half, 1), f32)
        for j in range(peers):
            x = ref[:, j, :, :width].reshape(half, width).astype(f32)
            total = total + jnp.sum(x * x, axis=1, keepdims=True)
        inverse = lax.rsqrt(total * (1.0 / model) + norm_epsilon)
        if side == 0:
            inverses[...] = jnp.broadcast_to(inverse, (half, LANES))
        for j in range(peers):
            x = ref[:, j, :, :width].reshape(half, width).astype(f32)
            cols = slice(j * width, (j + 1) * width)
            normed[side * half : (side + 1) * half, cols] = (x * inverse * gain[:, cols]).astype(bf16)
    gather_rows(own, other, width, both, grads)
    outs = []
    for i, part in enumerate(parts):
        finish(pairs[i])
        gate = dot(normed[...], gate_w[part, :], 1, 1)
        up = dot(normed[...], up_w[part, :], 1, 1)
        sig = jax.nn.sigmoid(gate)
        coef_gate[:, part] = up * sig * (1.0 + gate * (1.0 - sig))
        coef_up[:, part] = gate * sig
        outs += launch(
            [
                pltpu.make_async_copy(coef_gate.at[:, part], coef_gate_hbm.at[:, part], out_sems.at[3 * i]),
                pltpu.make_async_copy(coef_up.at[:, part], coef_up_hbm.at[:, part], out_sems.at[3 * i + 1]),
            ]
        )
    finish(downs)
    for i, part in enumerate(parts):
        hidden_early[:, part] = dot(grads[...], down_w[part, :], 1, 1)
        outs += launch(
            [pltpu.make_async_copy(hidden_early.at[:, part], hidden_hbm.at[:, part], out_sems.at[3 * i + 2])]
        )
    finish(outs)


def back_kernel(
    own, other, hidden_hbm, coef_gate_hbm, coef_up_hbm, gate_hbm, up_hbm, down_hbm, out_own, out_other,
    grads, hidden_early, coef_gate, coef_up, gate_grad, up_grad, gate_w, up_w, down_w, sems, *, width, block,
):
    ctx, peers, slots, late = own.shape
    half = ctx * slots
    columns, hidden, column = gate_w.shape
    blocks = hidden // block
    parts = [slice(i * block, (i + 1) * block) for i in range(blocks)]
    used = 0

    def copy(source, target):
        nonlocal used
        used += 1
        return pltpu.make_async_copy(source, target, sems.at[used - 1])

    waits = []
    for part in parts:
        downs = launch(packed_copies(down_hbm, part, width, width - late, width, down_w, sems, used))
        used += peers
        waits.append(
            downs
            + launch(
                [
                    copy(hidden_hbm.at[:, part], hidden_early.at[:, part]),
                    copy(coef_gate_hbm.at[:, part], coef_gate.at[:, part]),
                    copy(coef_up_hbm.at[:, part], coef_up.at[:, part]),
                ]
            )
        )
    slabs = [slice(i * column, (i + 1) * column) for i in range(columns)]
    pairs = [
        launch([copy(gate_hbm.at[0, :, cols], gate_w.at[i]), copy(up_hbm.at[0, :, cols], up_w.at[i])])
        for i, cols in enumerate(slabs)
    ]
    gather_rows(own, other, 0, late, grads)
    for i, part in enumerate(parts):
        finish(waits[i])
        grad = hidden_early[:, part] + dot(grads[...], down_w[part, :], 1, 1)
        gate_grad[:, part] = (grad * coef_gate[:, part]).astype(bf16)
        up_grad[:, part] = (grad * coef_up[:, part]).astype(bf16)
    for i, cols in enumerate(slabs):
        finish(pairs[i])
        out = (dot(gate_grad[...], gate_w[i], 1, 0) + dot(up_grad[...], up_w[i], 1, 0)).astype(bf16)
        out_own[:, cols] = out[:half]
        out_other[:, cols] = out[half:]


def slot_kernel(own, swapped, gain, inverses, x_rows, out, sums):
    ctx, peers, slots, width = out.shape
    half = ctx * slots
    model = peers * width
    product = jnp.zeros((half, 1), f32)
    for j in range(peers):
        cols = slice(j * width, (j + 1) * width)
        total = (own[:, cols].astype(f32) + swapped[:, cols].astype(f32)) * gain[:, cols]
        sums[:, cols] = total
        x = x_rows[:, j, :, :width].reshape(half, width).astype(f32)
        product = product + jnp.sum(total * x, axis=1, keepdims=True)
    inverse = inverses[:, 0:1]
    shift = inverse * inverse * inverse * product * (1.0 / model)
    for j in range(peers):
        cols = slice(j * width, (j + 1) * width)
        x = x_rows[:, j, :, :width].reshape(half, width).astype(f32)
        out[:, j] = (sums[:, cols] * inverse - x * shift).astype(bf16).reshape(ctx, slots, width)


def mixer_setup_kernel(
    log_t, step_t, skip, state_in, state_out, mix, weigh, step_l, tail_l, head_l, skip_l, total_l, *, groups
):
    heads, tokens = log_t.shape
    width = step_l.shape[1]
    size = width // heads
    row = iota((tokens, tokens), 0)
    col = iota((tokens, tokens), 1)
    upto = jnp.where(row <= col, 1.0, 0.0)
    eye = jnp.where(row == col, 1.0, 0.0)
    cum_t = dot(log_t[...], upto, 1, 0, highest)
    cum = dot(upto, log_t[...], 0, 1, highest)
    steps = dot(eye, step_t[...], 1, 1, highest)
    last = cum[tokens - 1 : tokens, :]
    spread = jnp.where(iota((heads, width), 0) == iota((heads, width), 1) // size, 1.0, 0.0)
    step_l[...] = dot(steps, spread, 1, 0, highest)
    tail_l[...] = dot(steps * jnp.exp(last - cum), spread, 1, 0, highest)
    head_l[...] = dot(jnp.exp(cum), spread, 1, 0, highest)
    skip_l[...] = dot(jnp.broadcast_to(skip[...], (8, heads)), spread, 1, 0, highest)
    total_l[...] = dot(jnp.broadcast_to(jnp.exp(last), (8, heads)), spread, 1, 0, highest)
    later = col >= row
    for g in range(groups):
        cols = slice(g * N, (g + 1) * N)
        inter = dot(state_in[:, cols], state_out[:, cols], 1, 1)
        for h in range(g * heads // groups, (g + 1) * heads // groups):
            gap = cum_t[h : h + 1, :] - cum[:, h : h + 1]
            decay = jnp.where(later, jnp.exp(jnp.where(later, gap, 0.0)), 0.0)
            mix[h] = (decay * inter).astype(bf16)
            weigh[h] = decay * steps[:, h : h + 1]


def upstream_kernel(moved, shares, grad, state_out, head_l, total_l, upstream, resid_grad, state):
    width = grad.shape[1]
    groups = state_out.shape[1] // N
    span = width // groups
    moe = dot(shares[...], moved[0], 0, 0)
    for c in range(1, moved.shape[0]):
        moe = moe + dot(shares[...], moved[c], 0, 0)
    moe = moe.astype(bf16)
    up = grad[...].astype(f32) + moe.astype(f32)
    upstream[...] = up
    resid_grad[...] = up.astype(bf16)
    for g in range(groups):
        cols = slice(g * N, (g + 1) * N)
        wide = slice(g * span, (g + 1) * span)
        scaled = (up[:, wide] * head_l[:, wide]).astype(bf16)
        state[0:N, wide] = dot(state_out[:, cols], scaled, 0, 0).astype(bf16)
    total = total_l[...]
    high = total.astype(bf16).astype(f32)
    state[N : N + 8, :] = jnp.where(iota(total.shape, 0) == 0, high, total - high).astype(bf16)


def mixer_local_kernel(upstream, resid_grad, mixer, state_out, mix, weigh, step_l, skip_l, base, local_b):
    tokens, width = upstream.shape
    heads = mix.shape[0]
    size = width // heads
    groups = state_out.shape[1] // N
    for g in range(groups):
        cols = slice(g * N, (g + 1) * N)
        weighted = jnp.zeros((tokens, tokens), f32)
        for h in range(g * heads // groups, (g + 1) * heads // groups):
            part = slice(h * size, (h + 1) * size)
            up_h = resid_grad[:, part]
            mixed = dot(mix[h], up_h, 1, 0)
            base[:, part] = step_l[:, part] * mixed + skip_l[0:1, part] * upstream[:, part]
            weighted = weighted + weigh[h] * dot(mixer[:, part], up_h, 1, 1)
        local_b[:, cols] = dot(weighted.astype(bf16), state_out[:, cols], 1, 0)


def join_kernel(first, later, out):
    decay = first[N : N + 1, :].astype(f32) + first[N + 1 : N + 2, :].astype(f32)
    out[0:N, :] = (first[0:N, :].astype(f32) + decay * later[0:N, :].astype(f32)).astype(bf16)
    total = decay * (later[N : N + 1, :].astype(f32) + later[N + 1 : N + 2, :].astype(f32))
    total = jnp.broadcast_to(total, (8, total.shape[1]))
    high = total.astype(bf16).astype(f32)
    out[N : N + 8, :] = jnp.where(iota(total.shape, 0) == 0, high, total - high).astype(bf16)


def mixer_far_kernel(*refs):
    base, local_b, mixer, state_in, tail_l, mixer_grad, input_grad = refs[-7:]
    states = refs[:-7]
    groups = state_in.shape[1] // N
    width = base.shape[1]
    span = width // groups
    incoming = states[-1][0:N, :].astype(f32)
    for ref in states[-2::-1]:
        decay = ref[N : N + 1, :].astype(f32) + ref[N + 1 : N + 2, :].astype(f32)
        incoming = ref[0:N, :].astype(f32) + decay * incoming
    incoming = incoming.astype(bf16)
    for g in range(groups):
        cols = slice(g * N, (g + 1) * N)
        wide = slice(g * span, (g + 1) * span)
        far = dot(state_in[:, cols], incoming[:, wide], 1, 0)
        mixer_grad[:, wide] = (base[:, wide] + tail_l[:, wide] * far).astype(bf16)
        scaled = (mixer[:, wide].astype(f32) * tail_l[:, wide]).astype(bf16)
        input_grad[:, cols] = local_b[:, cols] + dot(scaled, incoming[:, wide], 1, 1)


def block_of(total, most):
    size = min(total, most)
    while total % size:
        size -= LANES if size > LANES else 1
    return size


def small(dims, dtype):
    return math.prod(dims) * jnp.dtype(dtype).itemsize <= resident_bytes


def in_vmem(x):
    return pltpu.with_memory_space_constraint(x, pltpu.VMEM) if small(x.shape, x.dtype) else x


def vmem_out(dims, dtype):
    return pltpu.VMEM(dims, dtype) if small(dims, dtype) else jax.ShapeDtypeStruct(dims, dtype)


def cost(flops, moved):
    return pl.CostEstimate(flops=flops, transcendentals=0, bytes_accessed=moved)


def body(
    resid_input,
    norm_gain,
    expert_ids,
    route_probs,
    gate_weight,
    up_weight,
    down_weight,
    grad_output,
    mixer_input,
    state_input,
    state_output,
    step_size,
    log_retention,
    skip_gain,
):
    ctx = lax.axis_size("ctx")
    peers = lax.axis_size("exp")
    experts = peers // 2
    token_rows, model = resid_input.shape
    tokens, width = grad_output.shape
    capacity = 2 * tokens // experts
    slots = capacity // 2
    heads = skip_gain.shape[0]
    groups = state_input.shape[1] // N
    hidden = gate_weight.shape[1]
    early = width // 2
    gain = norm_gain.reshape(1, model)
    partner = [(i, i ^ 1) for i in range(peers)]
    shape = jax.ShapeDtypeStruct

    packed, grad_early = pl.pallas_call(
        pack_kernel,
        out_shape=(
            vmem_out((peers, token_rows, width + LANES), bf16),
            vmem_out((tokens, early), bf16),
        ),
        compiler_params=params(),
        name="pack",
    )(resid_input, expert_ids.T, route_probs.T, grad_output)
    packed = lax.all_to_all(packed, "exp", split_axis=0, concat_axis=0, tiled=True)

    mix, weigh, step_l, tail_l, head_l, skip_l, total_l = pl.pallas_call(
        partial(mixer_setup_kernel, groups=groups),
        out_shape=(
            shape((heads, tokens, tokens), bf16),
            shape((heads, tokens, tokens), f32),
            shape((tokens, width), f32),
            shape((tokens, width), f32),
            shape((tokens, width), f32),
            shape((8, width), f32),
            shape((8, width), f32),
        ),
        compiler_params=params(),
        cost_estimate=cost(2 * 10**9, 2 * 10**6),
        name="mixer_setup",
    )(log_retention.T, step_size.T, skip_gain.reshape(1, heads), state_input, state_output)

    table, shares, rows_early = pl.pallas_call(
        partial(dispatch_kernel, experts=experts, capacity=capacity),
        out_shape=(
            shape((experts * capacity, tokens), bf16),
            shape((experts * capacity, tokens), bf16),
            vmem_out((ctx, experts * capacity, width + early), bf16),
        ),
        compiler_params=params(),
        name="dispatch",
    )(in_vmem(packed.reshape(tokens, width + LANES)), in_vmem(grad_early))
    rows_late = pl.pallas_call(
        select_kernel,
        out_shape=vmem_out((ctx, experts * capacity, width - early), bf16),
        compiler_params=params(),
        cost_estimate=cost(10**9, 2 * 10**6),
        name="select",
    )(table, grad_output)

    def spread(rows):
        got = lax.all_to_all(
            rows.reshape(ctx * peers, slots, -1), ("ctx", "exp"), split_axis=0, concat_axis=0, tiled=True
        ).reshape(ctx, peers, slots, -1)
        return in_vmem(got), in_vmem(lax.ppermute(got, "exp", partner))

    own_x, other_x = spread(rows_early)
    own_g, other_g = spread(rows_late)
    rows = 2 * ctx * slots
    half = rows // 2
    block = block_of(hidden, 512)
    blocks = hidden // block
    column = block_of(model, 512)
    columns = model // column
    product = 2 * rows * model * hidden
    any_spec = pl.BlockSpec(memory_space=pl.ANY)
    vmem_spec = pl.BlockSpec(memory_space=pltpu.VMEM)
    acts = pltpu.VMEM((rows, hidden), f32)
    coef_gate, coef_up, hidden_early, inverses = pl.pallas_call(
        partial(gate_up_kernel, width=width, block=block),
        in_specs=[vmem_spec] * 3 + [any_spec] * 3,
        out_specs=[any_spec] * 3 + [vmem_spec],
        out_shape=[shape((rows, hidden), f32)] * 3 + [vmem_out((half, LANES), f32)],
        scratch_shapes=[
            pltpu.VMEM((rows, model), bf16),
            pltpu.VMEM((rows, peers * early), bf16),
            pltpu.VMEM((hidden, model), bf16),
            pltpu.VMEM((hidden, model), bf16),
            pltpu.VMEM((hidden, peers * early), bf16),
            acts,
            acts,
            acts,
            pltpu.SemaphoreType.DMA((2 * blocks + peers,)),
            pltpu.SemaphoreType.DMA((3 * blocks,)),
        ],
        compiler_params=params(),
        cost_estimate=cost(5 * product // 2, 4 * model * hidden),
        name="gate_up",
    )(own_x, other_x, in_vmem(gain), gate_weight, up_weight, down_weight)
    out_own, out_other = pl.pallas_call(
        partial(back_kernel, width=width, block=block),
        in_specs=[vmem_spec] * 2 + [any_spec] * 6,
        out_specs=[vmem_spec] * 2,
        out_shape=[vmem_out((half, model), bf16)] * 2,
        scratch_shapes=[
            pltpu.VMEM((rows, peers * (width - early)), bf16),
            acts,
            acts,
            acts,
            pltpu.VMEM((rows, hidden), bf16),
            pltpu.VMEM((rows, hidden), bf16),
            pltpu.VMEM((columns, hidden, column), bf16),
            pltpu.VMEM((columns, hidden, column), bf16),
            pltpu.VMEM((hidden, peers * (width - early)), bf16),
            pltpu.SemaphoreType.DMA((blocks * (peers + 3) + 2 * columns,)),
        ],
        compiler_params=params(),
        cost_estimate=cost(5 * product // 2, 6 * model * hidden),
        name="back",
    )(own_g, other_g, hidden_early, coef_gate, coef_up, gate_weight, up_weight, down_weight)

    swapped = lax.ppermute(out_other, "exp", partner)
    moved = pl.pallas_call(
        slot_kernel,
        out_shape=vmem_out((ctx, peers, slots, width), bf16),
        scratch_shapes=[pltpu.VMEM((half, model), f32)],
        compiler_params=params(),
        name="slot",
    )(in_vmem(out_own), in_vmem(swapped), in_vmem(gain), in_vmem(inverses), own_x)
    moved = lax.all_to_all(
        moved.reshape(ctx * peers, slots, width), ("ctx", "exp"), split_axis=0, concat_axis=0, tiled=True
    ).reshape(ctx, experts * capacity, width)

    upstream, resid_grad, state = pl.pallas_call(
        upstream_kernel,
        out_shape=(
            vmem_out((tokens, width), f32),
            vmem_out((tokens, width), bf16),
            vmem_out((N + 8, width), bf16),
        ),
        compiler_params=params(),
        name="upstream",
    )(*map(in_vmem, (moved, shares, grad_output, state_output, head_l, total_l)))

    def from_later(window, k):
        return in_vmem(lax.ppermute(window, "ctx", [(i, i - k) for i in range(k, ctx)]))

    spans = [1 << b for b in range((ctx - 1).bit_length()) if (ctx - 1) >> b & 1]
    window, length, windows = state, 1, {}
    while spans and length <= spans[-1]:
        offset = 1 + sum(span for span in spans if span > length)
        again = 2 * length <= spans[-1]
        near = from_later(window, length) if again else None
        if length in spans:
            far_window = near if again and offset == length else from_later(window, offset)
            windows[offset] = far_window
        if again:
            window = pl.pallas_call(
                join_kernel,
                out_shape=vmem_out((N + 8, width), bf16),
                compiler_params=params(),
                name="join",
            )(in_vmem(window), near)
        length *= 2
    states = [windows[offset] for offset in sorted(windows)]
    base, local_b = pl.pallas_call(
        mixer_local_kernel,
        out_shape=(vmem_out((tokens, width), f32), vmem_out((tokens, groups * N), f32)),
        compiler_params=params(),
        cost_estimate=cost(3 * 10**9, 2 * 10**6),
        name="mixer_local",
    )(*map(in_vmem, (upstream, resid_grad, mixer_input, state_output, mix, weigh, step_l, skip_l)))
    mixer_grad, state_input_grad = pl.pallas_call(
        mixer_far_kernel,
        out_shape=(shape((tokens, width), bf16), shape((tokens, groups * N), f32)),
        compiler_params=params(),
        name="mixer_far",
    )(*map(in_vmem, (*states, base, local_b, mixer_input, state_input, tail_l)))
    return (resid_grad, mixer_grad, state_input_grad)


def solution(mesh):
    in_specs = (
        P(("ctx", "exp"), None),
        P(),
        P(("ctx", "exp"), None),
        P(("ctx", "exp"), None),
        P("exp", "ctx", None),
        P("exp", "ctx", None),
        P("exp", "ctx", None),
        P("ctx", "exp"),
        P("ctx", "exp"),
        P("ctx", "exp"),
        P("ctx", "exp"),
        P("ctx", "exp"),
        P("ctx", "exp"),
        P("exp"),
    )
    out_specs = (P("ctx", "exp"), P("ctx", "exp"), P("ctx", "exp"))
    return jax.shard_map(body, mesh=mesh, in_specs=in_specs, out_specs=out_specs, check_vma=False)
```

```python
import math
from functools import partial

import jax
import jax.numpy as jnp
from jax import lax
from jax.experimental import pallas as pl
from jax.experimental.pallas import tpu as pltpu
from jax.sharding import PartitionSpec as P


N = 128
LANES = 128
norm_epsilon = 1e-05
f32 = jnp.float32
bf16 = jnp.bfloat16
highest = lax.Precision.HIGHEST
vmem_bytes = 56 * 1024 * 1024
resident_bytes = 2 * 1024 * 1024


def params(steps=0, limit=vmem_bytes):
    return pltpu.CompilerParams(dimension_semantics=("arbitrary",) * steps, vmem_limit_bytes=limit)


def iota(shape, dim):
    return lax.broadcasted_iota(jnp.int32, shape, dim)


def dot(a, b, ca, cb, precision=None):
    return lax.dot_general(
        a, b, (((ca,), (cb,)), ((), ())), precision=precision, preferred_element_type=f32
    )


def pack_kernel(resid, gain, ids_t, probs_t, grad, out, grad_early):
    grad_early[...] = grad[:, : grad_early.shape[1]]
    peers, rows = out.shape[0], out.shape[1]
    width = out.shape[2] - LANES
    eye = jnp.where(iota((rows, rows), 0) == iota((rows, rows), 1), 1.0, 0.0).astype(bf16)
    ids = dot(eye, ids_t[...].astype(f32).astype(bf16), 1, 1)
    probs = dot(eye, probs_t[...], 1, 1)
    lane = iota((rows, LANES), 1)
    meta = jnp.where(lane == 0, ids[:, 0:1], 0.0) + jnp.where(lane == 1, ids[:, 1:2], 0.0)
    meta = meta + jnp.where(lane == 2, probs[:, 0:1], 0.0) + jnp.where(lane == 3, probs[:, 1:2], 0.0)
    total = jnp.zeros((rows, 1), f32)
    for j in range(peers):
        x = resid[:, j * width : (j + 1) * width].astype(f32)
        total = total + jnp.sum(x * x, axis=1, keepdims=True)
    inverse = lax.rsqrt(total * (1.0 / (peers * width)) + norm_epsilon)
    high = inverse.astype(bf16).astype(f32)
    meta = meta + jnp.where(lane == 4, high, 0.0) + jnp.where(lane == 5, inverse - high, 0.0)
    meta = meta.astype(bf16)
    for j in range(peers):
        cols = slice(j * width, (j + 1) * width)
        out[j, :, :width] = (resid[:, cols].astype(f32) * inverse * gain[:, cols]).astype(bf16)
        out[j, :, width:] = meta


def dispatch_kernel(packed, grad, table, shares, inverses, rows, *, experts, capacity):
    tokens = packed.shape[0]
    width = packed.shape[1] - LANES
    meta = packed[:, width:].astype(f32)
    lane = iota((tokens, LANES), 1).astype(f32)
    first = meta[:, 0:1] == lane
    second = meta[:, 1:2] == lane
    member = jnp.where(first | second, 1.0, 0.0).astype(bf16)
    weight = (jnp.where(first, meta[:, 2:3], 0.0) + jnp.where(second, meta[:, 3:4], 0.0)).astype(bf16)
    row = iota((tokens, tokens), 0)
    col = iota((tokens, tokens), 1)
    before = jnp.where(row < col, 1.0, 0.0).astype(bf16)
    same = jnp.where(row == col, 1.0, 0.0).astype(bf16)
    position = dot(member, before, 0, 0)
    member_t = dot(member, same, 0, 0)
    weight_t = dot(weight, same, 0, 0)
    inverses[...] = jnp.broadcast_to(meta[:, 4:5] + meta[:, 5:6], (tokens, LANES))
    slot = iota((capacity, tokens), 0).astype(f32)
    for e in range(experts):
        hit = (slot == position[e : e + 1, :]) & (member_t[e : e + 1, :] > 0.5)
        entry = jnp.where(hit, 1.0, 0.0)
        table[e * capacity : (e + 1) * capacity, :] = entry.astype(bf16)
        shares[e * capacity : (e + 1) * capacity, :] = (entry * weight_t[e : e + 1, :]).astype(bf16)
    out_x = dot(table[...], packed[:, :width], 1, 0).astype(bf16)
    out_g = dot(table[...], grad[...], 1, 0).astype(bf16)
    for c in range(rows.shape[0]):
        rows[c, :, :width] = out_x
        rows[c, :, width:] = out_g


def select_kernel(table, grad, rows):
    late = rows.shape[2]
    out_g = dot(table[...], grad[:, grad.shape[1] - late :], 1, 0).astype(bf16)
    for c in range(rows.shape[0]):
        rows[c] = out_g


def gather_rows(ref, first, start, stop, out):
    ctx, peers, slots = ref.shape[:3]
    for j in range(peers):
        at = slice(j * (stop - start), (j + 1) * (stop - start))
        out[first : first + ctx * slots, at] = ref[:, j, :, start:stop].reshape(ctx * slots, stop - start)


def packed_copies(hbm, rows, width, start, stop, out, sems, base):
    size = stop - start
    return [
        pltpu.make_async_copy(
            hbm.at[0, rows, j * width + start : j * width + stop],
            out.at[rows, j * size : (j + 1) * size],
            sems.at[base + j],
        )
        for j in range(out.shape[1] // size)
    ]


def launch(copies):
    for copy in copies:
        copy.start()
    return copies


def finish(copies):
    for copy in copies:
        copy.wait()


def gate_up_kernel(
    own, other_hbm, gate_hbm, up_hbm, down_hbm, coef_gate_hbm, coef_up_hbm, hidden_hbm,
    other, normed, grads, gate_w, up_w, down_w, coef_gate, coef_up, hidden_early, in_sems, out_sems, *, width, block,
):
    ctx, peers, slots, both = own.shape
    half = ctx * slots
    blocks = gate_w.shape[0] // block
    parts = [slice(i * block, (i + 1) * block) for i in range(blocks)]
    swap = launch([pltpu.make_async_copy(other_hbm, other, in_sems.at[2 * blocks + peers])])
    pairs = [
        launch(
            [
                pltpu.make_async_copy(gate_hbm.at[0, part, :], gate_w.at[part, :], in_sems.at[2 * i]),
                pltpu.make_async_copy(up_hbm.at[0, part, :], up_w.at[part, :], in_sems.at[2 * i + 1]),
            ]
        )
        for i, part in enumerate(parts)
    ]
    downs = launch(
        packed_copies(down_hbm, slice(0, gate_w.shape[0]), width, 0, both - width, down_w, in_sems, 2 * blocks)
    )
    gather_rows(own, 0, 0, width, normed)
    gather_rows(own, 0, width, both, grads)
    finish(swap)
    gather_rows(other, half, 0, width, normed)
    gather_rows(other, half, width, both, grads)
    outs = []
    for i, part in enumerate(parts):
        finish(pairs[i])
        gate = dot(normed[...], gate_w[part, :], 1, 1)
        up = dot(normed[...], up_w[part, :], 1, 1)
        sig = jax.nn.sigmoid(gate)
        coef_gate[:, part] = up * sig * (1.0 + gate * (1.0 - sig))
        coef_up[:, part] = gate * sig
        outs += launch(
            [
                pltpu.make_async_copy(coef_gate.at[:, part], coef_gate_hbm.at[:, part], out_sems.at[3 * i]),
                pltpu.make_async_copy(coef_up.at[:, part], coef_up_hbm.at[:, part], out_sems.at[3 * i + 1]),
            ]
        )
    finish(downs)
    for i, part in enumerate(parts):
        hidden_early[:, part] = dot(grads[...], down_w[part, :], 1, 1)
        outs += launch(
            [pltpu.make_async_copy(hidden_early.at[:, part], hidden_hbm.at[:, part], out_sems.at[3 * i + 2])]
        )
    finish(outs)


def back_kernel(
    own, other, hidden_hbm, coef_gate_hbm, coef_up_hbm, gate_hbm, up_hbm, down_hbm, out_own, out_other,
    grads, hidden_early, coef_gate, coef_up, gate_grad, up_grad, gate_w, up_w, down_w, sems, *, width, block,
):
    ctx, peers, slots, late = own.shape
    half = ctx * slots
    columns, hidden, column = gate_w.shape
    blocks = hidden // block
    parts = [slice(i * block, (i + 1) * block) for i in range(blocks)]
    used = 0

    def copy(source, target):
        nonlocal used
        used += 1
        return pltpu.make_async_copy(source, target, sems.at[used - 1])

    waits = []
    for part in parts:
        downs = launch(packed_copies(down_hbm, part, width, width - late, width, down_w, sems, used))
        used += peers
        acts = [
            copy(hidden_hbm.at[:, part], hidden_early.at[:, part]),
            copy(coef_gate_hbm.at[:, part], coef_gate.at[:, part]),
            copy(coef_up_hbm.at[:, part], coef_up.at[:, part]),
        ]
        waits.append((downs, launch(acts)))
    slabs = [slice(i * column, (i + 1) * column) for i in range(columns)]
    pairs = [
        launch([copy(gate_hbm.at[0, :, cols], gate_w.at[i]), copy(up_hbm.at[0, :, cols], up_w.at[i])])
        for i, cols in enumerate(slabs)
    ]
    gather_rows(own, 0, 0, late, grads)
    gather_rows(other, half, 0, late, grads)
    for i, part in enumerate(parts):
        downs, acts = waits[i]
        finish(downs)
        late_part = dot(grads[...], down_w[part, :], 1, 1)
        finish(acts)
        grad = hidden_early[:, part] + late_part
        gate_grad[:, part] = (grad * coef_gate[:, part]).astype(bf16)
        up_grad[:, part] = (grad * coef_up[:, part]).astype(bf16)
    for i, cols in enumerate(slabs):
        finish(pairs[i])
        out = (dot(gate_grad[...], gate_w[i], 1, 0) + dot(up_grad[...], up_w[i], 1, 0)).astype(bf16)
        out_own[:, cols] = out[:half]
        out_other[:, cols] = out[half:]


def slot_kernel(own, swapped, gain, rows, out, sums):
    ctx, peers, slots, width = out.shape
    half = ctx * slots
    model = peers * width
    product = jnp.zeros((half, 1), f32)
    for j in range(peers):
        cols = slice(j * width, (j + 1) * width)
        total = own[:, cols].astype(f32) + swapped[:, cols].astype(f32)
        sums[:, cols] = total
        normed = rows[:, j, :, :width].reshape(half, width).astype(f32)
        product = product + jnp.sum(total * normed, axis=1, keepdims=True)
    shift = product * (1.0 / model)
    for j in range(peers):
        cols = slice(j * width, (j + 1) * width)
        scaled = rows[:, j, :, :width].reshape(half, width).astype(f32) * (1.0 / gain[:, cols])
        out[:, j] = (sums[:, cols] * gain[:, cols] - scaled * shift).astype(bf16).reshape(ctx, slots, width)


def mixer_setup_kernel(
    log_t, step_t, skip, state_in, state_out, mix, weigh, step_l, tail_l, head_l, skip_l, total_l, *, groups
):
    heads, tokens = log_t.shape
    width = step_l.shape[1]
    size = width // heads
    row = iota((tokens, tokens), 0)
    col = iota((tokens, tokens), 1)
    upto = jnp.where(row <= col, 1.0, 0.0)
    eye = jnp.where(row == col, 1.0, 0.0)
    cum_t = dot(log_t[...], upto, 1, 0, highest)
    cum = dot(upto, log_t[...], 0, 1, highest)
    steps = dot(eye, step_t[...], 1, 1, highest)
    last = cum[tokens - 1 : tokens, :]
    spread = jnp.where(iota((heads, width), 0) == iota((heads, width), 1) // size, 1.0, 0.0)
    step_l[...] = dot(steps, spread, 1, 0, highest)
    tail_l[...] = dot(steps * jnp.exp(last - cum), spread, 1, 0, highest)
    head_l[...] = dot(jnp.exp(cum), spread, 1, 0, highest)
    skip_l[...] = dot(jnp.broadcast_to(skip[...], (8, heads)), spread, 1, 0, highest)
    total_l[...] = dot(jnp.broadcast_to(jnp.exp(last), (8, heads)), spread, 1, 0, highest)
    later = col >= row
    for g in range(groups):
        cols = slice(g * N, (g + 1) * N)
        inter = dot(state_in[:, cols], state_out[:, cols], 1, 1)
        for h in range(g * heads // groups, (g + 1) * heads // groups):
            gap = cum_t[h : h + 1, :] - cum[:, h : h + 1]
            decay = jnp.where(later, jnp.exp(jnp.where(later, gap, 0.0)), 0.0)
            mix[h] = (decay * inter).astype(bf16)
            weigh[h] = decay * steps[:, h : h + 1]


def upstream_kernel(moved, shares, inverses, grad, state_out, head_l, total_l, upstream, resid_grad, state):
    width = grad.shape[1]
    groups = state_out.shape[1] // N
    span = width // groups
    moe = dot(shares[...], moved[0], 0, 0)
    for c in range(1, moved.shape[0]):
        moe = moe + dot(shares[...], moved[c], 0, 0)
    moe = (moe * inverses[:, 0:1]).astype(bf16)
    up = grad[...].astype(f32) + moe.astype(f32)
    upstream[...] = up
    resid_grad[...] = up.astype(bf16)
    for g in range(groups):
        cols = slice(g * N, (g + 1) * N)
        wide = slice(g * span, (g + 1) * span)
        scaled = (up[:, wide] * head_l[:, wide]).astype(bf16)
        state[0:N, wide] = dot(state_out[:, cols], scaled, 0, 0).astype(bf16)
    total = total_l[...]
    high = total.astype(bf16).astype(f32)
    state[N : N + 8, :] = jnp.where(iota(total.shape, 0) == 0, high, total - high).astype(bf16)


def mixer_local_kernel(upstream, resid_grad, mixer, state_out, mix, weigh, step_l, skip_l, base, local_b):
    tokens, width = upstream.shape
    heads = mix.shape[0]
    size = width // heads
    groups = state_out.shape[1] // N
    for g in range(groups):
        cols = slice(g * N, (g + 1) * N)
        weighted = jnp.zeros((tokens, tokens), f32)
        for h in range(g * heads // groups, (g + 1) * heads // groups):
            part = slice(h * size, (h + 1) * size)
            up_h = resid_grad[:, part]
            mixed = dot(mix[h], up_h, 1, 0)
            base[:, part] = step_l[:, part] * mixed + skip_l[0:1, part] * upstream[:, part]
            weighted = weighted + weigh[h] * dot(mixer[:, part], up_h, 1, 1)
        local_b[:, cols] = dot(weighted.astype(bf16), state_out[:, cols], 1, 0)


def join_kernel(first, later, out):
    decay = first[N : N + 1, :].astype(f32) + first[N + 1 : N + 2, :].astype(f32)
    out[0:N, :] = (first[0:N, :].astype(f32) + decay * later[0:N, :].astype(f32)).astype(bf16)
    total = decay * (later[N : N + 1, :].astype(f32) + later[N + 1 : N + 2, :].astype(f32))
    total = jnp.broadcast_to(total, (8, total.shape[1]))
    high = total.astype(bf16).astype(f32)
    out[N : N + 8, :] = jnp.where(iota(total.shape, 0) == 0, high, total - high).astype(bf16)


def mixer_far_kernel(*refs):
    base, local_b, mixer, state_in, tail_l, mixer_grad, input_grad = refs[-7:]
    states = refs[:-7]
    groups = state_in.shape[1] // N
    width = base.shape[1]
    span = width // groups
    incoming = states[-1][0:N, :].astype(f32)
    for ref in states[-2::-1]:
        decay = ref[N : N + 1, :].astype(f32) + ref[N + 1 : N + 2, :].astype(f32)
        incoming = ref[0:N, :].astype(f32) + decay * incoming
    incoming = incoming.astype(bf16)
    for g in range(groups):
        cols = slice(g * N, (g + 1) * N)
        wide = slice(g * span, (g + 1) * span)
        far = dot(state_in[:, cols], incoming[:, wide], 1, 0)
        mixer_grad[:, wide] = (base[:, wide] + tail_l[:, wide] * far).astype(bf16)
        scaled = (mixer[:, wide].astype(f32) * tail_l[:, wide]).astype(bf16)
        input_grad[:, cols] = local_b[:, cols] + dot(scaled, incoming[:, wide], 1, 1)


def block_of(total, most):
    size = min(total, most)
    while total % size:
        size -= LANES if size > LANES else 1
    return size


def small(dims, dtype):
    return math.prod(dims) * jnp.dtype(dtype).itemsize <= resident_bytes


def in_vmem(x):
    return pltpu.with_memory_space_constraint(x, pltpu.VMEM) if small(x.shape, x.dtype) else x


def vmem_out(dims, dtype):
    return pltpu.VMEM(dims, dtype) if small(dims, dtype) else jax.ShapeDtypeStruct(dims, dtype)


def cost(flops, moved):
    return pl.CostEstimate(flops=flops, transcendentals=0, bytes_accessed=moved)


def body(
    resid_input,
    norm_gain,
    expert_ids,
    route_probs,
    gate_weight,
    up_weight,
    down_weight,
    grad_output,
    mixer_input,
    state_input,
    state_output,
    step_size,
    log_retention,
    skip_gain,
):
    ctx = lax.axis_size("ctx")
    peers = lax.axis_size("exp")
    experts = peers // 2
    token_rows, model = resid_input.shape
    tokens, width = grad_output.shape
    capacity = 2 * tokens // experts
    slots = capacity // 2
    heads = skip_gain.shape[0]
    groups = state_input.shape[1] // N
    hidden = gate_weight.shape[1]
    early = width // 2
    gain = norm_gain.reshape(1, model)
    partner = [(i, i ^ 1) for i in range(peers)]
    shape = jax.ShapeDtypeStruct

    packed, grad_early = pl.pallas_call(
        pack_kernel,
        out_shape=(
            vmem_out((peers, token_rows, width + LANES), bf16),
            vmem_out((tokens, early), bf16),
        ),
        compiler_params=params(),
        name="pack",
    )(resid_input, gain, expert_ids.T, route_probs.T, grad_output)
    packed = lax.all_to_all(packed, "exp", split_axis=0, concat_axis=0, tiled=True)

    mix, weigh, step_l, tail_l, head_l, skip_l, total_l = pl.pallas_call(
        partial(mixer_setup_kernel, groups=groups),
        out_shape=(
            shape((heads, tokens, tokens), bf16),
            shape((heads, tokens, tokens), f32),
            shape((tokens, width), f32),
            shape((tokens, width), f32),
            shape((tokens, width), f32),
            shape((8, width), f32),
            shape((8, width), f32),
        ),
        compiler_params=params(),
        cost_estimate=cost(2 * 10**9, 2 * 10**6),
        name="mixer_setup",
    )(log_retention.T, step_size.T, skip_gain.reshape(1, heads), state_input, state_output)

    table, shares, inverses, rows_early = pl.pallas_call(
        partial(dispatch_kernel, experts=experts, capacity=capacity),
        out_shape=(
            vmem_out((experts * capacity, tokens), bf16),
            vmem_out((experts * capacity, tokens), bf16),
            vmem_out((tokens, LANES), f32),
            vmem_out((ctx, experts * capacity, width + early), bf16),
        ),
        compiler_params=params(),
        name="dispatch",
    )(in_vmem(packed.reshape(tokens, width + LANES)), in_vmem(grad_early))
    rows_late = pl.pallas_call(
        select_kernel,
        out_shape=vmem_out((ctx, experts * capacity, width - early), bf16),
        compiler_params=params(),
        cost_estimate=cost(10**9, 2 * 10**6),
        name="select",
    )(in_vmem(table), grad_output)

    def spread(rows):
        got = lax.all_to_all(
            rows.reshape(ctx * peers, slots, -1), ("ctx", "exp"), split_axis=0, concat_axis=0, tiled=True
        ).reshape(ctx, peers, slots, -1)
        return in_vmem(got), lax.ppermute(got, "exp", partner)

    own_x, other_x = spread(rows_early)
    own_g, other_g = spread(rows_late)
    rows = 2 * ctx * slots
    half = rows // 2
    block = block_of(hidden, 512)
    blocks = hidden // block
    column = block_of(model, 512)
    columns = model // column
    product = 2 * rows * model * hidden
    any_spec = pl.BlockSpec(memory_space=pl.ANY)
    vmem_spec = pl.BlockSpec(memory_space=pltpu.VMEM)
    acts = pltpu.VMEM((rows, hidden), f32)
    coef_gate, coef_up, hidden_early = pl.pallas_call(
        partial(gate_up_kernel, width=width, block=block),
        in_specs=[vmem_spec] + [any_spec] * 4,
        out_specs=[any_spec] * 3,
        out_shape=[shape((rows, hidden), f32)] * 3,
        scratch_shapes=[
            pltpu.VMEM((ctx, peers, slots, width + early), bf16),
            pltpu.VMEM((rows, model), bf16),
            pltpu.VMEM((rows, peers * early), bf16),
            pltpu.VMEM((hidden, model), bf16),
            pltpu.VMEM((hidden, model), bf16),
            pltpu.VMEM((hidden, peers * early), bf16),
            acts,
            acts,
            acts,
            pltpu.SemaphoreType.DMA((2 * blocks + peers + 1,)),
            pltpu.SemaphoreType.DMA((3 * blocks,)),
        ],
        compiler_params=params(),
        cost_estimate=cost(5 * product // 2, 4 * model * hidden),
        name="gate_up",
    )(own_x, other_x, gate_weight, up_weight, down_weight)
    out_own, out_other = pl.pallas_call(
        partial(back_kernel, width=width, block=block),
        in_specs=[vmem_spec] * 2 + [any_spec] * 6,
        out_specs=[vmem_spec] * 2,
        out_shape=[vmem_out((half, model), bf16)] * 2,
        scratch_shapes=[
            pltpu.VMEM((rows, peers * (width - early)), bf16),
            acts,
            acts,
            acts,
            pltpu.VMEM((rows, hidden), bf16),
            pltpu.VMEM((rows, hidden), bf16),
            pltpu.VMEM((columns, hidden, column), bf16),
            pltpu.VMEM((columns, hidden, column), bf16),
            pltpu.VMEM((hidden, peers * (width - early)), bf16),
            pltpu.SemaphoreType.DMA((blocks * (peers + 3) + 2 * columns,)),
        ],
        compiler_params=params(),
        cost_estimate=cost(5 * product // 2, 6 * model * hidden),
        name="back",
    )(own_g, in_vmem(other_g), hidden_early, coef_gate, coef_up, gate_weight, up_weight, down_weight)

    swapped = lax.ppermute(out_other, "exp", partner)
    moved = pl.pallas_call(
        slot_kernel,
        out_shape=vmem_out((ctx, peers, slots, width), bf16),
        scratch_shapes=[pltpu.VMEM((half, model), f32)],
        compiler_params=params(),
        name="slot",
    )(in_vmem(out_own), in_vmem(swapped), in_vmem(gain), own_x)
    moved = lax.all_to_all(
        moved.reshape(ctx * peers, slots, width), ("ctx", "exp"), split_axis=0, concat_axis=0, tiled=True
    ).reshape(ctx, experts * capacity, width)

    upstream, resid_grad, state = pl.pallas_call(
        upstream_kernel,
        out_shape=(
            vmem_out((tokens, width), f32),
            vmem_out((tokens, width), bf16),
            vmem_out((N + 8, width), bf16),
        ),
        compiler_params=params(),
        name="upstream",
    )(*map(in_vmem, (moved, shares, inverses, grad_output, state_output, head_l, total_l)))

    def from_later(window, k):
        return in_vmem(lax.ppermute(window, "ctx", [(i, i - k) for i in range(k, ctx)]))

    spans = [1 << b for b in range((ctx - 1).bit_length()) if (ctx - 1) >> b & 1]
    window, length, windows = state, 1, {}
    while spans and length <= spans[-1]:
        offset = 1 + sum(span for span in spans if span > length)
        again = 2 * length <= spans[-1]
        near = from_later(window, length) if again else None
        if length in spans:
            far_window = near if again and offset == length else from_later(window, offset)
            windows[offset] = far_window
        if again:
            window = pl.pallas_call(
                join_kernel,
                out_shape=vmem_out((N + 8, width), bf16),
                compiler_params=params(),
                name="join",
            )(in_vmem(window), near)
        length *= 2
    states = [windows[offset] for offset in sorted(windows)]
    base, local_b = pl.pallas_call(
        mixer_local_kernel,
        out_shape=(vmem_out((tokens, width), f32), vmem_out((tokens, groups * N), f32)),
        compiler_params=params(),
        cost_estimate=cost(3 * 10**9, 2 * 10**6),
        name="mixer_local",
    )(*map(in_vmem, (upstream, resid_grad, mixer_input, state_output, mix, weigh, step_l, skip_l)))
    mixer_grad, state_input_grad = pl.pallas_call(
        mixer_far_kernel,
        out_shape=(shape((tokens, width), bf16), shape((tokens, groups * N), f32)),
        compiler_params=params(),
        name="mixer_far",
    )(*map(in_vmem, (*states, base, local_b, mixer_input, state_input, tail_l)))
    return (resid_grad, mixer_grad, state_input_grad)


def solution(mesh):
    in_specs = (
        P(("ctx", "exp"), None),
        P(),
        P(("ctx", "exp"), None),
        P(("ctx", "exp"), None),
        P("exp", "ctx", None),
        P("exp", "ctx", None),
        P("exp", "ctx", None),
        P("ctx", "exp"),
        P("ctx", "exp"),
        P("ctx", "exp"),
        P("ctx", "exp"),
        P("ctx", "exp"),
        P("ctx", "exp"),
        P("exp"),
    )
    out_specs = (P("ctx", "exp"), P("ctx", "exp"), P("ctx", "exp"))
    return jax.shard_map(body, mesh=mesh, in_specs=in_specs, out_specs=out_specs, check_vma=False)
```

```python
import math
from functools import partial

import jax
import jax.numpy as jnp
from jax import lax
from jax.experimental import pallas as pl
from jax.experimental.pallas import tpu as pltpu
from jax.sharding import PartitionSpec as P


N = 128
LANES = 128
norm_epsilon = 1e-05
f32 = jnp.float32
bf16 = jnp.bfloat16
highest = lax.Precision.HIGHEST
vmem_bytes = 56 * 1024 * 1024
resident_bytes = 2 * 1024 * 1024


def params(steps=0, limit=vmem_bytes):
    return pltpu.CompilerParams(dimension_semantics=("arbitrary",) * steps, vmem_limit_bytes=limit)


def iota(shape, dim):
    return lax.broadcasted_iota(jnp.int32, shape, dim)


def dot(a, b, ca, cb, precision=None):
    return lax.dot_general(
        a, b, (((ca,), (cb,)), ((), ())), precision=precision, preferred_element_type=f32
    )


def pack_kernel(resid, gain, ids_t, probs_t, grad, out, grad_early):
    grad_early[...] = grad[:, : grad_early.shape[1]]
    peers, rows = out.shape[0], out.shape[1]
    width = out.shape[2] - LANES
    eye = jnp.where(iota((rows, rows), 0) == iota((rows, rows), 1), 1.0, 0.0).astype(bf16)
    ids = dot(eye, ids_t[...].astype(f32).astype(bf16), 1, 1)
    probs = dot(eye, probs_t[...], 1, 1)
    lane = iota((rows, LANES), 1)
    meta = jnp.where(lane == 0, ids[:, 0:1], 0.0) + jnp.where(lane == 1, ids[:, 1:2], 0.0)
    meta = meta + jnp.where(lane == 2, probs[:, 0:1], 0.0) + jnp.where(lane == 3, probs[:, 1:2], 0.0)
    total = jnp.zeros((rows, 1), f32)
    for j in range(peers):
        x = resid[:, j * width : (j + 1) * width].astype(f32)
        total = total + jnp.sum(x * x, axis=1, keepdims=True)
    inverse = lax.rsqrt(total * (1.0 / (peers * width)) + norm_epsilon)
    high = inverse.astype(bf16).astype(f32)
    meta = meta + jnp.where(lane == 4, high, 0.0) + jnp.where(lane == 5, inverse - high, 0.0)
    meta = meta.astype(bf16)
    for j in range(peers):
        cols = slice(j * width, (j + 1) * width)
        out[j, :, :width] = (resid[:, cols].astype(f32) * inverse * gain[:, cols]).astype(bf16)
        out[j, :, width:] = meta


def dispatch_kernel(packed, grad, table, rows, *, experts, capacity):
    tokens = packed.shape[0]
    width = packed.shape[1] - LANES
    meta = packed[:, width:].astype(f32)
    lane = iota((tokens, LANES), 1).astype(f32)
    member = jnp.where((meta[:, 0:1] == lane) | (meta[:, 1:2] == lane), 1.0, 0.0).astype(bf16)
    row = iota((tokens, tokens), 0)
    col = iota((tokens, tokens), 1)
    position = dot(member, jnp.where(row < col, 1.0, 0.0).astype(bf16), 0, 0)
    member_t = dot(member, jnp.where(row == col, 1.0, 0.0).astype(bf16), 0, 0)
    position = jnp.where(member_t > 0.5, position, -1.0)
    slot = iota((capacity, tokens), 0).astype(f32)
    for e in range(experts):
        hit = slot == position[e : e + 1, :]
        table[e * capacity : (e + 1) * capacity, :] = jnp.where(hit, 1.0, 0.0).astype(bf16)
    out_x = dot(table[...], packed[:, :width], 1, 0).astype(bf16)
    out_g = dot(table[...], grad[...], 1, 0).astype(bf16)
    for c in range(rows.shape[0]):
        rows[c, :, :width] = out_x
        rows[c, :, width:] = out_g


def select_kernel(packed, table, grad, shares, inverses, rows, *, experts, capacity):
    tokens = packed.shape[0]
    meta = packed[:, packed.shape[1] - LANES :].astype(f32)
    late = rows.shape[2]
    out_g = dot(table[...], grad[:, grad.shape[1] - late :], 1, 0).astype(bf16)
    for c in range(rows.shape[0]):
        rows[c] = out_g
    inverses[...] = jnp.broadcast_to(meta[:, 4:5] + meta[:, 5:6], (tokens, LANES))
    lane = iota((tokens, LANES), 1).astype(f32)
    weight = jnp.where(meta[:, 0:1] == lane, meta[:, 2:3], 0.0) + jnp.where(meta[:, 1:2] == lane, meta[:, 3:4], 0.0)
    same = jnp.where(iota((tokens, tokens), 0) == iota((tokens, tokens), 1), 1.0, 0.0).astype(bf16)
    weight_t = dot(weight.astype(bf16), same, 0, 0)
    for e in range(experts):
        at = slice(e * capacity, (e + 1) * capacity)
        shares[at, :] = (table[at, :].astype(f32) * weight_t[e : e + 1, :]).astype(bf16)


def gather_rows(ref, first, start, stop, out):
    ctx, peers, slots = ref.shape[:3]
    for j in range(peers):
        at = slice(j * (stop - start), (j + 1) * (stop - start))
        out[first : first + ctx * slots, at] = ref[:, j, :, start:stop].reshape(ctx * slots, stop - start)


def packed_copies(hbm, rows, width, start, stop, out, sems, base):
    size = stop - start
    return [
        pltpu.make_async_copy(
            hbm.at[0, rows, j * width + start : j * width + stop],
            out.at[rows, j * size : (j + 1) * size],
            sems.at[base + j],
        )
        for j in range(out.shape[1] // size)
    ]


def launch(copies):
    for copy in copies:
        copy.start()
    return copies


def finish(copies):
    for copy in copies:
        copy.wait()


def gate_up_kernel(
    own, other_hbm, gate_hbm, up_hbm, down_hbm, coef_gate_hbm, coef_up_hbm, hidden_hbm,
    other, normed, grads, gate_w, up_w, down_w, coef_gate, coef_up, hidden_early, in_sems, out_sems, *, width, block,
):
    ctx, peers, slots, both = own.shape
    half = ctx * slots
    blocks = gate_w.shape[0] // block
    parts = [slice(i * block, (i + 1) * block) for i in range(blocks)]
    swap = launch([pltpu.make_async_copy(other_hbm, other, in_sems.at[2 * blocks + peers])])
    pairs = [
        launch(
            [
                pltpu.make_async_copy(gate_hbm.at[0, part, :], gate_w.at[part, :], in_sems.at[2 * i]),
                pltpu.make_async_copy(up_hbm.at[0, part, :], up_w.at[part, :], in_sems.at[2 * i + 1]),
            ]
        )
        for i, part in enumerate(parts)
    ]
    downs = launch(
        packed_copies(down_hbm, slice(0, gate_w.shape[0]), width, 0, both - width, down_w, in_sems, 2 * blocks)
    )
    gather_rows(own, 0, 0, width, normed)
    gather_rows(own, 0, width, both, grads)
    finish(swap)
    gather_rows(other, half, 0, width, normed)
    gather_rows(other, half, width, both, grads)
    outs = []
    for i, part in enumerate(parts):
        finish(pairs[i])
        gate = dot(normed[...], gate_w[part, :], 1, 1)
        up = dot(normed[...], up_w[part, :], 1, 1)
        sig = jax.nn.sigmoid(gate)
        coef_gate[:, part] = up * sig * (1.0 + gate * (1.0 - sig))
        coef_up[:, part] = gate * sig
        outs += launch(
            [
                pltpu.make_async_copy(coef_gate.at[:, part], coef_gate_hbm.at[:, part], out_sems.at[3 * i]),
                pltpu.make_async_copy(coef_up.at[:, part], coef_up_hbm.at[:, part], out_sems.at[3 * i + 1]),
            ]
        )
    finish(downs)
    for i, part in enumerate(parts):
        hidden_early[:, part] = dot(grads[...], down_w[part, :], 1, 1)
        outs += launch(
            [pltpu.make_async_copy(hidden_early.at[:, part], hidden_hbm.at[:, part], out_sems.at[3 * i + 2])]
        )
    finish(outs)


def back_kernel(
    own, other, hidden_hbm, coef_gate_hbm, coef_up_hbm, gate_hbm, up_hbm, down_hbm, out_own, out_other,
    grads, hidden_early, coef_gate, coef_up, gate_grad, up_grad, gate_w, up_w, down_w, sems, *, width, block,
):
    ctx, peers, slots, late = own.shape
    half = ctx * slots
    columns, hidden, column = gate_w.shape
    blocks = hidden // block
    parts = [slice(i * block, (i + 1) * block) for i in range(blocks)]
    used = 0

    def copy(source, target):
        nonlocal used
        used += 1
        return pltpu.make_async_copy(source, target, sems.at[used - 1])

    waits = []
    for part in parts:
        downs = launch(packed_copies(down_hbm, part, width, width - late, width, down_w, sems, used))
        used += peers
        acts = [
            copy(hidden_hbm.at[:, part], hidden_early.at[:, part]),
            copy(coef_gate_hbm.at[:, part], coef_gate.at[:, part]),
            copy(coef_up_hbm.at[:, part], coef_up.at[:, part]),
        ]
        waits.append((downs, launch(acts)))
    slabs = [slice(i * column, (i + 1) * column) for i in range(columns)]
    pairs = [
        launch([copy(gate_hbm.at[0, :, cols], gate_w.at[i]), copy(up_hbm.at[0, :, cols], up_w.at[i])])
        for i, cols in enumerate(slabs)
    ]
    gather_rows(own, 0, 0, late, grads)
    gather_rows(other, half, 0, late, grads)
    for i, part in enumerate(parts):
        downs, acts = waits[i]
        finish(downs)
        late_part = dot(grads[...], down_w[part, :], 1, 1)
        finish(acts)
        grad = hidden_early[:, part] + late_part
        gate_grad[:, part] = (grad * coef_gate[:, part]).astype(bf16)
        up_grad[:, part] = (grad * coef_up[:, part]).astype(bf16)
    for i, cols in enumerate(slabs):
        finish(pairs[i])
        out = (dot(gate_grad[...], gate_w[i], 1, 0) + dot(up_grad[...], up_w[i], 1, 0)).astype(bf16)
        out_own[:, cols] = out[:half]
        out_other[:, cols] = out[half:]


def slot_kernel(own, swapped, gain, rows, out, sums):
    ctx, peers, slots, width = out.shape
    half = ctx * slots
    model = peers * width
    product = jnp.zeros((half, 1), f32)
    for j in range(peers):
        cols = slice(j * width, (j + 1) * width)
        total = own[:, cols].astype(f32) + swapped[:, cols].astype(f32)
        sums[:, cols] = total
        normed = rows[:, j, :, :width].reshape(half, width).astype(f32)
        product = product + jnp.sum(total * normed, axis=1, keepdims=True)
    shift = product * (1.0 / model)
    for j in range(peers):
        cols = slice(j * width, (j + 1) * width)
        scaled = rows[:, j, :, :width].reshape(half, width).astype(f32) * (1.0 / gain[:, cols])
        out[:, j] = (sums[:, cols] * gain[:, cols] - scaled * shift).astype(bf16).reshape(ctx, slots, width)


def mixer_setup_kernel(
    log_t, step_t, skip, state_in, state_out, mix, weigh, step_l, tail_l, head_l, skip_l, total_l, *, groups
):
    heads, tokens = log_t.shape
    width = step_l.shape[1]
    size = width // heads
    row = iota((tokens, tokens), 0)
    col = iota((tokens, tokens), 1)
    upto = jnp.where(row <= col, 1.0, 0.0)
    eye = jnp.where(row == col, 1.0, 0.0)
    cum_t = dot(log_t[...], upto, 1, 0, highest)
    cum = dot(upto, log_t[...], 0, 1, highest)
    steps = dot(eye, step_t[...], 1, 1, highest)
    last = cum[tokens - 1 : tokens, :]
    spread = jnp.where(iota((heads, width), 0) == iota((heads, width), 1) // size, 1.0, 0.0)
    step_l[...] = dot(steps, spread, 1, 0, highest)
    tail_l[...] = dot(steps * jnp.exp(last - cum), spread, 1, 0, highest)
    head_l[...] = dot(jnp.exp(cum), spread, 1, 0, highest)
    skip_l[...] = dot(jnp.broadcast_to(skip[...], (8, heads)), spread, 1, 0, highest)
    total_l[...] = dot(jnp.broadcast_to(jnp.exp(last), (8, heads)), spread, 1, 0, highest)
    later = col >= row
    for g in range(groups):
        cols = slice(g * N, (g + 1) * N)
        inter = dot(state_in[:, cols], state_out[:, cols], 1, 1)
        for h in range(g * heads // groups, (g + 1) * heads // groups):
            gap = cum_t[h : h + 1, :] - cum[:, h : h + 1]
            decay = jnp.where(later, jnp.exp(jnp.where(later, gap, 0.0)), 0.0)
            mix[h] = (decay * inter).astype(bf16)
            weigh[h] = decay * steps[:, h : h + 1]


def upstream_kernel(moved, shares, inverses, grad, state_out, head_l, total_l, upstream, resid_grad, state):
    width = grad.shape[1]
    groups = state_out.shape[1] // N
    span = width // groups
    moe = dot(shares[...], moved[0], 0, 0)
    for c in range(1, moved.shape[0]):
        moe = moe + dot(shares[...], moved[c], 0, 0)
    moe = (moe * inverses[:, 0:1]).astype(bf16)
    up = grad[...].astype(f32) + moe.astype(f32)
    upstream[...] = up
    resid_grad[...] = up.astype(bf16)
    for g in range(groups):
        cols = slice(g * N, (g + 1) * N)
        wide = slice(g * span, (g + 1) * span)
        scaled = (up[:, wide] * head_l[:, wide]).astype(bf16)
        state[0:N, wide] = dot(state_out[:, cols], scaled, 0, 0).astype(bf16)
    total = total_l[...]
    high = total.astype(bf16).astype(f32)
    state[N : N + 8, :] = jnp.where(iota(total.shape, 0) == 0, high, total - high).astype(bf16)


def mixer_local_kernel(upstream, resid_grad, mixer, state_out, mix, weigh, step_l, skip_l, base, local_b):
    tokens, width = upstream.shape
    heads = mix.shape[0]
    size = width // heads
    groups = state_out.shape[1] // N
    for g in range(groups):
        cols = slice(g * N, (g + 1) * N)
        weighted = jnp.zeros((tokens, tokens), f32)
        for h in range(g * heads // groups, (g + 1) * heads // groups):
            part = slice(h * size, (h + 1) * size)
            up_h = resid_grad[:, part]
            mixed = dot(mix[h], up_h, 1, 0)
            base[:, part] = step_l[:, part] * mixed + skip_l[0:1, part] * upstream[:, part]
            weighted = weighted + weigh[h] * dot(mixer[:, part], up_h, 1, 1)
        local_b[:, cols] = dot(weighted.astype(bf16), state_out[:, cols], 1, 0)


def join_kernel(first, later, out):
    decay = first[N : N + 1, :].astype(f32) + first[N + 1 : N + 2, :].astype(f32)
    out[0:N, :] = (first[0:N, :].astype(f32) + decay * later[0:N, :].astype(f32)).astype(bf16)
    total = decay * (later[N : N + 1, :].astype(f32) + later[N + 1 : N + 2, :].astype(f32))
    total = jnp.broadcast_to(total, (8, total.shape[1]))
    high = total.astype(bf16).astype(f32)
    out[N : N + 8, :] = jnp.where(iota(total.shape, 0) == 0, high, total - high).astype(bf16)


def mixer_far_kernel(*refs):
    base, local_b, mixer, state_in, tail_l, mixer_grad, input_grad = refs[-7:]
    states = refs[:-7]
    groups = state_in.shape[1] // N
    width = base.shape[1]
    span = width // groups
    incoming = states[-1][0:N, :].astype(f32)
    for ref in states[-2::-1]:
        decay = ref[N : N + 1, :].astype(f32) + ref[N + 1 : N + 2, :].astype(f32)
        incoming = ref[0:N, :].astype(f32) + decay * incoming
    incoming = incoming.astype(bf16)
    for g in range(groups):
        cols = slice(g * N, (g + 1) * N)
        wide = slice(g * span, (g + 1) * span)
        far = dot(state_in[:, cols], incoming[:, wide], 1, 0)
        mixer_grad[:, wide] = (base[:, wide] + tail_l[:, wide] * far).astype(bf16)
        scaled = (mixer[:, wide].astype(f32) * tail_l[:, wide]).astype(bf16)
        input_grad[:, cols] = local_b[:, cols] + dot(scaled, incoming[:, wide], 1, 1)


def block_of(total, most):
    size = min(total, most)
    while total % size:
        size -= LANES if size > LANES else 1
    return size


def small(dims, dtype):
    return math.prod(dims) * jnp.dtype(dtype).itemsize <= resident_bytes


def in_vmem(x):
    return pltpu.with_memory_space_constraint(x, pltpu.VMEM) if small(x.shape, x.dtype) else x


def vmem_out(dims, dtype):
    return pltpu.VMEM(dims, dtype) if small(dims, dtype) else jax.ShapeDtypeStruct(dims, dtype)


def cost(flops, moved):
    return pl.CostEstimate(flops=flops, transcendentals=0, bytes_accessed=moved)


def body(
    resid_input,
    norm_gain,
    expert_ids,
    route_probs,
    gate_weight,
    up_weight,
    down_weight,
    grad_output,
    mixer_input,
    state_input,
    state_output,
    step_size,
    log_retention,
    skip_gain,
):
    ctx = lax.axis_size("ctx")
    peers = lax.axis_size("exp")
    experts = peers // 2
    token_rows, model = resid_input.shape
    tokens, width = grad_output.shape
    capacity = 2 * tokens // experts
    slots = capacity // 2
    heads = skip_gain.shape[0]
    groups = state_input.shape[1] // N
    hidden = gate_weight.shape[1]
    early = max(LANES, width // 4)
    gain = norm_gain.reshape(1, model)
    partner = [(i, i ^ 1) for i in range(peers)]
    shape = jax.ShapeDtypeStruct

    packed, grad_early = pl.pallas_call(
        pack_kernel,
        out_shape=(
            vmem_out((peers, token_rows, width + LANES), bf16),
            vmem_out((tokens, early), bf16),
        ),
        compiler_params=params(),
        name="pack",
    )(resid_input, gain, expert_ids.T, route_probs.T, grad_output)
    packed = lax.all_to_all(packed, "exp", split_axis=0, concat_axis=0, tiled=True).reshape(
        tokens, width + LANES
    )

    mix, weigh, step_l, tail_l, head_l, skip_l, total_l = pl.pallas_call(
        partial(mixer_setup_kernel, groups=groups),
        out_shape=(
            shape((heads, tokens, tokens), bf16),
            shape((heads, tokens, tokens), f32),
            shape((tokens, width), f32),
            shape((tokens, width), f32),
            shape((tokens, width), f32),
            shape((8, width), f32),
            shape((8, width), f32),
        ),
        compiler_params=params(),
        cost_estimate=cost(2 * 10**9, 2 * 10**6),
        name="mixer_setup",
    )(log_retention.T, step_size.T, skip_gain.reshape(1, heads), state_input, state_output)

    table, rows_early = pl.pallas_call(
        partial(dispatch_kernel, experts=experts, capacity=capacity),
        out_shape=(
            vmem_out((experts * capacity, tokens), bf16),
            vmem_out((ctx, experts * capacity, width + early), bf16),
        ),
        compiler_params=params(),
        name="dispatch",
    )(in_vmem(packed), in_vmem(grad_early))
    shares, inverses, rows_late = pl.pallas_call(
        partial(select_kernel, experts=experts, capacity=capacity),
        out_shape=(
            vmem_out((experts * capacity, tokens), bf16),
            vmem_out((tokens, LANES), f32),
            vmem_out((ctx, experts * capacity, width - early), bf16),
        ),
        compiler_params=params(),
        cost_estimate=cost(10**9, 2 * 10**6),
        name="select",
    )(in_vmem(packed), in_vmem(table), grad_output)

    def spread(rows):
        got = lax.all_to_all(
            rows.reshape(ctx * peers, slots, -1), ("ctx", "exp"), split_axis=0, concat_axis=0, tiled=True
        ).reshape(ctx, peers, slots, -1)
        return in_vmem(got), lax.ppermute(got, "exp", partner)

    own_x, other_x = spread(rows_early)
    own_g, other_g = spread(rows_late)
    rows = 2 * ctx * slots
    half = rows // 2
    block = block_of(hidden, 512)
    blocks = hidden // block
    column = block_of(model, 512)
    columns = model // column
    product = 2 * rows * model * hidden
    any_spec = pl.BlockSpec(memory_space=pl.ANY)
    vmem_spec = pl.BlockSpec(memory_space=pltpu.VMEM)
    acts = pltpu.VMEM((rows, hidden), f32)
    coef_gate, coef_up, hidden_early = pl.pallas_call(
        partial(gate_up_kernel, width=width, block=block),
        in_specs=[vmem_spec] + [any_spec] * 4,
        out_specs=[any_spec] * 3,
        out_shape=[shape((rows, hidden), f32)] * 3,
        scratch_shapes=[
            pltpu.VMEM((ctx, peers, slots, width + early), bf16),
            pltpu.VMEM((rows, model), bf16),
            pltpu.VMEM((rows, peers * early), bf16),
            pltpu.VMEM((hidden, model), bf16),
            pltpu.VMEM((hidden, model), bf16),
            pltpu.VMEM((hidden, peers * early), bf16),
            acts,
            acts,
            acts,
            pltpu.SemaphoreType.DMA((2 * blocks + peers + 1,)),
            pltpu.SemaphoreType.DMA((3 * blocks,)),
        ],
        compiler_params=params(),
        cost_estimate=cost(5 * product // 2, 4 * model * hidden),
        name="gate_up",
    )(own_x, other_x, gate_weight, up_weight, down_weight)
    out_own, out_other = pl.pallas_call(
        partial(back_kernel, width=width, block=block),
        in_specs=[vmem_spec] * 2 + [any_spec] * 6,
        out_specs=[vmem_spec] * 2,
        out_shape=[vmem_out((half, model), bf16)] * 2,
        scratch_shapes=[
            pltpu.VMEM((rows, peers * (width - early)), bf16),
            acts,
            acts,
            acts,
            pltpu.VMEM((rows, hidden), bf16),
            pltpu.VMEM((rows, hidden), bf16),
            pltpu.VMEM((columns, hidden, column), bf16),
            pltpu.VMEM((columns, hidden, column), bf16),
            pltpu.VMEM((hidden, peers * (width - early)), bf16),
            pltpu.SemaphoreType.DMA((blocks * (peers + 3) + 2 * columns,)),
        ],
        compiler_params=params(),
        cost_estimate=cost(5 * product // 2, 6 * model * hidden),
        name="back",
    )(own_g, in_vmem(other_g), hidden_early, coef_gate, coef_up, gate_weight, up_weight, down_weight)

    swapped = lax.ppermute(out_other, "exp", partner)
    moved = pl.pallas_call(
        slot_kernel,
        out_shape=vmem_out((ctx, peers, slots, width), bf16),
        scratch_shapes=[pltpu.VMEM((half, model), f32)],
        compiler_params=params(),
        name="slot",
    )(in_vmem(out_own), in_vmem(swapped), in_vmem(gain), own_x)
    moved = lax.all_to_all(
        moved.reshape(ctx * peers, slots, width), ("ctx", "exp"), split_axis=0, concat_axis=0, tiled=True
    ).reshape(ctx, experts * capacity, width)

    upstream, resid_grad, state = pl.pallas_call(
        upstream_kernel,
        out_shape=(
            vmem_out((tokens, width), f32),
            vmem_out((tokens, width), bf16),
            vmem_out((N + 8, width), bf16),
        ),
        compiler_params=params(),
        name="upstream",
    )(*map(in_vmem, (moved, shares, inverses, grad_output, state_output, head_l, total_l)))

    def from_later(window, k):
        return in_vmem(lax.ppermute(window, "ctx", [(i, i - k) for i in range(k, ctx)]))

    spans = [1 << b for b in range((ctx - 1).bit_length()) if (ctx - 1) >> b & 1]
    window, length, windows = state, 1, {}
    while spans and length <= spans[-1]:
        offset = 1 + sum(span for span in spans if span > length)
        again = 2 * length <= spans[-1]
        near = from_later(window, length) if again else None
        if length in spans:
            far_window = near if again and offset == length else from_later(window, offset)
            windows[offset] = far_window
        if again:
            window = pl.pallas_call(
                join_kernel,
                out_shape=vmem_out((N + 8, width), bf16),
                compiler_params=params(),
                name="join",
            )(in_vmem(window), near)
        length *= 2
    states = [windows[offset] for offset in sorted(windows)]
    base, local_b = pl.pallas_call(
        mixer_local_kernel,
        out_shape=(vmem_out((tokens, width), f32), vmem_out((tokens, groups * N), f32)),
        compiler_params=params(),
        cost_estimate=cost(3 * 10**9, 2 * 10**6),
        name="mixer_local",
    )(*map(in_vmem, (upstream, resid_grad, mixer_input, state_output, mix, weigh, step_l, skip_l)))
    mixer_grad, state_input_grad = pl.pallas_call(
        mixer_far_kernel,
        out_shape=(shape((tokens, width), bf16), shape((tokens, groups * N), f32)),
        compiler_params=params(),
        name="mixer_far",
    )(*map(in_vmem, (*states, base, local_b, mixer_input, state_input, tail_l)))
    return (resid_grad, mixer_grad, state_input_grad)


def solution(mesh):
    in_specs = (
        P(("ctx", "exp"), None),
        P(),
        P(("ctx", "exp"), None),
        P(("ctx", "exp"), None),
        P("exp", "ctx", None),
        P("exp", "ctx", None),
        P("exp", "ctx", None),
        P("ctx", "exp"),
        P("ctx", "exp"),
        P("ctx", "exp"),
        P("ctx", "exp"),
        P("ctx", "exp"),
        P("ctx", "exp"),
        P("exp"),
    )
    out_specs = (P("ctx", "exp"), P("ctx", "exp"), P("ctx", "exp"))
    return jax.shard_map(body, mesh=mesh, in_specs=in_specs, out_specs=out_specs, check_vma=False)
```

```python
import math
from functools import partial

import jax
import jax.numpy as jnp
from jax import lax
from jax.experimental import pallas as pl
from jax.experimental.pallas import tpu as pltpu
from jax.sharding import PartitionSpec as P


N = 128
LANES = 128
norm_epsilon = 1e-05
f32 = jnp.float32
bf16 = jnp.bfloat16
highest = lax.Precision.HIGHEST
vmem_bytes = 56 * 1024 * 1024
resident_bytes = 2 * 1024 * 1024


def params(steps=0, limit=vmem_bytes):
    return pltpu.CompilerParams(dimension_semantics=("arbitrary",) * steps, vmem_limit_bytes=limit)


def iota(shape, dim):
    return lax.broadcasted_iota(jnp.int32, shape, dim)


def dot(a, b, ca, cb, precision=None):
    return lax.dot_general(
        a, b, (((ca,), (cb,)), ((), ())), precision=precision, preferred_element_type=f32
    )


def pack_kernel(resid, gain, ids_t, probs_t, grad, out, grad_early):
    grad_early[...] = grad[:, : grad_early.shape[1]]
    peers, rows = out.shape[0], out.shape[1]
    width = out.shape[2] - LANES
    eye = jnp.where(iota((rows, rows), 0) == iota((rows, rows), 1), 1.0, 0.0).astype(bf16)
    ids = dot(eye, ids_t[...].astype(f32).astype(bf16), 1, 1)
    probs = dot(eye, probs_t[...], 1, 1)
    lane = iota((rows, LANES), 1)
    meta = jnp.where(lane == 0, ids[:, 0:1], 0.0) + jnp.where(lane == 1, ids[:, 1:2], 0.0)
    meta = meta + jnp.where(lane == 2, probs[:, 0:1], 0.0) + jnp.where(lane == 3, probs[:, 1:2], 0.0)
    total = jnp.zeros((rows, 1), f32)
    for j in range(peers):
        x = resid[:, j * width : (j + 1) * width].astype(f32)
        total = total + jnp.sum(x * x, axis=1, keepdims=True)
    inverse = lax.rsqrt(total * (1.0 / (peers * width)) + norm_epsilon)
    high = inverse.astype(bf16).astype(f32)
    meta = meta + jnp.where(lane == 4, high, 0.0) + jnp.where(lane == 5, inverse - high, 0.0)
    meta = meta.astype(bf16)
    for j in range(peers):
        cols = slice(j * width, (j + 1) * width)
        out[j, :, :width] = (resid[:, cols].astype(f32) * inverse * gain[:, cols]).astype(bf16)
        out[j, :, width:] = meta


def dispatch_kernel(packed, grad, table, rows, *, experts, capacity):
    tokens = packed.shape[0]
    width = packed.shape[1] - LANES
    meta = packed[:, width:].astype(f32)
    lane = iota((tokens, LANES), 1).astype(f32)
    member = jnp.where((meta[:, 0:1] == lane) | (meta[:, 1:2] == lane), 1.0, 0.0).astype(bf16)
    row = iota((tokens, tokens), 0)
    col = iota((tokens, tokens), 1)
    position = dot(member, jnp.where(row < col, 1.0, 0.0).astype(bf16), 0, 0)
    member_t = dot(member, jnp.where(row == col, 1.0, 0.0).astype(bf16), 0, 0)
    position = jnp.where(member_t > 0.5, position, -1.0)
    slot = iota((capacity, tokens), 0).astype(f32)
    for e in range(experts):
        hit = slot == position[e : e + 1, :]
        table[e * capacity : (e + 1) * capacity, :] = jnp.where(hit, 1.0, 0.0).astype(bf16)
    out_x = dot(table[...], packed[:, :width], 1, 0).astype(bf16)
    out_g = dot(table[...], grad[...], 1, 0).astype(bf16)
    for c in range(rows.shape[0]):
        rows[c, :, :width] = out_x
        rows[c, :, width:] = out_g


def select_kernel(packed, table, grad, shares, inverses, rows, *, experts, capacity):
    tokens = packed.shape[0]
    meta = packed[:, packed.shape[1] - LANES :].astype(f32)
    late = rows.shape[2]
    out_g = dot(table[...], grad[:, grad.shape[1] - late :], 1, 0).astype(bf16)
    for c in range(rows.shape[0]):
        rows[c] = out_g
    inverses[...] = jnp.broadcast_to(meta[:, 4:5] + meta[:, 5:6], (tokens, LANES))
    lane = iota((tokens, LANES), 1).astype(f32)
    weight = jnp.where(meta[:, 0:1] == lane, meta[:, 2:3], 0.0) + jnp.where(meta[:, 1:2] == lane, meta[:, 3:4], 0.0)
    same = jnp.where(iota((tokens, tokens), 0) == iota((tokens, tokens), 1), 1.0, 0.0).astype(bf16)
    weight_t = dot(weight.astype(bf16), same, 0, 0)
    for e in range(experts):
        at = slice(e * capacity, (e + 1) * capacity)
        shares[at, :] = (table[at, :].astype(f32) * weight_t[e : e + 1, :]).astype(bf16)


def gather_rows(ref, first, start, stop, out):
    ctx, peers, slots = ref.shape[:3]
    for j in range(peers):
        at = slice(j * (stop - start), (j + 1) * (stop - start))
        out[first : first + ctx * slots, at] = ref[:, j, :, start:stop].reshape(ctx * slots, stop - start)


def packed_copies(hbm, rows, width, start, stop, out, sems, base):
    size = stop - start
    return [
        pltpu.make_async_copy(
            hbm.at[0, rows, j * width + start : j * width + stop],
            out.at[rows, j * size : (j + 1) * size],
            sems.at[base + j],
        )
        for j in range(out.shape[1] // size)
    ]


def launch(copies):
    for copy in copies:
        copy.start()
    return copies


def finish(copies):
    for copy in copies:
        copy.wait()


def gate_up_kernel(
    own, other_hbm, gate_hbm, up_hbm, down_hbm, coef_gate_hbm, coef_up_hbm, hidden_hbm,
    other, normed, grads, gate_w, up_w, down_w, coef_gate, coef_up, hidden_early, in_sems, out_sems, *, width, block,
):
    ctx, peers, slots, both = own.shape
    half = ctx * slots
    blocks = gate_w.shape[0] // block
    parts = [slice(i * block, (i + 1) * block) for i in range(blocks)]
    swap = launch([pltpu.make_async_copy(other_hbm, other, in_sems.at[2 * blocks])])
    downs = [
        launch(
            packed_copies(down_hbm, part, width, 0, both - width, down_w, in_sems, 2 * blocks + 1 + i * peers)
        )
        for i, part in enumerate(parts)
    ]
    pairs = [
        launch(
            [
                pltpu.make_async_copy(gate_hbm.at[0, part, :], gate_w.at[part, :], in_sems.at[2 * i]),
                pltpu.make_async_copy(up_hbm.at[0, part, :], up_w.at[part, :], in_sems.at[2 * i + 1]),
            ]
        )
        for i, part in enumerate(parts)
    ]
    gather_rows(own, 0, width, both, grads)
    finish(swap)
    gather_rows(other, half, width, both, grads)
    outs = []
    for i, part in enumerate(parts):
        finish(downs[i])
        hidden_early[:, part] = dot(grads[...], down_w[part, :], 1, 1)
        outs += launch(
            [pltpu.make_async_copy(hidden_early.at[:, part], hidden_hbm.at[:, part], out_sems.at[3 * i + 2])]
        )
    gather_rows(own, 0, 0, width, normed)
    gather_rows(other, half, 0, width, normed)
    for i, part in enumerate(parts):
        finish(pairs[i])
        gate = dot(normed[...], gate_w[part, :], 1, 1)
        up = dot(normed[...], up_w[part, :], 1, 1)
        sig = jax.nn.sigmoid(gate)
        coef_gate[:, part] = (up * sig * (1.0 + gate * (1.0 - sig))).astype(coef_gate.dtype)
        coef_up[:, part] = (gate * sig).astype(coef_up.dtype)
        outs += launch(
            [
                pltpu.make_async_copy(coef_gate.at[:, part], coef_gate_hbm.at[:, part], out_sems.at[3 * i]),
                pltpu.make_async_copy(coef_up.at[:, part], coef_up_hbm.at[:, part], out_sems.at[3 * i + 1]),
            ]
        )
    finish(outs)


def back_kernel(
    own, other, hidden_hbm, coef_gate_hbm, coef_up_hbm, gate_hbm, up_hbm, down_hbm, out_own, out_other,
    grads, hidden_early, coef_gate, coef_up, gate_grad, up_grad, gate_w, up_w, down_w, sems, *, width, block,
):
    ctx, peers, slots, late = own.shape
    half = ctx * slots
    columns, hidden, column = gate_w.shape
    blocks = hidden // block
    parts = [slice(i * block, (i + 1) * block) for i in range(blocks)]
    used = 0

    def copy(source, target):
        nonlocal used
        used += 1
        return pltpu.make_async_copy(source, target, sems.at[used - 1])

    waits = []
    for part in parts:
        downs = launch(packed_copies(down_hbm, part, width, width - late, width, down_w, sems, used))
        used += peers
        acts = [
            copy(hidden_hbm.at[:, part], hidden_early.at[:, part]),
            copy(coef_gate_hbm.at[:, part], coef_gate.at[:, part]),
            copy(coef_up_hbm.at[:, part], coef_up.at[:, part]),
        ]
        waits.append((downs, launch(acts)))
    slabs = [slice(i * column, (i + 1) * column) for i in range(columns)]
    pairs = [
        launch([copy(gate_hbm.at[0, :, cols], gate_w.at[i]), copy(up_hbm.at[0, :, cols], up_w.at[i])])
        for i, cols in enumerate(slabs)
    ]
    gather_rows(own, 0, 0, late, grads)
    gather_rows(other, half, 0, late, grads)
    for i, part in enumerate(parts):
        downs, acts = waits[i]
        finish(downs)
        late_part = dot(grads[...], down_w[part, :], 1, 1)
        finish(acts)
        grad = hidden_early[:, part] + late_part
        gate_grad[:, part] = (grad * coef_gate[:, part].astype(f32)).astype(bf16)
        up_grad[:, part] = (grad * coef_up[:, part].astype(f32)).astype(bf16)
    for i, cols in enumerate(slabs):
        finish(pairs[i])
        out = (dot(gate_grad[...], gate_w[i], 1, 0) + dot(up_grad[...], up_w[i], 1, 0)).astype(bf16)
        out_own[:, cols] = out[:half]
        out_other[:, cols] = out[half:]


def slot_kernel(own, swapped, gain, rows, out, sums):
    ctx, peers, slots, width = out.shape
    half = ctx * slots
    model = peers * width
    product = jnp.zeros((half, 1), f32)
    for j in range(peers):
        cols = slice(j * width, (j + 1) * width)
        total = own[:, cols].astype(f32) + swapped[:, cols].astype(f32)
        sums[:, cols] = total
        normed = rows[:, j, :, :width].reshape(half, width).astype(f32)
        product = product + jnp.sum(total * normed, axis=1, keepdims=True)
    shift = product * (1.0 / model)
    for j in range(peers):
        cols = slice(j * width, (j + 1) * width)
        scaled = rows[:, j, :, :width].reshape(half, width).astype(f32) * (1.0 / gain[:, cols])
        out[:, j] = (sums[:, cols] * gain[:, cols] - scaled * shift).astype(bf16).reshape(ctx, slots, width)


def mixer_setup_kernel(
    log_t, step_t, skip, state_in, state_out, mix, weigh, step_l, tail_l, head_l, skip_l, total_l, *, groups
):
    heads, tokens = log_t.shape
    width = step_l.shape[1]
    size = width // heads
    row = iota((tokens, tokens), 0)
    col = iota((tokens, tokens), 1)
    upto = jnp.where(row <= col, 1.0, 0.0)
    eye = jnp.where(row == col, 1.0, 0.0)
    cum_t = dot(log_t[...], upto, 1, 0, highest)
    cum = dot(upto, log_t[...], 0, 1, highest)
    steps = dot(eye, step_t[...], 1, 1, highest)
    last = cum[tokens - 1 : tokens, :]
    spread = jnp.where(iota((heads, width), 0) == iota((heads, width), 1) // size, 1.0, 0.0)
    step_l[...] = dot(steps, spread, 1, 0, highest)
    tail_l[...] = dot(steps * jnp.exp(last - cum), spread, 1, 0, highest)
    head_l[...] = dot(jnp.exp(cum), spread, 1, 0, highest)
    skip_l[...] = dot(jnp.broadcast_to(skip[...], (8, heads)), spread, 1, 0, highest)
    total_l[...] = dot(jnp.broadcast_to(jnp.exp(last), (8, heads)), spread, 1, 0, highest)
    later = col >= row
    for g in range(groups):
        cols = slice(g * N, (g + 1) * N)
        inter = dot(state_in[:, cols], state_out[:, cols], 1, 1)
        for h in range(g * heads // groups, (g + 1) * heads // groups):
            gap = cum_t[h : h + 1, :] - cum[:, h : h + 1]
            decay = jnp.where(later, jnp.exp(jnp.where(later, gap, 0.0)), 0.0)
            mix[h] = (decay * inter).astype(bf16)
            weigh[h] = decay * steps[:, h : h + 1]


def upstream_kernel(moved, shares, inverses, grad, state_out, head_l, total_l, upstream, resid_grad, state):
    width = grad.shape[1]
    groups = state_out.shape[1] // N
    span = width // groups
    moe = dot(shares[...], moved[0], 0, 0)
    for c in range(1, moved.shape[0]):
        moe = moe + dot(shares[...], moved[c], 0, 0)
    moe = (moe * inverses[:, 0:1]).astype(bf16)
    up = grad[...].astype(f32) + moe.astype(f32)
    upstream[...] = up
    resid_grad[...] = up.astype(bf16)
    for g in range(groups):
        cols = slice(g * N, (g + 1) * N)
        wide = slice(g * span, (g + 1) * span)
        scaled = (up[:, wide] * head_l[:, wide]).astype(bf16)
        state[0:N, wide] = dot(state_out[:, cols], scaled, 0, 0).astype(bf16)
    total = total_l[...]
    high = total.astype(bf16).astype(f32)
    state[N : N + 8, :] = jnp.where(iota(total.shape, 0) == 0, high, total - high).astype(bf16)


def mixer_local_kernel(upstream, resid_grad, mixer, state_out, mix, weigh, step_l, skip_l, base, local_b):
    tokens, width = upstream.shape
    heads = mix.shape[0]
    size = width // heads
    groups = state_out.shape[1] // N
    for g in range(groups):
        cols = slice(g * N, (g + 1) * N)
        weighted = jnp.zeros((tokens, tokens), f32)
        for h in range(g * heads // groups, (g + 1) * heads // groups):
            part = slice(h * size, (h + 1) * size)
            up_h = resid_grad[:, part]
            mixed = dot(mix[h], up_h, 1, 0)
            base[:, part] = step_l[:, part] * mixed + skip_l[0:1, part] * upstream[:, part]
            weighted = weighted + weigh[h] * dot(mixer[:, part], up_h, 1, 1)
        local_b[:, cols] = dot(weighted.astype(bf16), state_out[:, cols], 1, 0)


def join_kernel(first, later, out):
    decay = first[N : N + 1, :].astype(f32) + first[N + 1 : N + 2, :].astype(f32)
    out[0:N, :] = (first[0:N, :].astype(f32) + decay * later[0:N, :].astype(f32)).astype(bf16)
    total = decay * (later[N : N + 1, :].astype(f32) + later[N + 1 : N + 2, :].astype(f32))
    total = jnp.broadcast_to(total, (8, total.shape[1]))
    high = total.astype(bf16).astype(f32)
    out[N : N + 8, :] = jnp.where(iota(total.shape, 0) == 0, high, total - high).astype(bf16)


def mixer_far_kernel(*refs):
    base, local_b, mixer, state_in, tail_l, mixer_grad, input_grad = refs[-7:]
    states = refs[:-7]
    groups = state_in.shape[1] // N
    width = base.shape[1]
    span = width // groups
    incoming = states[-1][0:N, :].astype(f32)
    for ref in states[-2::-1]:
        decay = ref[N : N + 1, :].astype(f32) + ref[N + 1 : N + 2, :].astype(f32)
        incoming = ref[0:N, :].astype(f32) + decay * incoming
    incoming = incoming.astype(bf16)
    for g in range(groups):
        cols = slice(g * N, (g + 1) * N)
        wide = slice(g * span, (g + 1) * span)
        far = dot(state_in[:, cols], incoming[:, wide], 1, 0)
        mixer_grad[:, wide] = (base[:, wide] + tail_l[:, wide] * far).astype(bf16)
        scaled = (mixer[:, wide].astype(f32) * tail_l[:, wide]).astype(bf16)
        input_grad[:, cols] = local_b[:, cols] + dot(scaled, incoming[:, wide], 1, 1)


def block_of(total, most):
    size = min(total, most)
    while total % size:
        size -= LANES if size > LANES else 1
    return size


def small(dims, dtype):
    return math.prod(dims) * jnp.dtype(dtype).itemsize <= resident_bytes


def in_vmem(x):
    return pltpu.with_memory_space_constraint(x, pltpu.VMEM) if small(x.shape, x.dtype) else x


def vmem_out(dims, dtype):
    return pltpu.VMEM(dims, dtype) if small(dims, dtype) else jax.ShapeDtypeStruct(dims, dtype)


def cost(flops, moved):
    return pl.CostEstimate(flops=flops, transcendentals=0, bytes_accessed=moved)


def body(
    resid_input,
    norm_gain,
    expert_ids,
    route_probs,
    gate_weight,
    up_weight,
    down_weight,
    grad_output,
    mixer_input,
    state_input,
    state_output,
    step_size,
    log_retention,
    skip_gain,
):
    ctx = lax.axis_size("ctx")
    peers = lax.axis_size("exp")
    experts = peers // 2
    token_rows, model = resid_input.shape
    tokens, width = grad_output.shape
    capacity = 2 * tokens // experts
    slots = capacity // 2
    heads = skip_gain.shape[0]
    groups = state_input.shape[1] // N
    hidden = gate_weight.shape[1]
    early = max(LANES, width // 4)
    gain = norm_gain.reshape(1, model)
    partner = [(i, i ^ 1) for i in range(peers)]
    shape = jax.ShapeDtypeStruct

    packed, grad_early = pl.pallas_call(
        pack_kernel,
        out_shape=(
            vmem_out((peers, token_rows, width + LANES), bf16),
            vmem_out((tokens, early), bf16),
        ),
        compiler_params=params(),
        name="pack",
    )(resid_input, gain, expert_ids.T, route_probs.T, grad_output)
    packed = lax.all_to_all(packed, "exp", split_axis=0, concat_axis=0, tiled=True).reshape(
        tokens, width + LANES
    )

    mix, weigh, step_l, tail_l, head_l, skip_l, total_l = pl.pallas_call(
        partial(mixer_setup_kernel, groups=groups),
        out_shape=(
            shape((heads, tokens, tokens), bf16),
            shape((heads, tokens, tokens), f32),
            shape((tokens, width), f32),
            shape((tokens, width), f32),
            shape((tokens, width), f32),
            shape((8, width), f32),
            shape((8, width), f32),
        ),
        compiler_params=params(),
        cost_estimate=cost(2 * 10**9, 2 * 10**6),
        name="mixer_setup",
    )(log_retention.T, step_size.T, skip_gain.reshape(1, heads), state_input, state_output)

    table, rows_early = pl.pallas_call(
        partial(dispatch_kernel, experts=experts, capacity=capacity),
        out_shape=(
            vmem_out((experts * capacity, tokens), bf16),
            vmem_out((ctx, experts * capacity, width + early), bf16),
        ),
        compiler_params=params(),
        name="dispatch",
    )(in_vmem(packed), in_vmem(grad_early))
    shares, inverses, rows_late = pl.pallas_call(
        partial(select_kernel, experts=experts, capacity=capacity),
        out_shape=(
            vmem_out((experts * capacity, tokens), bf16),
            vmem_out((tokens, LANES), f32),
            vmem_out((ctx, experts * capacity, width - early), bf16),
        ),
        compiler_params=params(),
        cost_estimate=cost(10**9, 2 * 10**6),
        name="select",
    )(in_vmem(packed), in_vmem(table), grad_output)

    def spread(rows):
        got = lax.all_to_all(
            rows.reshape(ctx * peers, slots, -1), ("ctx", "exp"), split_axis=0, concat_axis=0, tiled=True
        ).reshape(ctx, peers, slots, -1)
        return in_vmem(got), lax.ppermute(got, "exp", partner)

    own_x, other_x = spread(rows_early)
    own_g, other_g = spread(rows_late)
    rows = 2 * ctx * slots
    half = rows // 2
    block = block_of(hidden, 512)
    blocks = hidden // block
    column = block_of(model, 512)
    columns = model // column
    product = 2 * rows * model * hidden
    any_spec = pl.BlockSpec(memory_space=pl.ANY)
    vmem_spec = pl.BlockSpec(memory_space=pltpu.VMEM)
    coefs = shape((rows, hidden), bf16)
    coef_buffer = pltpu.VMEM((rows, hidden), bf16)
    hidden_buffer = pltpu.VMEM((rows, hidden), f32)
    coef_gate, coef_up, hidden_early = pl.pallas_call(
        partial(gate_up_kernel, width=width, block=block),
        in_specs=[vmem_spec] + [any_spec] * 4,
        out_specs=[any_spec] * 3,
        out_shape=[coefs, coefs, shape((rows, hidden), f32)],
        scratch_shapes=[
            pltpu.VMEM((ctx, peers, slots, width + early), bf16),
            pltpu.VMEM((rows, model), bf16),
            pltpu.VMEM((rows, peers * early), bf16),
            pltpu.VMEM((hidden, model), bf16),
            pltpu.VMEM((hidden, model), bf16),
            pltpu.VMEM((hidden, peers * early), bf16),
            coef_buffer,
            coef_buffer,
            hidden_buffer,
            pltpu.SemaphoreType.DMA((blocks * (peers + 2) + 1,)),
            pltpu.SemaphoreType.DMA((3 * blocks,)),
        ],
        compiler_params=params(),
        cost_estimate=cost(5 * product // 2, 4 * model * hidden),
        name="gate_up",
    )(own_x, other_x, gate_weight, up_weight, down_weight)
    out_own, out_other = pl.pallas_call(
        partial(back_kernel, width=width, block=block),
        in_specs=[vmem_spec] * 2 + [any_spec] * 6,
        out_specs=[vmem_spec] * 2,
        out_shape=[vmem_out((half, model), bf16)] * 2,
        scratch_shapes=[
            pltpu.VMEM((rows, peers * (width - early)), bf16),
            hidden_buffer,
            coef_buffer,
            coef_buffer,
            pltpu.VMEM((rows, hidden), bf16),
            pltpu.VMEM((rows, hidden), bf16),
            pltpu.VMEM((columns, hidden, column), bf16),
            pltpu.VMEM((columns, hidden, column), bf16),
            pltpu.VMEM((hidden, peers * (width - early)), bf16),
            pltpu.SemaphoreType.DMA((blocks * (peers + 3) + 2 * columns,)),
        ],
        compiler_params=params(),
        cost_estimate=cost(5 * product // 2, 6 * model * hidden),
        name="back",
    )(own_g, in_vmem(other_g), hidden_early, coef_gate, coef_up, gate_weight, up_weight, down_weight)

    swapped = lax.ppermute(out_other, "exp", partner)
    moved = pl.pallas_call(
        slot_kernel,
        out_shape=vmem_out((ctx, peers, slots, width), bf16),
        scratch_shapes=[pltpu.VMEM((half, model), f32)],
        compiler_params=params(),
        name="slot",
    )(in_vmem(out_own), in_vmem(swapped), in_vmem(gain), own_x)
    moved = lax.all_to_all(
        moved.reshape(ctx * peers, slots, width), ("ctx", "exp"), split_axis=0, concat_axis=0, tiled=True
    ).reshape(ctx, experts * capacity, width)

    upstream, resid_grad, state = pl.pallas_call(
        upstream_kernel,
        out_shape=(
            vmem_out((tokens, width), f32),
            vmem_out((tokens, width), bf16),
            vmem_out((N + 8, width), bf16),
        ),
        compiler_params=params(),
        name="upstream",
    )(*map(in_vmem, (moved, shares, inverses, grad_output, state_output, head_l, total_l)))

    def from_later(window, k):
        return in_vmem(lax.ppermute(window, "ctx", [(i, i - k) for i in range(k, ctx)]))

    spans = [1 << b for b in range((ctx - 1).bit_length()) if (ctx - 1) >> b & 1]
    window, length, windows = state, 1, {}
    while spans and length <= spans[-1]:
        offset = 1 + sum(span for span in spans if span > length)
        again = 2 * length <= spans[-1]
        near = from_later(window, length) if again else None
        if length in spans:
            far_window = near if again and offset == length else from_later(window, offset)
            windows[offset] = far_window
        if again:
            window = pl.pallas_call(
                join_kernel,
                out_shape=vmem_out((N + 8, width), bf16),
                compiler_params=params(),
                name="join",
            )(in_vmem(window), near)
        length *= 2
    states = [windows[offset] for offset in sorted(windows)]
    base, local_b = pl.pallas_call(
        mixer_local_kernel,
        out_shape=(vmem_out((tokens, width), f32), vmem_out((tokens, groups * N), f32)),
        compiler_params=params(),
        cost_estimate=cost(3 * 10**9, 2 * 10**6),
        name="mixer_local",
    )(*map(in_vmem, (upstream, resid_grad, mixer_input, state_output, mix, weigh, step_l, skip_l)))
    mixer_grad, state_input_grad = pl.pallas_call(
        mixer_far_kernel,
        out_shape=(shape((tokens, width), bf16), shape((tokens, groups * N), f32)),
        compiler_params=params(),
        name="mixer_far",
    )(*map(in_vmem, (*states, base, local_b, mixer_input, state_input, tail_l)))
    return (resid_grad, mixer_grad, state_input_grad)


def solution(mesh):
    in_specs = (
        P(("ctx", "exp"), None),
        P(),
        P(("ctx", "exp"), None),
        P(("ctx", "exp"), None),
        P("exp", "ctx", None),
        P("exp", "ctx", None),
        P("exp", "ctx", None),
        P("ctx", "exp"),
        P("ctx", "exp"),
        P("ctx", "exp"),
        P("ctx", "exp"),
        P("ctx", "exp"),
        P("ctx", "exp"),
        P("exp"),
    )
    out_specs = (P("ctx", "exp"), P("ctx", "exp"), P("ctx", "exp"))
    return jax.shard_map(body, mesh=mesh, in_specs=in_specs, out_specs=out_specs, check_vma=False)
```

```python
import math
from functools import partial

import jax
import jax.numpy as jnp
from jax import lax
from jax.experimental import pallas as pl
from jax.experimental.pallas import tpu as pltpu
from jax.sharding import PartitionSpec as P


N = 128
LANES = 128
norm_epsilon = 1e-05
f32 = jnp.float32
bf16 = jnp.bfloat16
highest = lax.Precision.HIGHEST
vmem_bytes = 56 * 1024 * 1024
resident_bytes = 2 * 1024 * 1024


def params(steps=0, limit=vmem_bytes):
    return pltpu.CompilerParams(dimension_semantics=("arbitrary",) * steps, vmem_limit_bytes=limit)


def iota(shape, dim):
    return lax.broadcasted_iota(jnp.int32, shape, dim)


def dot(a, b, ca, cb, precision=None):
    return lax.dot_general(
        a, b, (((ca,), (cb,)), ((), ())), precision=precision, preferred_element_type=f32
    )


def pack_kernel(resid, gain, ids_t, probs_t, grad, out, grad_early):
    grad_early[...] = grad[:, : grad_early.shape[1]]
    peers, rows = out.shape[0], out.shape[1]
    width = out.shape[2] - LANES
    eye = jnp.where(iota((rows, rows), 0) == iota((rows, rows), 1), 1.0, 0.0).astype(bf16)
    ids = dot(eye, ids_t[...].astype(f32).astype(bf16), 1, 1)
    probs = dot(eye, probs_t[...], 1, 1)
    lane = iota((rows, LANES), 1)
    meta = jnp.where(lane == 0, ids[:, 0:1], 0.0) + jnp.where(lane == 1, ids[:, 1:2], 0.0)
    meta = meta + jnp.where(lane == 2, probs[:, 0:1], 0.0) + jnp.where(lane == 3, probs[:, 1:2], 0.0)
    total = jnp.zeros((rows, 1), f32)
    for j in range(peers):
        x = resid[:, j * width : (j + 1) * width].astype(f32)
        total = total + jnp.sum(x * x, axis=1, keepdims=True)
    inverse = lax.rsqrt(total * (1.0 / (peers * width)) + norm_epsilon)
    high = inverse.astype(bf16).astype(f32)
    meta = meta + jnp.where(lane == 4, high, 0.0) + jnp.where(lane == 5, inverse - high, 0.0)
    meta = meta.astype(bf16)
    for j in range(peers):
        cols = slice(j * width, (j + 1) * width)
        out[j, :, :width] = (resid[:, cols].astype(f32) * inverse * gain[:, cols]).astype(bf16)
        out[j, :, width:] = meta


def dispatch_kernel(packed, grad, table, rows, *, experts, capacity):
    tokens = packed.shape[0]
    width = packed.shape[1] - LANES
    meta = packed[:, width:].astype(f32)
    lane = iota((tokens, LANES), 1).astype(f32)
    member = jnp.where((meta[:, 0:1] == lane) | (meta[:, 1:2] == lane), 1.0, 0.0).astype(bf16)
    row = iota((tokens, tokens), 0)
    col = iota((tokens, tokens), 1)
    position = dot(member, jnp.where(row < col, 1.0, 0.0).astype(bf16), 0, 0)
    member_t = dot(member, jnp.where(row == col, 1.0, 0.0).astype(bf16), 0, 0)
    position = jnp.where(member_t > 0.5, position, -1.0)
    slot = iota((capacity, tokens), 0).astype(f32)
    for e in range(experts):
        hit = slot == position[e : e + 1, :]
        table[e * capacity : (e + 1) * capacity, :] = jnp.where(hit, 1.0, 0.0).astype(bf16)
    out_x = dot(table[...], packed[:, :width], 1, 0).astype(bf16)
    out_g = dot(table[...], grad[...], 1, 0).astype(bf16)
    for c in range(rows.shape[0]):
        rows[c, :, :width] = out_x
        rows[c, :, width:] = out_g


def select_kernel(packed, table, grad, shares, inverses, rows, *, experts, capacity):
    tokens = packed.shape[0]
    meta = packed[:, packed.shape[1] - LANES :].astype(f32)
    late = rows.shape[2]
    out_g = dot(table[...], grad[:, grad.shape[1] - late :], 1, 0).astype(bf16)
    for c in range(rows.shape[0]):
        rows[c] = out_g
    inverses[...] = jnp.broadcast_to(meta[:, 4:5] + meta[:, 5:6], (tokens, LANES))
    lane = iota((tokens, LANES), 1).astype(f32)
    weight = jnp.where(meta[:, 0:1] == lane, meta[:, 2:3], 0.0) + jnp.where(meta[:, 1:2] == lane, meta[:, 3:4], 0.0)
    same = jnp.where(iota((tokens, tokens), 0) == iota((tokens, tokens), 1), 1.0, 0.0).astype(bf16)
    weight_t = dot(weight.astype(bf16), same, 0, 0)
    for e in range(experts):
        at = slice(e * capacity, (e + 1) * capacity)
        shares[at, :] = (table[at, :].astype(f32) * weight_t[e : e + 1, :]).astype(bf16)


def gather_rows(ref, first, start, stop, out):
    ctx, peers, slots = ref.shape[:3]
    for j in range(peers):
        at = slice(j * (stop - start), (j + 1) * (stop - start))
        out[first : first + ctx * slots, at] = ref[:, j, :, start:stop].reshape(ctx * slots, stop - start)


def packed_copies(hbm, rows, width, start, stop, out, sems, base):
    size = stop - start
    return [
        pltpu.make_async_copy(
            hbm.at[0, rows, j * width + start : j * width + stop],
            out.at[rows, j * size : (j + 1) * size],
            sems.at[base + j],
        )
        for j in range(out.shape[1] // size)
    ]


def launch(copies):
    for copy in copies:
        copy.start()
    return copies


def finish(copies):
    for copy in copies:
        copy.wait()


def gate_up_kernel(
    own, other_hbm, gate_hbm, up_hbm, down_hbm, coef_gate_hbm, coef_up_hbm, hidden_hbm,
    other, normed, grads, gate_w, up_w, down_w, coef_gate, coef_up, hidden_early, in_sems, out_sems, *, width, block,
):
    ctx, peers, slots, both = own.shape
    half = ctx * slots
    blocks = gate_w.shape[0] // block
    parts = [slice(i * block, (i + 1) * block) for i in range(blocks)]
    swap = launch([pltpu.make_async_copy(other_hbm, other, in_sems.at[2 * blocks])])
    downs = [
        launch(
            packed_copies(down_hbm, part, width, 0, both - width, down_w, in_sems, 2 * blocks + 1 + i * peers)
        )
        for i, part in enumerate(parts)
    ]
    pairs = [
        launch(
            [
                pltpu.make_async_copy(gate_hbm.at[0, part, :], gate_w.at[part, :], in_sems.at[2 * i]),
                pltpu.make_async_copy(up_hbm.at[0, part, :], up_w.at[part, :], in_sems.at[2 * i + 1]),
            ]
        )
        for i, part in enumerate(parts)
    ]
    gather_rows(own, 0, width, both, grads)
    finish(swap)
    gather_rows(other, half, width, both, grads)
    outs = []
    for i, part in enumerate(parts):
        finish(downs[i])
        hidden_early[:, part] = dot(grads[...], down_w[part, :], 1, 1).astype(hidden_early.dtype)
        outs += launch(
            [pltpu.make_async_copy(hidden_early.at[:, part], hidden_hbm.at[:, part], out_sems.at[3 * i + 2])]
        )
    gather_rows(own, 0, 0, width, normed)
    gather_rows(other, half, 0, width, normed)
    for i, part in enumerate(parts):
        finish(pairs[i])
        gate = dot(normed[...], gate_w[part, :], 1, 1)
        up = dot(normed[...], up_w[part, :], 1, 1)
        sig = jax.nn.sigmoid(gate)
        coef_gate[:, part] = (up * sig * (1.0 + gate * (1.0 - sig))).astype(coef_gate.dtype)
        coef_up[:, part] = (gate * sig).astype(coef_up.dtype)
        outs += launch(
            [
                pltpu.make_async_copy(coef_gate.at[:, part], coef_gate_hbm.at[:, part], out_sems.at[3 * i]),
                pltpu.make_async_copy(coef_up.at[:, part], coef_up_hbm.at[:, part], out_sems.at[3 * i + 1]),
            ]
        )
    finish(outs)


def back_kernel(
    own, other, hidden_hbm, coef_gate_hbm, coef_up_hbm, gate_hbm, up_hbm, down_hbm, out_own, out_other,
    grads, hidden_early, coef_gate, coef_up, gate_grad, up_grad, gate_w, up_w, down_w, sems, *, width, block,
):
    ctx, peers, slots, late = own.shape
    half = ctx * slots
    columns, hidden, column = gate_w.shape
    blocks = hidden // block
    parts = [slice(i * block, (i + 1) * block) for i in range(blocks)]
    used = 0

    def copy(source, target):
        nonlocal used
        used += 1
        return pltpu.make_async_copy(source, target, sems.at[used - 1])

    waits = []
    for part in parts:
        downs = launch(packed_copies(down_hbm, part, width, width - late, width, down_w, sems, used))
        used += peers
        acts = [
            copy(hidden_hbm.at[:, part], hidden_early.at[:, part]),
            copy(coef_gate_hbm.at[:, part], coef_gate.at[:, part]),
            copy(coef_up_hbm.at[:, part], coef_up.at[:, part]),
        ]
        waits.append((downs, launch(acts)))
    slabs = [slice(i * column, (i + 1) * column) for i in range(columns)]
    pairs = [
        launch([copy(gate_hbm.at[0, :, cols], gate_w.at[i]), copy(up_hbm.at[0, :, cols], up_w.at[i])])
        for i, cols in enumerate(slabs)
    ]
    gather_rows(own, 0, 0, late, grads)
    gather_rows(other, half, 0, late, grads)
    for i, part in enumerate(parts):
        downs, acts = waits[i]
        finish(downs)
        late_part = dot(grads[...], down_w[part, :], 1, 1)
        finish(acts)
        grad = hidden_early[:, part].astype(f32) + late_part
        gate_grad[:, part] = (grad * coef_gate[:, part].astype(f32)).astype(bf16)
        up_grad[:, part] = (grad * coef_up[:, part].astype(f32)).astype(bf16)
    for i, cols in enumerate(slabs):
        finish(pairs[i])
        out = (dot(gate_grad[...], gate_w[i], 1, 0) + dot(up_grad[...], up_w[i], 1, 0)).astype(bf16)
        out_own[:, cols] = out[:half]
        out_other[:, cols] = out[half:]


def slot_kernel(own, swapped, gain, rows, out, sums):
    ctx, peers, slots, width = out.shape
    half = ctx * slots
    model = peers * width
    product = jnp.zeros((half, 1), f32)
    for j in range(peers):
        cols = slice(j * width, (j + 1) * width)
        total = own[:, cols].astype(f32) + swapped[:, cols].astype(f32)
        sums[:, cols] = total
        normed = rows[:, j, :, :width].reshape(half, width).astype(f32)
        product = product + jnp.sum(total * normed, axis=1, keepdims=True)
    shift = product * (1.0 / model)
    for j in range(peers):
        cols = slice(j * width, (j + 1) * width)
        scaled = rows[:, j, :, :width].reshape(half, width).astype(f32) * (1.0 / gain[:, cols])
        out[:, j] = (sums[:, cols] * gain[:, cols] - scaled * shift).astype(bf16).reshape(ctx, slots, width)


def mixer_setup_kernel(
    log_t, step_t, skip, state_in, state_out, mix, weigh, step_l, tail_l, head_l, skip_l, total_l, *, groups
):
    heads, tokens = log_t.shape
    width = step_l.shape[1]
    size = width // heads
    row = iota((tokens, tokens), 0)
    col = iota((tokens, tokens), 1)
    upto = jnp.where(row <= col, 1.0, 0.0)
    eye = jnp.where(row == col, 1.0, 0.0)
    cum_t = dot(log_t[...], upto, 1, 0, highest)
    cum = dot(upto, log_t[...], 0, 1, highest)
    steps = dot(eye, step_t[...], 1, 1, highest)
    last = cum[tokens - 1 : tokens, :]
    spread = jnp.where(iota((heads, width), 0) == iota((heads, width), 1) // size, 1.0, 0.0)
    step_l[...] = dot(steps, spread, 1, 0, highest)
    tail_l[...] = dot(steps * jnp.exp(last - cum), spread, 1, 0, highest)
    head_l[...] = dot(jnp.exp(cum), spread, 1, 0, highest)
    skip_l[...] = dot(jnp.broadcast_to(skip[...], (8, heads)), spread, 1, 0, highest)
    total_l[...] = dot(jnp.broadcast_to(jnp.exp(last), (8, heads)), spread, 1, 0, highest)
    later = col >= row
    for g in range(groups):
        cols = slice(g * N, (g + 1) * N)
        inter = dot(state_in[:, cols], state_out[:, cols], 1, 1)
        for h in range(g * heads // groups, (g + 1) * heads // groups):
            gap = cum_t[h : h + 1, :] - cum[:, h : h + 1]
            decay = jnp.where(later, jnp.exp(jnp.where(later, gap, 0.0)), 0.0)
            mix[h] = (decay * inter).astype(bf16)
            weigh[h] = decay * steps[:, h : h + 1]


def upstream_kernel(moved, shares, inverses, grad, state_out, head_l, total_l, upstream, resid_grad, state):
    width = grad.shape[1]
    groups = state_out.shape[1] // N
    span = width // groups
    moe = dot(shares[...], moved[0], 0, 0)
    for c in range(1, moved.shape[0]):
        moe = moe + dot(shares[...], moved[c], 0, 0)
    moe = (moe * inverses[:, 0:1]).astype(bf16)
    up = grad[...].astype(f32) + moe.astype(f32)
    upstream[...] = up
    resid_grad[...] = up.astype(bf16)
    for g in range(groups):
        cols = slice(g * N, (g + 1) * N)
        wide = slice(g * span, (g + 1) * span)
        scaled = (up[:, wide] * head_l[:, wide]).astype(bf16)
        state[0:N, wide] = dot(state_out[:, cols], scaled, 0, 0).astype(bf16)
    total = total_l[...]
    high = total.astype(bf16).astype(f32)
    state[N : N + 8, :] = jnp.where(iota(total.shape, 0) == 0, high, total - high).astype(bf16)


def mixer_local_kernel(upstream, resid_grad, mixer, state_out, mix, weigh, step_l, skip_l, base, local_b):
    tokens, width = upstream.shape
    heads = mix.shape[0]
    size = width // heads
    groups = state_out.shape[1] // N
    for g in range(groups):
        cols = slice(g * N, (g + 1) * N)
        weighted = jnp.zeros((tokens, tokens), f32)
        for h in range(g * heads // groups, (g + 1) * heads // groups):
            part = slice(h * size, (h + 1) * size)
            up_h = resid_grad[:, part]
            mixed = dot(mix[h], up_h, 1, 0)
            base[:, part] = step_l[:, part] * mixed + skip_l[0:1, part] * upstream[:, part]
            weighted = weighted + weigh[h] * dot(mixer[:, part], up_h, 1, 1)
        local_b[:, cols] = dot(weighted.astype(bf16), state_out[:, cols], 1, 0)


def join_kernel(first, later, out):
    decay = first[N : N + 1, :].astype(f32) + first[N + 1 : N + 2, :].astype(f32)
    out[0:N, :] = (first[0:N, :].astype(f32) + decay * later[0:N, :].astype(f32)).astype(bf16)
    total = decay * (later[N : N + 1, :].astype(f32) + later[N + 1 : N + 2, :].astype(f32))
    total = jnp.broadcast_to(total, (8, total.shape[1]))
    high = total.astype(bf16).astype(f32)
    out[N : N + 8, :] = jnp.where(iota(total.shape, 0) == 0, high, total - high).astype(bf16)


def mixer_far_kernel(*refs):
    base, local_b, mixer, state_in, tail_l, mixer_grad, input_grad = refs[-7:]
    states = refs[:-7]
    groups = state_in.shape[1] // N
    width = base.shape[1]
    span = width // groups
    incoming = states[-1][0:N, :].astype(f32)
    for ref in states[-2::-1]:
        decay = ref[N : N + 1, :].astype(f32) + ref[N + 1 : N + 2, :].astype(f32)
        incoming = ref[0:N, :].astype(f32) + decay * incoming
    incoming = incoming.astype(bf16)
    for g in range(groups):
        cols = slice(g * N, (g + 1) * N)
        wide = slice(g * span, (g + 1) * span)
        far = dot(state_in[:, cols], incoming[:, wide], 1, 0)
        mixer_grad[:, wide] = (base[:, wide] + tail_l[:, wide] * far).astype(bf16)
        scaled = (mixer[:, wide].astype(f32) * tail_l[:, wide]).astype(bf16)
        input_grad[:, cols] = local_b[:, cols] + dot(scaled, incoming[:, wide], 1, 1)


def block_of(total, most):
    size = min(total, most)
    while total % size:
        size -= LANES if size > LANES else 1
    return size


def small(dims, dtype):
    return math.prod(dims) * jnp.dtype(dtype).itemsize <= resident_bytes


def in_vmem(x):
    return pltpu.with_memory_space_constraint(x, pltpu.VMEM) if small(x.shape, x.dtype) else x


def vmem_out(dims, dtype):
    return pltpu.VMEM(dims, dtype) if small(dims, dtype) else jax.ShapeDtypeStruct(dims, dtype)


def cost(flops, moved):
    return pl.CostEstimate(flops=flops, transcendentals=0, bytes_accessed=moved)


def body(
    resid_input,
    norm_gain,
    expert_ids,
    route_probs,
    gate_weight,
    up_weight,
    down_weight,
    grad_output,
    mixer_input,
    state_input,
    state_output,
    step_size,
    log_retention,
    skip_gain,
):
    ctx = lax.axis_size("ctx")
    peers = lax.axis_size("exp")
    experts = peers // 2
    token_rows, model = resid_input.shape
    tokens, width = grad_output.shape
    capacity = 2 * tokens // experts
    slots = capacity // 2
    heads = skip_gain.shape[0]
    groups = state_input.shape[1] // N
    hidden = gate_weight.shape[1]
    early = max(LANES, width // 4)
    gain = norm_gain.reshape(1, model)
    partner = [(i, i ^ 1) for i in range(peers)]
    shape = jax.ShapeDtypeStruct

    packed, grad_early = pl.pallas_call(
        pack_kernel,
        out_shape=(
            vmem_out((peers, token_rows, width + LANES), bf16),
            vmem_out((tokens, early), bf16),
        ),
        compiler_params=params(),
        name="pack",
    )(resid_input, gain, expert_ids.T, route_probs.T, grad_output)
    packed = lax.all_to_all(packed, "exp", split_axis=0, concat_axis=0, tiled=True).reshape(
        tokens, width + LANES
    )

    mix, weigh, step_l, tail_l, head_l, skip_l, total_l = pl.pallas_call(
        partial(mixer_setup_kernel, groups=groups),
        out_shape=(
            shape((heads, tokens, tokens), bf16),
            shape((heads, tokens, tokens), f32),
            shape((tokens, width), f32),
            shape((tokens, width), f32),
            shape((tokens, width), f32),
            shape((8, width), f32),
            shape((8, width), f32),
        ),
        compiler_params=params(),
        cost_estimate=cost(2 * 10**9, 2 * 10**6),
        name="mixer_setup",
    )(log_retention.T, step_size.T, skip_gain.reshape(1, heads), state_input, state_output)

    table, rows_early = pl.pallas_call(
        partial(dispatch_kernel, experts=experts, capacity=capacity),
        out_shape=(
            vmem_out((experts * capacity, tokens), bf16),
            vmem_out((ctx, experts * capacity, width + early), bf16),
        ),
        compiler_params=params(),
        name="dispatch",
    )(in_vmem(packed), in_vmem(grad_early))
    shares, inverses, rows_late = pl.pallas_call(
        partial(select_kernel, experts=experts, capacity=capacity),
        out_shape=(
            vmem_out((experts * capacity, tokens), bf16),
            vmem_out((tokens, LANES), f32),
            vmem_out((ctx, experts * capacity, width - early), bf16),
        ),
        compiler_params=params(),
        cost_estimate=cost(10**9, 2 * 10**6),
        name="select",
    )(in_vmem(packed), in_vmem(table), grad_output)

    def spread(rows):
        got = lax.all_to_all(
            rows.reshape(ctx * peers, slots, -1), ("ctx", "exp"), split_axis=0, concat_axis=0, tiled=True
        ).reshape(ctx, peers, slots, -1)
        return in_vmem(got), lax.ppermute(got, "exp", partner)

    own_x, other_x = spread(rows_early)
    own_g, other_g = spread(rows_late)
    rows = 2 * ctx * slots
    half = rows // 2
    block = block_of(hidden, 512)
    blocks = hidden // block
    column = block_of(model, 512)
    columns = model // column
    product = 2 * rows * model * hidden
    any_spec = pl.BlockSpec(memory_space=pl.ANY)
    vmem_spec = pl.BlockSpec(memory_space=pltpu.VMEM)
    coefs = shape((rows, hidden), bf16)
    coef_buffer = pltpu.VMEM((rows, hidden), bf16)
    hidden_buffer = pltpu.VMEM((rows, hidden), bf16)
    coef_gate, coef_up, hidden_early = pl.pallas_call(
        partial(gate_up_kernel, width=width, block=block),
        in_specs=[vmem_spec] + [any_spec] * 4,
        out_specs=[any_spec] * 3,
        out_shape=[coefs, coefs, coefs],
        scratch_shapes=[
            pltpu.VMEM((ctx, peers, slots, width + early), bf16),
            pltpu.VMEM((rows, model), bf16),
            pltpu.VMEM((rows, peers * early), bf16),
            pltpu.VMEM((hidden, model), bf16),
            pltpu.VMEM((hidden, model), bf16),
            pltpu.VMEM((hidden, peers * early), bf16),
            coef_buffer,
            coef_buffer,
            hidden_buffer,
            pltpu.SemaphoreType.DMA((blocks * (peers + 2) + 1,)),
            pltpu.SemaphoreType.DMA((3 * blocks,)),
        ],
        compiler_params=params(),
        cost_estimate=cost(5 * product // 2, 4 * model * hidden),
        name="gate_up",
    )(own_x, other_x, gate_weight, up_weight, down_weight)
    out_own, out_other = pl.pallas_call(
        partial(back_kernel, width=width, block=block),
        in_specs=[vmem_spec] * 2 + [any_spec] * 6,
        out_specs=[vmem_spec] * 2,
        out_shape=[vmem_out((half, model), bf16)] * 2,
        scratch_shapes=[
            pltpu.VMEM((rows, peers * (width - early)), bf16),
            hidden_buffer,
            coef_buffer,
            coef_buffer,
            pltpu.VMEM((rows, hidden), bf16),
            pltpu.VMEM((rows, hidden), bf16),
            pltpu.VMEM((columns, hidden, column), bf16),
            pltpu.VMEM((columns, hidden, column), bf16),
            pltpu.VMEM((hidden, peers * (width - early)), bf16),
            pltpu.SemaphoreType.DMA((blocks * (peers + 3) + 2 * columns,)),
        ],
        compiler_params=params(),
        cost_estimate=cost(5 * product // 2, 6 * model * hidden),
        name="back",
    )(own_g, in_vmem(other_g), hidden_early, coef_gate, coef_up, gate_weight, up_weight, down_weight)

    swapped = lax.ppermute(out_other, "exp", partner)
    moved = pl.pallas_call(
        slot_kernel,
        out_shape=vmem_out((ctx, peers, slots, width), bf16),
        scratch_shapes=[pltpu.VMEM((half, model), f32)],
        compiler_params=params(),
        name="slot",
    )(in_vmem(out_own), in_vmem(swapped), in_vmem(gain), own_x)
    moved = lax.all_to_all(
        moved.reshape(ctx * peers, slots, width), ("ctx", "exp"), split_axis=0, concat_axis=0, tiled=True
    ).reshape(ctx, experts * capacity, width)

    upstream, resid_grad, state = pl.pallas_call(
        upstream_kernel,
        out_shape=(
            vmem_out((tokens, width), f32),
            vmem_out((tokens, width), bf16),
            vmem_out((N + 8, width), bf16),
        ),
        compiler_params=params(),
        name="upstream",
    )(*map(in_vmem, (moved, shares, inverses, grad_output, state_output, head_l, total_l)))

    def from_later(window, k):
        return in_vmem(lax.ppermute(window, "ctx", [(i, i - k) for i in range(k, ctx)]))

    spans = [1 << b for b in range((ctx - 1).bit_length()) if (ctx - 1) >> b & 1]
    window, length, windows = state, 1, {}
    while spans and length <= spans[-1]:
        offset = 1 + sum(span for span in spans if span > length)
        again = 2 * length <= spans[-1]
        near = from_later(window, length) if again else None
        if length in spans:
            far_window = near if again and offset == length else from_later(window, offset)
            windows[offset] = far_window
        if again:
            window = pl.pallas_call(
                join_kernel,
                out_shape=vmem_out((N + 8, width), bf16),
                compiler_params=params(),
                name="join",
            )(in_vmem(window), near)
        length *= 2
    states = [windows[offset] for offset in sorted(windows)]
    base, local_b = pl.pallas_call(
        mixer_local_kernel,
        out_shape=(vmem_out((tokens, width), f32), vmem_out((tokens, groups * N), f32)),
        compiler_params=params(),
        cost_estimate=cost(3 * 10**9, 2 * 10**6),
        name="mixer_local",
    )(*map(in_vmem, (upstream, resid_grad, mixer_input, state_output, mix, weigh, step_l, skip_l)))
    mixer_grad, state_input_grad = pl.pallas_call(
        mixer_far_kernel,
        out_shape=(shape((tokens, width), bf16), shape((tokens, groups * N), f32)),
        compiler_params=params(),
        name="mixer_far",
    )(*map(in_vmem, (*states, base, local_b, mixer_input, state_input, tail_l)))
    return (resid_grad, mixer_grad, state_input_grad)


def solution(mesh):
    in_specs = (
        P(("ctx", "exp"), None),
        P(),
        P(("ctx", "exp"), None),
        P(("ctx", "exp"), None),
        P("exp", "ctx", None),
        P("exp", "ctx", None),
        P("exp", "ctx", None),
        P("ctx", "exp"),
        P("ctx", "exp"),
        P("ctx", "exp"),
        P("ctx", "exp"),
        P("ctx", "exp"),
        P("ctx", "exp"),
        P("exp"),
    )
    out_specs = (P("ctx", "exp"), P("ctx", "exp"), P("ctx", "exp"))
    return jax.shard_map(body, mesh=mesh, in_specs=in_specs, out_specs=out_specs, check_vma=False)
```
